32 devices in a mesh: seq: 8 (over y, x, core), dp: 4 (over z).
Axes of the slice: x: 2, y: 2, z: 4, core: 2. Of those that a mesh axis runs over, the one named last changes fastest.
Arguments:
- block_input: float32 [4, 1024, 2048], P('dp', 'seq'), may hold values from -6 to 6
- lengths: int32 [4, 4], P('dp'), may hold values from 1 to 512, 1024 in all within a row
- cotangent: float32 [4, 1024, 2048], P('dp', 'seq'), may hold values from -6 to 6
- attn_gain: float32 [2048], P(('seq', 'dp')), may hold values from 0.5 to 1.5
- w_qa: float32 [2048, 1024], P(('seq', 'dp')), may hold values from -0.125 to 0.125
- q_gain: float32 [1024], P(('seq', 'dp')), may hold values from 0.5 to 1.5
- w_qb: float32 [1024, 4096], P(('seq', 'dp')), may hold values from -0.1875 to 0.1875
- w_k: float32 [2048, 256], P(('seq', 'dp')), may hold values from -0.125 to 0.125
- k_gain: float32 [256], P(('seq', 'dp')), may hold values from 0.5 to 1.5
- w_v: float32 [2048, 256], P(('seq', 'dp')), may hold values from -0.125 to 0.125
- w_o: float32 [4096, 2048], P(('seq', 'dp')), may hold values from -1.5 to 1.5
- mlp_gain: float32 [2048], P(('seq', 'dp')), may hold values from 0.5 to 1.5
- w_gate: float32 [2048, 5632], P(('seq', 'dp')), may hold values from -0.125 to 0.125
- w_up: float32 [2048, 5632], P(('seq', 'dp')), may hold values from -0.125 to 0.125
- w_down: float32 [5632, 2048], P(('seq', 'dp')), may hold values from -0.078125 to 0.078125
Outputs:
- block_output: float32 [4, 1024, 2048], P('dp', 'seq')
- grad_input: float32 [4, 1024, 2048], P('dp', 'seq')
- grad_attn_gain: float32 [2048], P(('seq', 'dp'))
- grad_w_qa: float32 [2048, 1024], P(('seq', 'dp'))
- grad_q_gain: float32 [1024], P(('seq', 'dp'))
- grad_w_qb: float32 [1024, 4096], P(('seq', 'dp'))
- grad_w_k: float32 [2048, 256], P(('seq', 'dp'))
- grad_k_gain: float32 [256], P(('seq', 'dp'))
- grad_w_v: float32 [2048, 256], P(('seq', 'dp'))
- grad_w_o: float32 [4096, 2048], P(('seq', 'dp'))
- grad_mlp_gain: float32 [2048], P(('seq', 'dp'))
- grad_w_gate: float32 [2048, 5632], P(('seq', 'dp'))
- grad_w_up: float32 [2048, 5632], P(('seq', 'dp'))
- grad_w_down: float32 [5632, 2048], P(('seq', 'dp'))
The draws below stay inside these ranges and needn't reach their ends.
Inputs may be any that keep to these rules, and one draw needn't show every extreme that they name: Each row of lengths holds the lengths of the 4 packed sequences of one group, in order, summing to 1024; in every row the longest is exactly 512.
All inputs are finite; a program needn't handle non-finite values.
Results may differ from the reference program's by a relative error of at most 0.018.
The reference program's roundings to bfloat16 on the way count: a program that leaves them out, or rounds other values in their place, can miss the bound.
Values may be sent and summed in bfloat16 or wider, within the bound.
A program may use at most 384 MiB of HBM per device.

```python
import math
import jax
import jax.numpy as jnp
import numpy as np
from jax import lax

D = 2048
R = 1024
H = 16
E = 256
FF = 5632
SEQS = 4
GROUP = 1024
MAXLEN = 512
N_DP = 4


def block_scale(own_key, dims, cuts, least, high):
    factor_of, own = 1.0, jax.random.fold_in(own_key, 6)
    for axis_at, shards_of in cuts:
        draws = jnp.exp(jax.random.uniform(jax.random.fold_in(own, axis_at), (shards_of,), jnp.float32, least / len(cuts), high / len(cuts)))
        factor_of = factor_of * jnp.repeat(draws, dims[axis_at] // shards_of).reshape([-1 if axis == axis_at else 1 for axis in range(len(dims))])
    return factor_of


def length_profile(amount, total, reach, lean):
    portions = [(1 << 20) // math.isqrt(rank ** lean) + 1 for rank in range(2, amount + 1)]
    rest, holding = total - reach - (amount - 1), [1] * (amount - 1)
    while rest > 0:
        free = [i for i in range(amount - 1) if holding[i] < reach]
        mass, left = sum([portions[i] for i in free]), rest
        for i in free:
            extra = min(reach - holding[i], max(1, left * portions[i] // mass), rest)
            holding[i] = holding[i] + extra
            rest = rest - extra
    return np.array([reach] + holding)


def ragged_sizes(own_key, count, total, most, slope):
    if count == 2:
        one = jax.random.randint(own_key, (), max(1, total - most), min(most, total - 1) + 1)
        return jnp.stack([one, total - one])
    sizes = jnp.asarray(length_profile(count, total, most, slope), jnp.int32)
    twos = (count - 1) // 2
    giver, receiver = sizes[1:1 + 2 * twos:2], sizes[2:2 + 2 * twos:2]
    room = jnp.minimum(giver - 1, most - receiver)
    moved = jax.random.randint(jax.random.fold_in(own_key, 1), (twos,), 0, 1 << 20) % (room + 1)
    sizes = sizes.at[1:1 + 2 * twos:2].set(giver - moved).at[2:2 + 2 * twos:2].set(receiver + moved)
    return sizes[jax.random.permutation(jax.random.fold_in(own_key, 2), count)]


def gaussian(stream_key, extent, scale, most, cuts=(), kind=jnp.bfloat16):
    drawn = scale * jax.random.normal(stream_key, extent, jnp.float32)
    if cuts:
        drawn = drawn * block_scale(stream_key, extent, cuts, -0.22, 0.18)
    return jnp.clip(drawn, -most, most).astype(kind)


def setup_inputs(seed: int = 0) -> dict:
    splits = jax.random.split(jax.random.key(seed), 16)
    block_input = gaussian(splits[0], (N_DP, GROUP, D), 1.0, 6.0, ((0, 4), (1, 8)), jnp.float32)
    lengths = jax.vmap(lambda own: ragged_sizes(own, SEQS, GROUP, MAXLEN, 2))(jax.random.split(splits[1], N_DP)).reshape((N_DP, SEQS)).astype(jnp.int32)
    cotangent = gaussian(splits[2], (N_DP, GROUP, D), 1.0, 6.0, ((0, 4), (1, 8)), jnp.float32)
    attn_gain = jnp.clip(1.0 + 0.1 * jax.random.normal(splits[3], (D,), jnp.float32), 0.5, 1.5)
    w_qa = gaussian(splits[4], (D, R), D ** -0.5, 0.125, ((0, 32),), jnp.float32)
    q_gain = jnp.clip(1.0 + 0.1 * jax.random.normal(splits[5], (R,), jnp.float32), 0.5, 1.5)
    w_qb = gaussian(splits[6], (R, H * E), R ** -0.5, 0.1875, ((0, 32),), jnp.float32)
    w_k = gaussian(splits[7], (D, E), D ** -0.5, 0.125, ((0, 32),), jnp.float32)
    k_gain = jnp.clip(1.0 + 0.1 * jax.random.normal(splits[8], (E,), jnp.float32), 0.5, 1.5)
    w_v = gaussian(splits[9], (D, E), D ** -0.5, 0.125, ((0, 32),), jnp.float32)
    w_o = gaussian(splits[10], (H * E, D), (H * E // 256) ** -0.5, 1.5, ((0, 32),), jnp.float32)
    mlp_gain = jnp.clip(1.0 + 0.1 * jax.random.normal(splits[11], (D,), jnp.float32), 0.5, 1.5)
    w_gate = gaussian(splits[12], (D, FF), D ** -0.5, 0.125, ((0, 32),), jnp.float32)
    w_up = gaussian(splits[13], (D, FF), D ** -0.5, 0.125, ((0, 32),), jnp.float32)
    w_down = gaussian(splits[14], (FF, D), FF ** -0.5, 0.078125, ((0, 32),), jnp.float32)
    return dict(block_input=block_input, lengths=lengths, cotangent=cotangent, attn_gain=attn_gain, w_qa=w_qa, q_gain=q_gain, w_qb=w_qb, w_k=w_k, k_gain=k_gain, w_v=w_v, w_o=w_o, mlp_gain=mlp_gain, w_gate=w_gate, w_up=w_up, w_down=w_down)


@jax.custom_vjp
def low(v):
    return lax.optimization_barrier(v.astype(jnp.bfloat16)).astype(jnp.float32)

@jax.custom_vjp
def low_back(v):
    return v

def low_keep(v):
    return (low(v), None)

def low_pass(kept, grad):
    return (grad,)

def back_keep(v):
    return (v, None)

def back_low(kept, grad):
    return (low(grad),)
low.defvjp(low_keep, low_pass)
low_back.defvjp(back_keep, back_low)
eps_norm = 1e-06
big_negative = -1e+30

def product(left, right):
    return jnp.dot(left, right, precision=lax.Precision.HIGHEST, preferred_element_type=jnp.float32)

def rms_scale(values, gain_vec):
    inverse = lax.rsqrt(lax.optimization_barrier(jnp.mean(values * values, axis=-1, keepdims=True)) + eps_norm)
    return values * inverse * gain_vec

def rotate(values, cosine, sine_tab):
    half_width = values.shape[-1] // 2
    turned = jnp.concatenate([-values[..., half_width:], values[..., :half_width]], axis=-1)
    return values * cosine + turned * sine_tab

def layout(seq_lengths, group_tokens):
    seq_ends = jnp.cumsum(seq_lengths).astype(jnp.int32)
    places = jnp.arange(group_tokens, dtype=jnp.int32)
    passed = places[:, None] >= seq_ends[None, :]
    segment = lax.optimization_barrier(jnp.sum(passed.astype(jnp.int32), axis=1)).astype(jnp.int32)
    starts = lax.optimization_barrier(jnp.sum(jnp.where(passed, seq_lengths[None, :], 0), axis=1)).astype(jnp.int32)
    return (segment, places, (places - starts).astype(jnp.int32))

def rope_tables(offsets, width):
    half_width = width // 2
    frequency = jnp.exp(jnp.arange(half_width, dtype=jnp.float32) * (-2.0 * math.log(10000.0) / width))
    angles = offsets.astype(jnp.float32)[:, None] * frequency[None, :]
    angles = jnp.concatenate([angles, angles], axis=-1)
    return (jnp.cos(angles), jnp.sin(angles))

def attend_group(queries, keys_all, values_all, segment, places):
    group_tokens = queries.shape[0]
    block_rows = min(512, group_tokens)
    count_blocks = group_tokens // block_rows
    score_scale = 1.0 / math.sqrt(keys_all.shape[-1])

    def one_block(pieces):
        query_block, seg_block, place_block = pieces
        scores = low_back(jnp.einsum('thd,kd->thk', query_block, keys_all, precision=lax.Precision.HIGHEST) * score_scale)
        allowed = (seg_block[:, None] == segment[None, :]) & (places[None, :] <= place_block[:, None])
        scores = jnp.where(allowed[:, None, :], scores, big_negative)
        shifted = jnp.exp(scores - lax.optimization_barrier(jnp.max(scores, axis=-1, keepdims=True)))
        weights = shifted / lax.optimization_barrier(jnp.sum(shifted, axis=-1, keepdims=True))
        return jnp.einsum('thk,kd->thd', low(weights), values_all, precision=lax.Precision.HIGHEST)
    outputs = lax.map(jax.checkpoint(one_block), (queries.reshape(count_blocks, block_rows, queries.shape[1], queries.shape[2]), segment.reshape(count_blocks, block_rows), places.reshape(count_blocks, block_rows)))
    return outputs.reshape(queries.shape)

def forward(block_input, attn_gain, w_qa, q_gain, w_qb, w_k, k_gain, w_v, w_o, mlp_gain, w_gate, w_up, w_down, segment, places, cosine, sine_tab):
    groups, group_tokens, width = block_input.shape
    total_rows = groups * group_tokens
    flat_rows = block_input.reshape(total_rows, width)
    normed = low(rms_scale(flat_rows, low(attn_gain)))
    latent = low_back(product(normed, low(w_qa)))
    latent_low = low(rms_scale(latent, low(q_gain)))
    queries = low_back(product(latent_low, low(w_qb))).reshape(total_rows, H, E)
    queries = low(rotate(queries, cosine[:, None, :], sine_tab[:, None, :]))
    key_pre = low_back(product(normed, low(w_k)))
    keys_all = low(rotate(rms_scale(key_pre, low(k_gain)), cosine, sine_tab))
    values_all = low(low_back(product(normed, low(w_v))))
    attended = lax.map(lambda pieces: attend_group(pieces[0], pieces[1], pieces[2], pieces[3], pieces[4]), (queries.reshape(groups, group_tokens, H, E), keys_all.reshape(groups, group_tokens, E), values_all.reshape(groups, group_tokens, E), segment, places))
    attended = low(low_back(attended.reshape(total_rows, H * E)))
    mixed_rows = flat_rows + low_back(product(attended, low(w_o)))
    normed_two = low(rms_scale(mixed_rows, low(mlp_gain)))
    gate_act = low_back(product(normed_two, low(w_gate)))
    up_act = low_back(product(normed_two, low(w_up)))
    hidden = low(gate_act * jax.nn.sigmoid(gate_act) * up_act)
    output_rows = mixed_rows + low_back(product(hidden, low(w_down)))
    return output_rows.reshape(block_input.shape)

def reference(block_input, lengths, cotangent, attn_gain, w_qa, q_gain, w_qb, w_k, k_gain, w_v, w_o, mlp_gain, w_gate, w_up, w_down):
    group_tokens = block_input.shape[1]
    segment, places, offsets = jax.vmap(lambda length_row: layout(length_row, group_tokens))(lengths)
    cosine, sine_tab = rope_tables(offsets.reshape(-1), E)

    def wrapped(inp, gain_one, qa_mat, gain_latent, qb_mat, k_mat, gain_key, v_mat, o_mat, gain_two, gate_mat, up_mat, down_mat):
        return forward(inp, gain_one, qa_mat, gain_latent, qb_mat, k_mat, gain_key, v_mat, o_mat, gain_two, gate_mat, up_mat, down_mat, segment, places, cosine, sine_tab)
    output, pullback = jax.vjp(wrapped, block_input, attn_gain, w_qa, q_gain, w_qb, w_k, k_gain, w_v, w_o, mlp_gain, w_gate, w_up, w_down)
    gradients = pullback(cotangent)
    return (output, gradients[0], gradients[1], gradients[2], gradients[3], gradients[4], gradients[5], gradients[6], gradients[7], gradients[8], gradients[9], gradients[10], gradients[11], gradients[12])
```

```python
import math

import jax
import jax.numpy as jnp
from jax import lax
from jax.sharding import PartitionSpec as P

D = 2048
H = 16
E = 256


eps_norm = 1e-06
big_negative = -1e30


def rms_scale(values, gain_vec):
    inverse = lax.rsqrt(jnp.mean(values * values, axis=-1, keepdims=True) + eps_norm)
    return values * inverse * gain_vec


def norm_back(values, gain_vec, upstream):
    inverse = lax.rsqrt(jnp.mean(values * values, axis=-1, keepdims=True) + eps_norm)
    gain_grad = jnp.sum(upstream * values * inverse, axis=0)
    scaled = upstream * gain_vec
    value_grad = inverse * scaled - values * (inverse * inverse * inverse) * jnp.mean(
        scaled * values, axis=-1, keepdims=True
    )
    return (value_grad, gain_grad)


def rotate(values, cosine, sine_tab):
    half_width = values.shape[-1] // 2
    turned = jnp.concatenate([-values[..., half_width:], values[..., :half_width]], axis=-1)
    return values * cosine + turned * sine_tab


def rotate_back(upstream, cosine, sine_tab):
    half_width = upstream.shape[-1] // 2
    weighted = upstream * sine_tab
    turned = jnp.concatenate([weighted[..., half_width:], -weighted[..., :half_width]], axis=-1)
    return upstream * cosine + turned


def layout(seq_lengths, group_tokens):
    seq_ends = jnp.cumsum(seq_lengths)
    places = jnp.arange(group_tokens, dtype=jnp.int32)
    passed = places[:, None] >= seq_ends[None, :]
    segment = jnp.sum(passed.astype(jnp.int32), axis=1)
    starts = jnp.sum(jnp.where(passed, seq_lengths[None, :], 0), axis=1)
    return (segment, places, places - starts)


def rope_tables(offsets, width):
    half_width = width // 2
    frequency = jnp.exp(
        jnp.arange(half_width, dtype=jnp.float32) * (-2.0 * math.log(10000.0) / width)
    )
    angles = offsets.astype(jnp.float32)[:, None] * frequency[None, :]
    angles = jnp.concatenate([angles, angles], axis=-1)
    return (jnp.cos(angles), jnp.sin(angles))


def gather_columns(weight, parts):
    rows, cols = weight.shape
    low = weight.astype(jnp.bfloat16).reshape(rows, parts, cols // parts)
    mine = lax.all_to_all(low, "seq", split_axis=1, concat_axis=0, tiled=False)
    mine = mine.reshape(parts, rows, cols // parts)
    full = lax.all_gather(mine, "dp", axis=1, tiled=False)
    return full.reshape(-1, cols // parts)


def gather_rows(weight):
    return lax.all_gather(weight.astype(jnp.bfloat16), "dp", axis=0, tiled=True)


def scatter_columns(grad, parts, groups):
    rows, cols = grad.shape
    piece = rows // (parts * groups)
    low = grad.astype(jnp.bfloat16).reshape(parts, groups, piece, cols)
    low = jnp.transpose(low, (1, 0, 2, 3)).reshape(rows, cols)
    own = lax.psum_scatter(low, "dp", scatter_dimension=0, tiled=True).reshape(parts, piece, cols)
    back = lax.all_to_all(own, "seq", split_axis=0, concat_axis=1, tiled=False)
    return back.reshape(piece, parts * cols).astype(jnp.float32)


def scatter_rows(grad):
    return lax.psum_scatter(
        grad.astype(jnp.bfloat16), "dp", scatter_dimension=0, tiled=True
    ).astype(jnp.float32)


def seq_gather(rows):
    return lax.all_gather(rows, "seq", axis=0, tiled=True)


def seq_scatter(rows):
    return lax.psum_scatter(
        rows.astype(jnp.bfloat16), "seq", scatter_dimension=0, tiled=True
    ).astype(jnp.float32)


def dot(left, right):
    return jnp.dot(left, right, preferred_element_type=jnp.float32)


def local(
    block_input,
    lengths,
    cotangent,
    attn_gain,
    w_qa,
    q_gain,
    w_qb,
    w_k,
    k_gain,
    w_v,
    w_o,
    mlp_gain,
    w_gate,
    w_up,
    w_down,
):
    tok_rows = block_input.shape[1]
    parts = lax.axis_size("seq")
    groups = lax.axis_size("dp")
    heads = H // parts
    group_tokens = tok_rows * parts
    first_row = lax.axis_index("seq") * tok_rows
    segment, places, offsets = layout(lengths[0], group_tokens)
    cos_all, sin_all = rope_tables(offsets, E)
    cosine = lax.dynamic_slice_in_dim(cos_all, first_row, tok_rows, 0)
    sine_tab = lax.dynamic_slice_in_dim(sin_all, first_row, tok_rows, 0)
    score_scale = 1.0 / math.sqrt(E)
    flat_rows = block_input.reshape(tok_rows, D)
    out_grad = cotangent.reshape(tok_rows, D)
    both = ("seq", "dp")
    rank = w_qa.shape[1]

    gains = jnp.concatenate([attn_gain, q_gain, k_gain, mlp_gain]).astype(jnp.bfloat16)
    gains = lax.all_gather(gains, both, axis=0, tiled=False).astype(jnp.float32)
    n1, n2, n3 = attn_gain.shape[0], q_gain.shape[0], k_gain.shape[0]
    gain_one = gains[:, :n1].reshape(-1)
    gain_latent = gains[:, n1 : n1 + n2].reshape(-1)
    gain_key = gains[:, n1 + n2 : n1 + n2 + n3].reshape(-1)
    gain_two = gains[:, n1 + n2 + n3 :].reshape(-1)

    w_in = jnp.concatenate([w_qa, w_k, w_v], axis=1).astype(jnp.bfloat16)
    w_in = lax.all_gather(w_in, both, axis=0, tiled=True)
    qb_cols = gather_columns(w_qb, parts)
    o_rows = gather_rows(w_o)
    gate_cols = gather_columns(w_gate, parts)
    up_cols = gather_columns(w_up, parts)
    down_rows = gather_rows(w_down)

    normed = rms_scale(flat_rows, gain_one).astype(jnp.bfloat16)
    projected = dot(normed, w_in)
    latent, key_pre, value_pre = (
        projected[:, :rank],
        projected[:, rank : rank + E],
        projected[:, rank + E :],
    )
    latent_low = rms_scale(latent, gain_latent).astype(jnp.bfloat16)
    key_low = rotate(rms_scale(key_pre, gain_key), cosine, sine_tab).astype(jnp.bfloat16)
    value_low = value_pre.astype(jnp.bfloat16)
    gathered = seq_gather(jnp.concatenate([latent_low, key_low, value_low], axis=1))
    latent_all = gathered[:, :rank]
    keys_all = gathered[:, rank : rank + E]
    values_all = gathered[:, rank + E :]
    grad_all = seq_gather(out_grad.astype(jnp.bfloat16))

    query = dot(latent_all, qb_cols).reshape(group_tokens, heads, E)
    query = jnp.transpose(query, (1, 0, 2))
    q_rot = rotate(query, cos_all[None], sin_all[None]).astype(jnp.bfloat16)
    allowed = (segment[:, None] == segment[None, :]) & (places[None, :] <= places[:, None])
    scores = (
        jnp.einsum("htd,kd->htk", q_rot, keys_all, preferred_element_type=jnp.float32)
        * score_scale
    )
    scores = jnp.where(allowed[None], scores, big_negative)
    shifted = jnp.exp(scores - jnp.max(scores, axis=-1, keepdims=True))
    probs = shifted / jnp.sum(shifted, axis=-1, keepdims=True)
    probs_low = probs.astype(jnp.bfloat16)
    attended = jnp.einsum("htk,kd->htd", probs_low, values_all, preferred_element_type=jnp.float32)
    attended_low = jnp.transpose(attended.astype(jnp.bfloat16), (1, 0, 2)).reshape(
        group_tokens, heads * E
    )
    mixed_rows = flat_rows + seq_scatter(dot(attended_low, o_rows))
    normed_two = rms_scale(mixed_rows, gain_two).astype(jnp.bfloat16)
    two_all = seq_gather(normed_two)

    gate_act = dot(two_all, gate_cols)
    up_act = dot(two_all, up_cols)
    sigmoid_gate = jax.nn.sigmoid(gate_act)
    hidden = (gate_act * sigmoid_gate * up_act).astype(jnp.bfloat16)
    hidden_grad = jnp.einsum("td,fd->tf", grad_all, down_rows, preferred_element_type=jnp.float32)
    gate_grad = (
        hidden_grad * up_act * (sigmoid_gate * (1.0 + gate_act * (1.0 - sigmoid_gate)))
    ).astype(jnp.bfloat16)
    up_grad = (hidden_grad * (gate_act * sigmoid_gate)).astype(jnp.bfloat16)
    two_grad = seq_scatter(
        jnp.einsum("tf,df->td", gate_grad, gate_cols, preferred_element_type=jnp.float32)
        + jnp.einsum("tf,df->td", up_grad, up_cols, preferred_element_type=jnp.float32)
    )
    output_rows = mixed_rows + seq_scatter(dot(hidden, down_rows))
    down_shard = scatter_rows(
        jnp.einsum("tf,td->fd", hidden, grad_all, preferred_element_type=jnp.float32)
    )
    gate_shard = scatter_columns(
        jnp.einsum("td,tf->df", two_all, gate_grad, preferred_element_type=jnp.float32),
        parts,
        groups,
    )
    up_shard = scatter_columns(
        jnp.einsum("td,tf->df", two_all, up_grad, preferred_element_type=jnp.float32),
        parts,
        groups,
    )

    mixed_part, gain_two_grad = norm_back(mixed_rows, gain_two, two_grad)
    mixed_grad = out_grad + mixed_part
    mixed_all = seq_gather(mixed_grad.astype(jnp.bfloat16))
    o_shard = scatter_rows(
        jnp.einsum("tf,td->fd", attended_low, mixed_all, preferred_element_type=jnp.float32)
    )
    att_grad = jnp.einsum("td,fd->tf", mixed_all, o_rows, preferred_element_type=jnp.float32)
    att_grad = jnp.transpose(
        att_grad.astype(jnp.bfloat16).reshape(group_tokens, heads, E), (1, 0, 2)
    )
    delta_rows = jnp.sum(att_grad.astype(jnp.float32) * attended, axis=-1)
    value_grads = jnp.einsum(
        "htk,htd->kd", probs_low, att_grad, preferred_element_type=jnp.float32
    )
    prob_grad = jnp.einsum("htd,kd->htk", att_grad, values_all, preferred_element_type=jnp.float32)
    score_grad = (probs * (prob_grad - delta_rows[..., None])).astype(jnp.bfloat16)
    query_grad = (
        jnp.einsum("htk,kd->htd", score_grad, keys_all, preferred_element_type=jnp.float32)
        * score_scale
    )
    key_grads = (
        jnp.einsum("htk,htd->kd", score_grad, q_rot, preferred_element_type=jnp.float32)
        * score_scale
    )
    query_grad = rotate_back(query_grad, cos_all[None], sin_all[None]).astype(jnp.bfloat16)
    query_grad = jnp.transpose(query_grad, (1, 0, 2)).reshape(group_tokens, heads * E)
    qb_shard = scatter_columns(
        jnp.einsum("tr,tf->rf", latent_all, query_grad, preferred_element_type=jnp.float32),
        parts,
        groups,
    )
    latent_part = jnp.einsum("tf,rf->tr", query_grad, qb_cols, preferred_element_type=jnp.float32)
    own = seq_scatter(jnp.concatenate([latent_part, key_grads, value_grads], axis=1))
    latent_grad, gain_latent_grad = norm_back(latent, gain_latent, own[:, :rank])
    key_back = rotate_back(own[:, rank : rank + E], cosine, sine_tab)
    key_grad, gain_key_grad = norm_back(key_pre, gain_key, key_back)
    in_grad = jnp.concatenate([latent_grad, key_grad, own[:, rank + E :]], axis=1).astype(
        jnp.bfloat16
    )
    in_wgrad = jnp.einsum("td,tr->dr", normed, in_grad, preferred_element_type=jnp.float32)
    in_shard = lax.psum_scatter(
        in_wgrad.astype(jnp.bfloat16), both, scatter_dimension=0, tiled=True
    ).astype(jnp.float32)
    normed_grad = jnp.einsum("tr,dr->td", in_grad, w_in, preferred_element_type=jnp.float32)
    input_part, gain_one_grad = norm_back(flat_rows, gain_one, normed_grad)
    input_grad = mixed_grad + input_part

    devices = parts * groups
    gain_grads = jnp.concatenate(
        [
            gain_one_grad.reshape(devices, -1),
            gain_latent_grad.reshape(devices, -1),
            gain_key_grad.reshape(devices, -1),
            gain_two_grad.reshape(devices, -1),
        ],
        axis=1,
    )
    gain_own = lax.psum_scatter(gain_grads, both, scatter_dimension=0, tiled=False)
    return (
        output_rows.reshape(1, tok_rows, D),
        input_grad.reshape(1, tok_rows, D),
        gain_own[:n1],
        in_shard[:, :rank],
        gain_own[n1 : n1 + n2],
        qb_shard,
        in_shard[:, rank : rank + E],
        gain_own[n1 + n2 : n1 + n2 + n3],
        in_shard[:, rank + E :],
        o_shard,
        gain_own[n1 + n2 + n3 :],
        gate_shard,
        up_shard,
        down_shard,
    )


def solution(mesh):
    return jax.shard_map(
        local,
        mesh=mesh,
        in_specs=(
            P("dp", "seq", None),
            P("dp", None),
            P("dp", "seq", None),
            P(("seq", "dp")),
            P(("seq", "dp"), None),
            P(("seq", "dp")),
            P(("seq", "dp"), None),
            P(("seq", "dp"), None),
            P(("seq", "dp")),
            P(("seq", "dp"), None),
            P(("seq", "dp"), None),
            P(("seq", "dp")),
            P(("seq", "dp"), None),
            P(("seq", "dp"), None),
            P(("seq", "dp"), None),
        ),
        out_specs=(
            P("dp", "seq", None),
            P("dp", "seq", None),
            P(("seq", "dp")),
            P(("seq", "dp"), None),
            P(("seq", "dp")),
            P(("seq", "dp"), None),
            P(("seq", "dp"), None),
            P(("seq", "dp")),
            P(("seq", "dp"), None),
            P(("seq", "dp"), None),
            P(("seq", "dp")),
            P(("seq", "dp"), None),
            P(("seq", "dp"), None),
            P(("seq", "dp"), None),
        ),
        check_vma=False,
    )
```

```python
import math

import jax
import jax.numpy as jnp
from jax import lax
from jax.experimental import pallas as pl
from jax.experimental.pallas import tpu as pltpu
from jax.sharding import PartitionSpec as P

D = 2048
H = 16
E = 256


MESH = pl.DeviceIdType.MESH
STEP = 16
VMEM_LIMIT = 48 * 1024 * 1024
COST = pl.CostEstimate(flops=0, transcendentals=0, bytes_accessed=1024)

eps_norm = 1e-06
big_negative = -1e30


def rms_scale(values, gain_vec):
    inverse = lax.rsqrt(jnp.mean(values * values, axis=-1, keepdims=True) + eps_norm)
    return values * inverse * gain_vec


def norm_back(values, gain_vec, upstream):
    inverse = lax.rsqrt(jnp.mean(values * values, axis=-1, keepdims=True) + eps_norm)
    gain_grad = jnp.sum(upstream * values * inverse, axis=0)
    scaled = upstream * gain_vec
    value_grad = inverse * scaled - values * (inverse * inverse * inverse) * jnp.mean(
        scaled * values, axis=-1, keepdims=True
    )
    return (value_grad, gain_grad)


def rotate(values, cosine, sine_tab):
    half_width = values.shape[-1] // 2
    turned = jnp.concatenate([-values[..., half_width:], values[..., :half_width]], axis=-1)
    return values * cosine + turned * sine_tab


def rotate_back(upstream, cosine, sine_tab):
    half_width = upstream.shape[-1] // 2
    weighted = upstream * sine_tab
    turned = jnp.concatenate([weighted[..., half_width:], -weighted[..., :half_width]], axis=-1)
    return upstream * cosine + turned


def layout(seq_lengths, group_tokens):
    seq_ends = jnp.cumsum(seq_lengths)
    places = jnp.arange(group_tokens, dtype=jnp.int32)
    passed = places[:, None] >= seq_ends[None, :]
    segment = jnp.sum(passed.astype(jnp.int32), axis=1)
    starts = jnp.sum(jnp.where(passed, seq_lengths[None, :], 0), axis=1)
    return (segment, places, places - starts)


def rope_tables(offsets, width):
    half_width = width // 2
    frequency = jnp.exp(
        jnp.arange(half_width, dtype=jnp.float32) * (-2.0 * math.log(10000.0) / width)
    )
    angles = offsets.astype(jnp.float32)[:, None] * frequency[None, :]
    angles = jnp.concatenate([angles, angles], axis=-1)
    return (jnp.cos(angles), jnp.sin(angles))


VMEM = pl.BlockSpec(memory_space=pltpu.VMEM)
ANY = pl.BlockSpec(memory_space=pl.ANY)
SIBLING = (1, 0)


def flip(index, bits):
    out, power = index, 1
    while power <= bits:
        if bits & power:
            out = out + power - 2 * power * ((index // power) % 2)
        power *= 2
    return out


def here():
    return lax.axis_index("seq"), lax.axis_index("dp")


def device(mask):
    me, group = here()
    return flip(me, mask[0]), flip(group, mask[1])


def copy_to(source, target, sems, seq_to, dp_to):
    return pltpu.make_async_remote_copy(
        src_ref=source,
        dst_ref=target,
        send_sem=sems.at[0],
        recv_sem=sems.at[1],
        device_id=(seq_to, dp_to),
        device_id_type=MESH,
    )


def remote(source, target, sems, mask):
    copy = copy_to(source, target, sems, *device(mask))
    copy.start()
    return copy


def keep(source, target, sem):
    copy = pltpu.make_async_copy(source, target, sem)
    copy.start()
    return copy


class Task:
    def __init__(self, inputs, outputs, scratch, masks, run):
        self.inputs, self.outputs, self.scratch = inputs, outputs, scratch
        self.masks, self.run = masks, run


def launch(name, collective_id, tasks, needs=(), passes=()):
    masks = sorted({mask for task in tasks for mask in task.masks})
    n_in = sum(len(task.inputs) for task in tasks)
    n_out = sum(len(task.outputs) for task in tasks)

    def body(*refs):
        refs = list(refs)
        ins = refs[:n_in]
        refs = refs[n_in + len(needs) + len(passes) :]
        outs, scratch = refs[:n_out], refs[n_out + len(passes) :]
        barrier = pltpu.get_barrier_semaphore()
        for mask in masks:
            pl.semaphore_signal(barrier, inc=1, device_id=device(mask), device_id_type=MESH)
        pl.semaphore_wait(barrier, len(masks))
        running = []
        for task in tasks:
            a, b, c = len(task.inputs), len(task.outputs), len(task.scratch)
            running.append(task.run(ins[:a], outs[:b], scratch[:c]))
            ins, outs, scratch = ins[a:], outs[b:], scratch[c:]
        while running:
            for step in list(running):
                if next(step, "done") == "done":
                    running.remove(step)

    inputs = [pair for task in tasks for pair in task.inputs]
    outputs = [pair for task in tasks for pair in task.outputs]
    results = pl.pallas_call(
        body,
        name=name,
        out_shape=[shape for shape, _ in outputs]
        + [jax.ShapeDtypeStruct(a.shape, a.dtype) for a in passes],
        in_specs=[spec for _, spec in inputs] + [ANY] * (len(needs) + len(passes)),
        out_specs=[spec for _, spec in outputs] + [ANY] * len(passes),
        input_output_aliases={n_in + len(needs) + i: n_out + i for i in range(len(passes))},
        scratch_shapes=[shape for task in tasks for shape in task.scratch],
        compiler_params=pltpu.CompilerParams(
            collective_id=collective_id, has_side_effects=True, vmem_limit_bytes=VMEM_LIMIT
        ),
        cost_estimate=COST,
    )(*[array for array, _ in inputs], *needs, *passes)
    results, split = list(results), []
    for task in tasks:
        split.append(results[: len(task.outputs)])
        results = results[len(task.outputs) :]
    return split + results


def rows_loop(start, stop, step):
    def one(i, carry):
        step(pl.ds(pl.multiple_of(i * STEP, STEP), STEP))
        return carry

    lax.fori_loop(start // STEP, stop // STEP, one, 0)


def axis_masks(axis):
    if axis == "chip":
        return [(2 * j, 0) for j in range(1, lax.axis_size("seq") // 2)]
    return [(0, j) for j in range(1, lax.axis_size("dp"))]


def axis_block(axis, mask=(0, 0)):
    seq_at, dp_at = device(mask)
    return seq_at if axis == "chip" else dp_at * 2 + seq_at % 2


def line_masks():
    masks, power = [], 2
    while power <= lax.axis_size("dp"):
        masks.append((0, power - 1))
        power *= 2
    return masks


def spread_masks(axis):
    if axis == "dp":
        return [SIBLING] + line_masks()
    return [SIBLING] + axis_masks(axis)


def spread(axis, low, all_ref, keep_sem, sems):
    own = all_ref.at[axis_block(axis)]
    rows = low.shape[0]
    sends = []
    if axis == "dp":
        yield from spread_line(low, all_ref, keep_sem, sems)
        return
    masks = axis_masks(axis)
    square = len(masks) == 3
    direct = [(2, 0), (4, 0)] if square else masks
    for i, mask in enumerate(direct):
        sends.append(remote(low, own, sems.at[i], mask))
    beside = [remote(low, own, sems.at[len(masks)], SIBLING)]
    kept = keep(low, own, keep_sem)
    yield
    at, halves = len(masks) + 1, []

    def block(mask):
        return all_ref.at[axis_block(axis, mask)]

    def half(mask, which):
        return all_ref.at[axis_block(axis, mask), pl.ds(which * (rows // 2), rows // 2)]

    for i, mask in enumerate(direct):
        sends[i].wait_recv()
        if square:
            halves.append(remote(half(mask, i), half(mask, i), sems.at[at], direct[1 - i]))
            at += 1
        beside.append(remote(block(mask), block(mask), sems.at[at], SIBLING))
        at += 1
        yield
    for i, copy in enumerate(halves):
        copy.wait_recv()
        part = half((6, 0), i)
        beside.append(remote(part, part, sems.at[at], SIBLING))
        at += 1
        yield
    for copy in beside:
        copy.wait_recv()
    for copy in sends + halves + beside:
        copy.wait_send()
    kept.wait()


def spread_line(low, all_ref, keep_sem, sems):
    me, group = here()
    core, groups = me % 2, lax.axis_size("dp")
    own = all_ref.at[axis_block("dp")]
    kept = keep(low, own, keep_sem)
    beside = remote(low, own, sems.at[0], SIBLING)

    def at(way, k, kind):
        return sems.at[1 + (way * (groups - 1) + k) * 2 + kind]

    def hop(way, k):
        step = 1 - 2 * way
        block = all_ref.at[(group - step * k) * 2 + core]
        return copy_to(low if k == 0 else block, block, at(way, k, 0), me, group + step)

    def landed(way, k):
        block = all_ref.at[(group - (1 - 2 * way) * (k + 1)) * 2 + core]
        return copy_to(block, block, at(way, k, 0), *device(SIBLING))

    def aside(way, k):
        block = all_ref.at[(group - (1 - 2 * way) * (k + 1)) * 2 + core]
        return copy_to(block, block, at(way, k, 1), *device(SIBLING))

    def sends(way, k):
        if way == 0:
            return (group >= k) & (group < groups - 1)
        return (group + k < groups) & (group > 0)

    def lands(way, k):
        return (group >= k + 1) if way == 0 else (group + k + 1 < groups)

    for k in range(groups - 1):
        for way in range(2):

            @pl.when(sends(way, k))
            def _(way=way, k=k):
                hop(way, k).start()

        yield
        for way in range(2):

            @pl.when(lands(way, k))
            def _(way=way, k=k):
                landed(way, k).wait_recv()
                aside(way, k).start()

    yield
    beside.wait_recv()
    for k in range(groups - 1):
        for way in range(2):

            @pl.when(lands(way, k))
            def _(way=way, k=k):
                aside(way, k).wait()

            @pl.when(sends(way, k))
            def _(way=way, k=k):
                hop(way, k).wait_send()

    beside.wait_send()
    kept.wait()


def exchange(
    partial,
    row_operands,
    vec_operands,
    row_function,
    own_widths,
    low_width,
    vec_width,
    sum_axis="chip",
    spread_axis="chip",
):
    blocks, rows, cols = partial.shape
    far = blocks // 2
    n_rows = len(row_operands)
    masks = axis_masks(sum_axis)
    square = sum_axis == "chip" and len(masks) == 3
    out_blocks = lax.axis_size("seq") if spread_axis == "chip" else 2 * lax.axis_size("dp")
    order = list(range(far - 1, 0, -1)) + [0]
    at_mask = [(0, 0)] + masks

    def run(ins, outs, scratch):
        ins, outs = list(ins), list(outs)
        partial_ref = ins.pop(0)
        row_refs, vec_refs = ins[:n_rows], ins[n_rows:]
        all_ref = outs.pop(0) if low_width else None
        vec_out = outs.pop(-1) if vec_width else None
        mine, beside, arrived, low, local_sem, sems, out_sems = scratch

        across, loads = {}, {}
        for j in order:
            block = axis_block(sum_axis, at_mask[j])
            other = axis_block(sum_axis, (at_mask[j][0] + 1, at_mask[j][1]))
            across[j] = remote(partial_ref.at[other], beside.at[j], sems.at[j], SIBLING)
            loads[j] = keep(partial_ref.at[block], mine.at[j], local_sem.at[j])
        yield
        sent = []

        def settle(j, low_row=0, high_row=rows, more=None):
            def add(at):
                total = mine[j, at, :].astype(jnp.float32) + beside[j, at, :].astype(jnp.float32)
                if more is not None:
                    total = total + arrived[more, at, :].astype(jnp.float32)
                mine[j, at, :] = total.astype(jnp.bfloat16)

            rows_loop(low_row, high_row, add)

        if square:
            middle = rows // 2
            first, second = pl.ds(0, middle), pl.ds(middle, middle)
            for j in (3, 1, 2):
                loads[j].wait()
                across[j].wait_recv()
                if j == 3:
                    settle(3)
                elif j == 1:
                    settle(1, 0, middle)
                else:
                    settle(2, middle, rows)
                base = far + 2 * (j - 1)
                if j in (3, 1):
                    sent.append(
                        remote(mine.at[j, first], arrived.at[j, first], sems.at[base], (2, 0))
                    )
                if j in (3, 2):
                    sent.append(
                        remote(mine.at[j, second], arrived.at[j, second], sems.at[base + 1], (4, 0))
                    )
            yield
            diagonal_x, diagonal_y = sent[0], sent[1]
            diagonal_x.wait_recv()
            settle(2, 0, middle, more=3)
            sent.append(
                remote(mine.at[2, first], arrived.at[2, first], sems.at[far + 2], (4, 0))
            )
            diagonal_y.wait_recv()
            settle(1, middle, rows, more=3)
            sent.append(
                remote(mine.at[1, second], arrived.at[1, second], sems.at[far + 1], (2, 0))
            )
            yield
            adds = [1, 2]
            landed = sent[2:]
        else:
            for j in order[:-1]:
                loads[j].wait()
                across[j].wait_recv()
                settle(j)
                sent.append(remote(mine.at[j], arrived.at[j], sems.at[far + j], at_mask[j]))
                yield
            adds = order[:-1]
            landed = sent
        loads[0].wait()
        across[0].wait_recv()
        for copy in landed:
            copy.wait_recv()
        if vec_width:
            vec_out[...] = jnp.zeros_like(vec_out)
        vecs = [v[...] for v in vec_refs]

        def finish(at):
            total = mine[0, at, :].astype(jnp.float32) + beside[0, at, :].astype(jnp.float32)
            for j in adds:
                total = total + arrived[j, at, :].astype(jnp.float32)
            low_now, own_now, vec_now = row_function(total, [r[at, :] for r in row_refs], vecs)
            if low_width:
                low[at, :] = low_now.astype(jnp.bfloat16)
            for ref, value in zip(outs, own_now, strict=True):
                ref[at, :] = value
            if vec_width:
                vec_out[...] += vec_now

        rows_loop(0, rows, finish)
        if low_width:
            yield from spread(spread_axis, low, all_ref, local_sem.at[0], out_sems)
        for copy in list(across.values()) + sent:
            copy.wait_send()

    outputs = []
    if low_width:
        outputs.append((jax.ShapeDtypeStruct((out_blocks, rows, low_width), jnp.bfloat16), ANY))
    outputs += [(jax.ShapeDtypeStruct((rows, width), jnp.float32), VMEM) for width in own_widths]
    if vec_width:
        outputs.append((jax.ShapeDtypeStruct((STEP, vec_width), jnp.float32), VMEM))
    return Task(
        [(partial, ANY)] + [(a, VMEM) for a in list(row_operands) + list(vec_operands)],
        outputs,
        [
            pltpu.VMEM((far, rows, cols), jnp.bfloat16),
            pltpu.VMEM((far, rows, cols), jnp.bfloat16),
            pltpu.VMEM((far, rows, cols), jnp.bfloat16),
            pltpu.VMEM((rows, max(low_width, 128)), jnp.bfloat16),
            pltpu.SemaphoreType.DMA((far,)),
            pltpu.SemaphoreType.DMA((far + max(6, far), 2)),
            pltpu.SemaphoreType.DMA((spread_sems(spread_axis), 2)),
        ],
        [SIBLING] + masks + (spread_masks(spread_axis) if low_width else []),
        run,
    )


def spread_sems(axis):
    if axis == "dp":
        return 1 + 4 * (lax.axis_size("dp") - 1)
    return 2 * lax.axis_size("seq")


def gather(low, axis):
    rows, cols = low.shape
    blocks = lax.axis_size("seq") if axis == "chip" else 2 * lax.axis_size("dp")

    def run(ins, outs, scratch):
        yield from spread(axis, ins[0], outs[0], scratch[0].at[0], scratch[1])

    return Task(
        [(low, ANY)],
        [(jax.ShapeDtypeStruct((blocks, rows, cols), low.dtype), ANY)],
        [pltpu.SemaphoreType.DMA((1,)), pltpu.SemaphoreType.DMA((spread_sems(axis), 2))],
        spread_masks(axis),
        run,
    )


def family(kind):
    parts, groups = lax.axis_size("seq"), lax.axis_size("dp")
    if kind == "seq":
        return [(m, 0) for m in range(1, parts)], lambda s, d: s
    if kind == "dp":
        return [(0, m) for m in range(1, groups)], lambda s, d: d
    return [(m % 2, m // 2) for m in range(1, 2 * groups)], lambda s, d: d * 2 + s % 2


def swap(array, kind, repeat=False):
    masks, index = family(kind)

    def run(ins, outs, scratch):
        own = index(*here())
        copies = [keep(ins[0] if repeat else ins[0].at[own], outs[0].at[own], scratch[0].at[0])]
        for i, mask in enumerate(masks):
            source = ins[0] if repeat else ins[0].at[index(*device(mask))]
            copies.append(remote(source, outs[0].at[own], scratch[1].at[i], mask))
        yield
        for copy in copies:
            copy.wait()

    shape = (len(masks) + 1,) + array.shape if repeat else array.shape
    return Task(
        [(array, ANY)],
        [(jax.ShapeDtypeStruct(shape, array.dtype), ANY)],
        [pltpu.SemaphoreType.DMA((1,)), pltpu.SemaphoreType.DMA((len(masks), 2))],
        masks,
        run,
    )


def gather_both(array):
    seq_masks, dp_masks = family("seq")[0], family("dp")[0]
    parts, groups = lax.axis_size("seq"), lax.axis_size("dp")

    def run(ins, outs, scratch):
        me, group = here()
        (small,), (everything, line) = ins, outs
        copies = [keep(small, line.at[group], scratch[0].at[0])]
        for i, mask in enumerate(dp_masks):
            copies.append(remote(small, line.at[group], scratch[1].at[i], mask))
        yield
        for copy in copies:
            copy.wait()
        copies = [keep(line, everything.at[me], scratch[0].at[1])]
        for i, mask in enumerate(seq_masks):
            at = scratch[1].at[len(dp_masks) + i]
            copies.append(remote(line, everything.at[me], at, mask))
        yield
        for copy in copies:
            copy.wait()

    return Task(
        [(array, VMEM)],
        [
            (jax.ShapeDtypeStruct((parts, groups) + array.shape, array.dtype), VMEM),
            (jax.ShapeDtypeStruct((groups,) + array.shape, array.dtype), VMEM),
        ],
        [
            pltpu.SemaphoreType.DMA((2,)),
            pltpu.SemaphoreType.DMA((len(seq_masks) + len(dp_masks), 2)),
        ],
        seq_masks + dp_masks,
        run,
    )


def sum_both(array):
    seq_masks, dp_masks = family("seq")[0], family("dp")[0]

    def run(ins, outs, scratch):
        me, group = here()
        stage_one, line, stage_two, local_sem, sems = scratch
        copies = [keep(ins[0].at[me], stage_one.at[me], local_sem.at[0])]
        for i, mask in enumerate(seq_masks):
            source = ins[0].at[flip(me, mask[0])]
            copies.append(remote(source, stage_one.at[me], sems.at[i], mask))
        yield
        for copy in copies:
            copy.wait()
        line[...] = jnp.sum(stage_one[...], axis=0)
        copies = [keep(line.at[group], stage_two.at[group], local_sem.at[1])]
        for i, mask in enumerate(dp_masks):
            at = sems.at[len(seq_masks) + i]
            copies.append(remote(line.at[flip(group, mask[1])], stage_two.at[group], at, mask))
        yield
        for copy in copies:
            copy.wait()
        outs[0][...] = jnp.sum(stage_two[...], axis=0)

    return Task(
        [(array, VMEM)],
        [(jax.ShapeDtypeStruct(array.shape[2:], array.dtype), VMEM)],
        [
            pltpu.VMEM(array.shape, array.dtype),
            pltpu.VMEM(array.shape[1:], array.dtype),
            pltpu.VMEM(array.shape[1:], array.dtype),
            pltpu.SemaphoreType.DMA((2,)),
            pltpu.SemaphoreType.DMA((len(seq_masks) + len(dp_masks), 2)),
        ],
        seq_masks + dp_masks,
        run,
    )


def tie(value, needs):
    def body(*refs):
        pass

    return pl.pallas_call(
        body,
        name="tie",
        out_shape=jax.ShapeDtypeStruct(value.shape, value.dtype),
        in_specs=[ANY] * (1 + len(needs)),
        out_specs=ANY,
        input_output_aliases={0: 0},
        cost_estimate=COST,
    )(value, *needs)


def dot(left, right):
    return jnp.dot(left, right, preferred_element_type=jnp.float32)


def back_rows(values, gain, upstream):
    inverse = lax.rsqrt(jnp.mean(values * values, axis=-1, keepdims=True) + eps_norm)
    scaled = upstream * gain
    value_grad = inverse * scaled - values * (inverse * inverse * inverse) * jnp.mean(
        scaled * values, axis=-1, keepdims=True
    )
    return value_grad, upstream * values * inverse


def columns(weight, parts):
    rows, cols = weight.shape
    low = weight.astype(jnp.bfloat16).reshape(rows, parts, cols // parts)
    return jnp.transpose(low, (1, 0, 2))


def join(pieces):
    parts, rows, cols = pieces.shape
    full = lax.all_gather(pieces.reshape(parts * rows, cols), "dp", axis=0, tiled=True)
    full = full.reshape(-1, parts, rows, cols)
    return jnp.transpose(full, (1, 0, 2, 3)).reshape(-1, cols)


def scatter_columns(grad, parts, groups):
    rows, cols = grad.shape
    piece = rows // (parts * groups)
    low = grad.astype(jnp.bfloat16).reshape(parts, groups, piece, cols)
    low = jnp.transpose(low, (1, 0, 2, 3)).reshape(rows, cols)
    own = lax.psum_scatter(low, "dp", scatter_dimension=0, tiled=True)
    return own.reshape(parts, piece, cols), low


def scatter_rows(grad):
    low = grad.astype(jnp.bfloat16)
    return lax.psum_scatter(low, "dp", scatter_dimension=0, tiled=True), low


def unfold(pieces):
    parts, rows, cols = pieces.shape
    return jnp.transpose(pieces, (1, 0, 2)).reshape(rows, parts * cols).astype(jnp.float32)


def line_columns(weight, chips, groups):
    rows, cols = weight.shape
    low = weight.astype(jnp.bfloat16).reshape(rows, chips, 2, groups, -1)
    return jnp.transpose(low, (3, 2, 0, 1, 4)).reshape(2 * groups, rows, -1)


def line_unfold(pieces, chips, groups):
    rows = pieces.shape[1]
    full = pieces.reshape(groups, 2, rows, chips, -1)
    return jnp.transpose(full, (2, 3, 1, 0, 4)).reshape(rows, -1).astype(jnp.float32)


def chip_groups(parts):
    return [[chip * 2 + core for chip in range(parts // 2)] for core in range(2)]


def chip_gather(rows, parts):
    return lax.all_gather(rows, "seq", axis=0, tiled=True, axis_index_groups=chip_groups(parts))


def chip_scatter(rows, parts):
    return lax.psum_scatter(
        rows, "seq", scatter_dimension=0, tiled=True, axis_index_groups=chip_groups(parts)
    )


def local(
    block_input,
    lengths,
    cotangent,
    attn_gain,
    w_qa,
    q_gain,
    w_qb,
    w_k,
    k_gain,
    w_v,
    w_o,
    mlp_gain,
    w_gate,
    w_up,
    w_down,
):
    tok_rows = block_input.shape[1]
    parts = lax.axis_size("seq")
    groups = lax.axis_size("dp")
    me = lax.axis_index("seq")
    heads = H // parts
    group_tokens = tok_rows * parts
    first_row = me * tok_rows
    segment, places, offsets = layout(lengths[0], group_tokens)
    cos_all, sin_all = rope_tables(offsets, E)
    cosine = lax.dynamic_slice_in_dim(cos_all, first_row, tok_rows, 0)
    sine_tab = lax.dynamic_slice_in_dim(sin_all, first_row, tok_rows, 0)
    score_scale = 1.0 / math.sqrt(E)
    flat_rows = block_input.reshape(tok_rows, D)
    out_grad = cotangent.reshape(tok_rows, D)
    rank = w_qa.shape[1]
    inner = rank + 2 * E
    width = D // parts

    own_gains = [attn_gain, q_gain, k_gain, mlp_gain]
    spans = [g.shape[0] for g in own_gains]
    gain_block = jnp.concatenate(
        [jnp.pad(g, (0, 128 - g.shape[0]))[None] for g in own_gains]
        + [jnp.zeros((4, 128), jnp.float32)],
        axis=0,
    )
    gain_block = lax.reduce_precision(gain_block, 8, 7)
    inverse_one = lax.rsqrt(jnp.mean(flat_rows * flat_rows, axis=-1, keepdims=True) + eps_norm)
    scaled_cols = jnp.transpose(
        (flat_rows * inverse_one).reshape(tok_rows, parts, width), (1, 0, 2)
    )
    w_in = jnp.concatenate([w_qa, w_k, w_v], axis=1).astype(jnp.bfloat16)
    (gains, gains_line), (scaled_cols,), (in_rows,), (qb_cols,), o_low = launch(
        "start",
        0,
        [
            gather_both(gain_block),
            swap(scaled_cols, "seq"),
            swap(w_in, "dp", repeat=True),
            swap(columns(w_qb, parts), "seq"),
        ],
        passes=[w_o.astype(jnp.bfloat16)],
    )
    gain_one = gains[:, :, 0, : spans[0]].reshape(1, -1)
    gain_latent = gains[:, :, 1, : spans[1]].reshape(1, -1)
    gain_key = gains[:, :, 2, : spans[2]].reshape(1, -1)
    gain_two = gains[:, :, 3, : spans[3]].reshape(1, -1)
    gain_mine = gains_line[:, 0, : spans[0]].reshape(1, -1)

    o_rows = lax.all_gather(o_low, "dp", axis=0, tiled=True)
    qb_cols = join(qb_cols)

    in_rows = in_rows.reshape(width, inner)
    normed = (scaled_cols.reshape(group_tokens, width) * gain_mine).astype(jnp.bfloat16)
    partial = dot(normed, in_rows).astype(jnp.bfloat16).reshape(parts, tok_rows, inner)

    def latent_rows(total, row, vec):
        latent, key, value = total[:, :rank], total[:, rank : rank + E], total[:, rank + E :]
        low = jnp.concatenate(
            [rms_scale(latent, vec[0]), rotate(rms_scale(key, vec[1]), row[0], row[1]), value],
            axis=1,
        )
        return low, [total], None

    (gathered, inner_own), (grad_all,), down_low = launch(
        "latent",
        1,
        [
            exchange(
                partial,
                [cosine, sine_tab],
                [gain_latent, gain_key],
                latent_rows,
                [inner],
                inner,
                0,
            ),
            gather(out_grad.astype(jnp.bfloat16), "dp"),
        ],
        passes=[w_down.astype(jnp.bfloat16)],
    )
    grad_all = grad_all.reshape(-1, D)
    down_rows = chip_gather(down_low, parts)
    chips = parts // 2
    both_cols = jnp.concatenate(
        [line_columns(w_gate, chips, groups), line_columns(w_up, chips, groups)], axis=2
    )
    ((both_cols,),) = launch("gate_up", 2, [swap(both_cols, "line")], needs=[gathered])
    gathered = gathered.reshape(group_tokens, inner)
    units = both_cols.shape[2] // 2
    latent_all = gathered[:, :rank]
    keys_all = gathered[:, rank : rank + E]
    values_all = gathered[:, rank + E :]

    query = dot(latent_all, qb_cols).reshape(group_tokens, heads, E)
    query = jnp.transpose(query, (1, 0, 2))
    q_rot = rotate(query, cos_all[None], sin_all[None]).astype(jnp.bfloat16)
    allowed = (segment[:, None] == segment[None, :]) & (places[None, :] <= places[:, None])
    scores = (
        jnp.einsum("htd,kd->htk", q_rot, keys_all, preferred_element_type=jnp.float32)
        * score_scale
    )
    scores = jnp.where(allowed[None], scores, big_negative)
    shifted = jnp.exp(scores - jnp.max(scores, axis=-1, keepdims=True))
    probs = shifted / jnp.sum(shifted, axis=-1, keepdims=True)
    probs_low = probs.astype(jnp.bfloat16)
    attended = jnp.einsum("htk,kd->htd", probs_low, values_all, preferred_element_type=jnp.float32)
    attended_low = jnp.transpose(attended.astype(jnp.bfloat16), (1, 0, 2)).reshape(
        group_tokens, heads * E
    )
    partial = dot(attended_low, o_rows).astype(jnp.bfloat16).reshape(parts, tok_rows, D)

    def mixed_function(total, row, vec):
        mixed = row[0] + total
        return rms_scale(mixed, vec[0]), [mixed], None

    ((two_all, mixed_rows),) = launch(
        "mixed",
        3,
        [
            exchange(
                partial,
                [flat_rows],
                [gain_two],
                mixed_function,
                [D],
                D,
                0,
                spread_axis="dp",
            )
        ],
        needs=[down_rows],
    )
    two_all = two_all.reshape(-1, D)
    wide = both_cols.shape[2]
    piece = both_cols.shape[1]
    both_cols = chip_gather(both_cols.reshape(-1, wide), parts)
    both_cols = both_cols.reshape(chips, groups, 2, piece, wide)
    both_cols = jnp.transpose(both_cols, (0, 2, 1, 3, 4)).reshape(D, wide)

    both_act = dot(two_all, both_cols)
    gate_act, up_act = both_act[:, :units], both_act[:, units:]
    sigmoid_gate = jax.nn.sigmoid(gate_act)
    hidden = (gate_act * sigmoid_gate * up_act).astype(jnp.bfloat16)
    hidden_grad = jnp.einsum("td,fd->tf", grad_all, down_rows, preferred_element_type=jnp.float32)
    gate_grad = (
        hidden_grad * up_act * (sigmoid_gate * (1.0 + gate_act * (1.0 - sigmoid_gate)))
    ).astype(jnp.bfloat16)
    up_grad = (hidden_grad * (gate_act * sigmoid_gate)).astype(jnp.bfloat16)
    down_low = jnp.einsum("tf,td->fd", hidden, grad_all, preferred_element_type=jnp.float32)
    down_low = down_low.astype(jnp.bfloat16)
    down_shard = chip_scatter(down_low, parts)
    both_grad = jnp.concatenate([gate_grad, up_grad], axis=1)
    both_low = jnp.einsum("td,tf->df", two_all, both_grad, preferred_element_type=jnp.float32)
    both_low = both_low.astype(jnp.bfloat16).reshape(chips, 2, groups, piece, wide)
    both_low = jnp.transpose(both_low, (0, 2, 1, 3, 4)).reshape(D, wide)
    both_shard = chip_scatter(both_low, parts).reshape(2 * groups, piece, wide)
    two_part = jnp.einsum(
        "tf,df->td", both_grad, both_cols, preferred_element_type=jnp.float32
    ).astype(jnp.bfloat16)

    def two_function(total, row, vec):
        value_grad, gain_grad = back_rows(row[0], vec[0], total)
        mixed_grad = row[1] + value_grad
        return mixed_grad, [mixed_grad], gain_grad

    ((mixed_all, mixed_grad, gain_two_grad),) = launch(
        "two_grad",
        4,
        [
            exchange(
                two_part.reshape(2 * groups, tok_rows, D),
                [mixed_rows, out_grad],
                [gain_two],
                two_function,
                [D],
                D,
                D,
                sum_axis="dp",
            )
        ],
        needs=[down_low, both_low],
    )
    mixed_all = tie(mixed_all, [down_shard]).reshape(group_tokens, D)
    o_shard, o_low = scatter_rows(
        jnp.einsum("tf,td->fd", attended_low, mixed_all, preferred_element_type=jnp.float32)
    )
    att_grad = jnp.einsum("td,fd->tf", mixed_all, o_rows, preferred_element_type=jnp.float32)
    att_grad = jnp.transpose(
        att_grad.astype(jnp.bfloat16).reshape(group_tokens, heads, E), (1, 0, 2)
    )
    delta_rows = jnp.sum(att_grad.astype(jnp.float32) * attended, axis=-1)
    value_grads = jnp.einsum(
        "htk,htd->kd", probs_low, att_grad, preferred_element_type=jnp.float32
    )
    prob_grad = jnp.einsum("htd,kd->htk", att_grad, values_all, preferred_element_type=jnp.float32)
    score_grad = (probs * (prob_grad - delta_rows[..., None])).astype(jnp.bfloat16)
    query_grad = (
        jnp.einsum("htk,kd->htd", score_grad, keys_all, preferred_element_type=jnp.float32)
        * score_scale
    )
    key_grads = (
        jnp.einsum("htk,htd->kd", score_grad, q_rot, preferred_element_type=jnp.float32)
        * score_scale
    )
    query_grad = rotate_back(query_grad, cos_all[None], sin_all[None]).astype(jnp.bfloat16)
    query_grad = jnp.transpose(query_grad, (1, 0, 2)).reshape(group_tokens, heads * E)
    qb_shard, qb_low = scatter_columns(
        jnp.einsum("tr,tf->rf", latent_all, query_grad, preferred_element_type=jnp.float32),
        parts,
        groups,
    )
    latent_part = jnp.einsum("tf,rf->tr", query_grad, qb_cols, preferred_element_type=jnp.float32)
    partial = jnp.concatenate([latent_part, key_grads, value_grads], axis=1).astype(jnp.bfloat16)

    def inner_function(total, row, vec):
        latent_grad, latent_gain = back_rows(row[0][:, :rank], vec[0], total[:, :rank])
        key_back = rotate_back(total[:, rank : rank + E], row[1], row[2])
        key_grad, key_gain = back_rows(row[0][:, rank : rank + E], vec[1], key_back)
        low = jnp.concatenate([latent_grad, key_grad, total[:, rank + E :]], axis=1)
        return low, [], jnp.concatenate([latent_gain, key_gain], axis=1)

    out_part = dot(hidden, down_rows).astype(jnp.bfloat16).reshape(2 * groups, tok_rows, D)

    def out_function(total, row, vec):
        return None, [row[0] + total], None

    (in_grad, inner_gain_grad), (output_rows,) = launch(
        "inner_grad",
        5,
        [
            exchange(
                partial.reshape(parts, tok_rows, inner),
                [inner_own, cosine, sine_tab],
                [gain_latent, gain_key],
                inner_function,
                [],
                inner,
                rank + E,
            ),
            exchange(out_part, [mixed_rows], [], out_function, [D], 0, 0, sum_axis="dp"),
        ],
        needs=[o_low, qb_low],
    )
    in_grad = in_grad.reshape(group_tokens, inner)
    in_low = jnp.einsum("td,tr->dr", normed, in_grad, preferred_element_type=jnp.float32)
    in_low = in_low.astype(jnp.bfloat16).reshape(groups, -1, inner)
    normed_part = jnp.einsum("tr,dr->td", in_grad, in_rows, preferred_element_type=jnp.float32)
    normed_part = normed_part.astype(jnp.bfloat16).reshape(parts, tok_rows, width)

    (normed_grad,), (in_shard,), (both_shard,) = launch(
        "normed_grad",
        6,
        [swap(normed_part, "seq"), swap(in_low, "dp"), swap(both_shard, "line")],
    )
    in_shard = jnp.sum(in_shard.astype(jnp.float32), axis=0)
    normed_grad = jnp.transpose(normed_grad.astype(jnp.float32), (1, 0, 2)).reshape(tok_rows, D)
    input_part, gain_one_grad = back_rows(flat_rows, gain_one, normed_grad)
    input_grad = mixed_grad + input_part

    gain_grads = [
        jnp.sum(gain_one_grad, axis=0),
        jnp.sum(inner_gain_grad[:, :rank], axis=0),
        jnp.sum(inner_gain_grad[:, rank:], axis=0),
        jnp.sum(gain_two_grad, axis=0),
    ]
    gain_grads = jnp.stack(
        [
            jnp.pad(g.reshape(parts, groups, n), ((0, 0), (0, 0), (0, 128 - n)))
            for g, n in zip(gain_grads, spans, strict=True)
        ]
        + [jnp.zeros((parts, groups, 128), jnp.float32)] * 4,
        axis=2,
    )
    (gain_own,), (qb_shard,) = launch("end", 7, [sum_both(gain_grads), swap(qb_shard, "seq")])
    return (
        output_rows.reshape(1, tok_rows, D),
        input_grad.reshape(1, tok_rows, D),
        gain_own[0, : spans[0]],
        in_shard[:, :rank],
        gain_own[1, : spans[1]],
        unfold(qb_shard),
        in_shard[:, rank : rank + E],
        gain_own[2, : spans[2]],
        in_shard[:, rank + E :],
        o_shard.astype(jnp.float32),
        gain_own[3, : spans[3]],
        line_unfold(both_shard[:, :, :units], chips, groups),
        line_unfold(both_shard[:, :, units:], chips, groups),
        down_shard.astype(jnp.float32),
    )


def solution(mesh):
    return jax.shard_map(
        local,
        mesh=mesh,
        in_specs=(
            P("dp", "seq", None),
            P("dp", None),
            P("dp", "seq", None),
            P(("seq", "dp")),
            P(("seq", "dp"), None),
            P(("seq", "dp")),
            P(("seq", "dp"), None),
            P(("seq", "dp"), None),
            P(("seq", "dp")),
            P(("seq", "dp"), None),
            P(("seq", "dp"), None),
            P(("seq", "dp")),
            P(("seq", "dp"), None),
            P(("seq", "dp"), None),
            P(("seq", "dp"), None),
        ),
        out_specs=(
            P("dp", "seq", None),
            P("dp", "seq", None),
            P(("seq", "dp")),
            P(("seq", "dp"), None),
            P(("seq", "dp")),
            P(("seq", "dp"), None),
            P(("seq", "dp"), None),
            P(("seq", "dp")),
            P(("seq", "dp"), None),
            P(("seq", "dp"), None),
            P(("seq", "dp")),
            P(("seq", "dp"), None),
            P(("seq", "dp"), None),
            P(("seq", "dp"), None),
        ),
        check_vma=False,
    )
```

```python
import math

import jax
import jax.numpy as jnp
from jax import lax
from jax.experimental import pallas as pl
from jax.experimental.pallas import tpu as pltpu
from jax.sharding import PartitionSpec as P

D = 2048
H = 16
E = 256


MESH = pl.DeviceIdType.MESH
STEP = 16
QUERIES = 256
VMEM_LIMIT = 60 * 1024 * 1024
COST = pl.CostEstimate(flops=0, transcendentals=0, bytes_accessed=1024)

eps_norm = 1e-06
big_negative = -1e30


def rms_scale(values, gain_vec):
    inverse = lax.rsqrt(jnp.mean(values * values, axis=-1, keepdims=True) + eps_norm)
    return values * inverse * gain_vec


def norm_back(values, gain_vec, upstream):
    inverse = lax.rsqrt(jnp.mean(values * values, axis=-1, keepdims=True) + eps_norm)
    gain_grad = jnp.sum(upstream * values * inverse, axis=0)
    scaled = upstream * gain_vec
    value_grad = inverse * scaled - values * (inverse * inverse * inverse) * jnp.mean(
        scaled * values, axis=-1, keepdims=True
    )
    return (value_grad, gain_grad)


def rotate(values, cosine, sine_tab):
    half_width = values.shape[-1] // 2
    turned = jnp.concatenate([-values[..., half_width:], values[..., :half_width]], axis=-1)
    return values * cosine + turned * sine_tab


def rotate_back(upstream, cosine, sine_tab):
    half_width = upstream.shape[-1] // 2
    weighted = upstream * sine_tab
    turned = jnp.concatenate([weighted[..., half_width:], -weighted[..., :half_width]], axis=-1)
    return upstream * cosine + turned


def layout(seq_lengths, group_tokens):
    seq_ends = jnp.cumsum(seq_lengths)
    places = jnp.arange(group_tokens, dtype=jnp.int32)
    passed = places[:, None] >= seq_ends[None, :]
    segment = jnp.sum(passed.astype(jnp.int32), axis=1)
    starts = jnp.sum(jnp.where(passed, seq_lengths[None, :], 0), axis=1)
    return (segment, places, places - starts)


def rope_tables(offsets, width):
    half_width = width // 2
    frequency = jnp.exp(
        jnp.arange(half_width, dtype=jnp.float32) * (-2.0 * math.log(10000.0) / width)
    )
    angles = offsets.astype(jnp.float32)[:, None] * frequency[None, :]
    angles = jnp.concatenate([angles, angles], axis=-1)
    return (jnp.cos(angles), jnp.sin(angles))


VMEM = pl.BlockSpec(memory_space=pltpu.VMEM)
ANY = pl.BlockSpec(memory_space=pl.ANY)
SIBLING = (1, 0)


def flip(index, bits):
    out, power = index, 1
    while power <= bits:
        if bits & power:
            out = out + power - 2 * power * ((index // power) % 2)
        power *= 2
    return out


def here():
    return lax.axis_index("seq"), lax.axis_index("dp")


def device(mask):
    me, group = here()
    return flip(me, mask[0]), flip(group, mask[1])


def copy_to(source, target, sems, seq_to, dp_to):
    return pltpu.make_async_remote_copy(
        src_ref=source,
        dst_ref=target,
        send_sem=sems.at[0],
        recv_sem=sems.at[1],
        device_id=(seq_to, dp_to),
        device_id_type=MESH,
    )


def remote(source, target, sems, mask):
    copy = copy_to(source, target, sems, *device(mask))
    copy.start()
    return copy


def keep(source, target, sem):
    copy = pltpu.make_async_copy(source, target, sem)
    copy.start()
    return copy


class Task:
    def __init__(self, inputs, outputs, scratch, masks, run):
        self.inputs, self.outputs, self.scratch = inputs, outputs, scratch
        self.masks, self.run = masks, run


def launch(name, collective_id, tasks, needs=(), passes=()):
    masks = sorted({mask for task in tasks for mask in task.masks})
    n_in = sum(len(task.inputs) for task in tasks)
    n_out = sum(len(task.outputs) for task in tasks)

    def body(*refs):
        refs = list(refs)
        ins = refs[:n_in]
        refs = refs[n_in + len(needs) + len(passes) :]
        outs, scratch = refs[:n_out], refs[n_out + len(passes) :]
        if masks:
            barrier = pltpu.get_barrier_semaphore()
            for mask in masks:
                pl.semaphore_signal(barrier, inc=1, device_id=device(mask), device_id_type=MESH)
            pl.semaphore_wait(barrier, len(masks))
        running = []
        for task in tasks:
            a, b, c = len(task.inputs), len(task.outputs), len(task.scratch)
            running.append(task.run(ins[:a], outs[:b], scratch[:c]))
            ins, outs, scratch = ins[a:], outs[b:], scratch[c:]
        while running:
            for step in list(running):
                if next(step, "done") == "done":
                    running.remove(step)

    inputs = [pair for task in tasks for pair in task.inputs]
    outputs = [pair for task in tasks for pair in task.outputs]
    results = pl.pallas_call(
        body,
        name=name,
        out_shape=[shape for shape, _ in outputs]
        + [jax.ShapeDtypeStruct(a.shape, a.dtype) for a in passes],
        in_specs=[spec for _, spec in inputs] + [ANY] * (len(needs) + len(passes)),
        out_specs=[spec for _, spec in outputs] + [ANY] * len(passes),
        input_output_aliases={n_in + len(needs) + i: n_out + i for i in range(len(passes))},
        scratch_shapes=[shape for task in tasks for shape in task.scratch],
        compiler_params=pltpu.CompilerParams(
            collective_id=collective_id if masks else None,
            has_side_effects=bool(masks),
            vmem_limit_bytes=VMEM_LIMIT,
        ),
        cost_estimate=COST,
    )(*[array for array, _ in inputs], *needs, *passes)
    results, split = list(results), []
    for task in tasks:
        split.append(results[: len(task.outputs)])
        results = results[len(task.outputs) :]
    return split + results


def chain(first, second, links):
    inputs = [pair for i, pair in enumerate(second.inputs) if i not in links]
    a, b, c = len(first.inputs), len(first.outputs), len(first.scratch)

    def run(ins, outs, scratch):
        yield from first.run(ins[:a], outs[:b], scratch[:c])
        rest = list(ins[a:])
        joined = [outs[links[i]] if i in links else rest.pop(0) for i in range(len(second.inputs))]
        yield from second.run(joined, outs[b:], scratch[c:])

    return Task(
        first.inputs + inputs,
        first.outputs + second.outputs,
        first.scratch + second.scratch,
        first.masks + second.masks,
        run,
    )


def paused(task, pauses):
    def run(ins, outs, scratch):
        for _ in range(pauses):
            yield
        yield from task.run(ins, outs, scratch)

    return Task(task.inputs, task.outputs, task.scratch, task.masks, run)


def rows_loop(start, stop, step):
    def one(i, carry):
        step(pl.ds(pl.multiple_of(i * STEP, STEP), STEP))
        return carry

    lax.fori_loop(start // STEP, stop // STEP, one, 0)


def axis_masks(axis):
    if axis == "chip":
        return [(2 * j, 0) for j in range(1, lax.axis_size("seq") // 2)]
    return [(0, j) for j in range(1, lax.axis_size("dp"))]


def axis_block(axis, mask=(0, 0)):
    seq_at, dp_at = device(mask)
    return seq_at if axis == "chip" else dp_at * 2 + seq_at % 2


def line_masks():
    masks, power = [], 2
    while power <= lax.axis_size("dp"):
        masks.append((0, power - 1))
        power *= 2
    return masks


def spread_masks(axis):
    if axis == "dp":
        return [SIBLING] + line_masks()
    return [SIBLING] + axis_masks(axis)


def spread(axis, low, all_ref, keep_sem, sems):
    own = all_ref.at[axis_block(axis)]
    rows = low.shape[0]
    sends = []
    if axis == "dp":
        yield from spread_line(low, all_ref, keep_sem, sems)
        return
    masks = axis_masks(axis)
    square = len(masks) == 3
    direct = [(2, 0), (4, 0)] if square else masks
    for i, mask in enumerate(direct):
        sends.append(remote(low, own, sems.at[i], mask))
    beside = [remote(low, own, sems.at[len(masks)], SIBLING)]
    kept = keep(low, own, keep_sem)
    yield
    at, halves = len(masks) + 1, []

    def block(mask):
        return all_ref.at[axis_block(axis, mask)]

    def half(mask, which):
        return all_ref.at[axis_block(axis, mask), pl.ds(which * (rows // 2), rows // 2)]

    for i, mask in enumerate(direct):
        sends[i].wait_recv()
        if square:
            halves.append(remote(half(mask, i), half(mask, i), sems.at[at], direct[1 - i]))
            at += 1
        beside.append(remote(block(mask), block(mask), sems.at[at], SIBLING))
        at += 1
        yield
    for i, copy in enumerate(halves):
        copy.wait_recv()
        part = half((6, 0), i)
        beside.append(remote(part, part, sems.at[at], SIBLING))
        at += 1
        yield
    for copy in beside:
        copy.wait_recv()
    for copy in sends + halves + beside:
        copy.wait_send()
    kept.wait()


def spread_line(low, all_ref, keep_sem, sems):
    me, group = here()
    core, groups = me % 2, lax.axis_size("dp")
    own = all_ref.at[axis_block("dp")]
    kept = keep(low, own, keep_sem)
    beside = remote(low, own, sems.at[0], SIBLING)

    def at(way, k, kind):
        return sems.at[1 + (way * (groups - 1) + k) * 2 + kind]

    def hop(way, k):
        step = 1 - 2 * way
        block = all_ref.at[(group - step * k) * 2 + core]
        return copy_to(low if k == 0 else block, block, at(way, k, 0), me, group + step)

    def landed(way, k):
        block = all_ref.at[(group - (1 - 2 * way) * (k + 1)) * 2 + core]
        return copy_to(block, block, at(way, k, 0), *device(SIBLING))

    def aside(way, k):
        block = all_ref.at[(group - (1 - 2 * way) * (k + 1)) * 2 + core]
        return copy_to(block, block, at(way, k, 1), *device(SIBLING))

    def sends(way, k):
        if way == 0:
            return (group >= k) & (group < groups - 1)
        return (group + k < groups) & (group > 0)

    def lands(way, k):
        return (group >= k + 1) if way == 0 else (group + k + 1 < groups)

    for k in range(groups - 1):
        for way in range(2):

            @pl.when(sends(way, k))
            def _(way=way, k=k):
                hop(way, k).start()

        yield
        for way in range(2):

            @pl.when(lands(way, k))
            def _(way=way, k=k):
                landed(way, k).wait_recv()
                aside(way, k).start()

    yield
    beside.wait_recv()
    for k in range(groups - 1):
        for way in range(2):

            @pl.when(lands(way, k))
            def _(way=way, k=k):
                aside(way, k).wait()

            @pl.when(sends(way, k))
            def _(way=way, k=k):
                hop(way, k).wait_send()

    beside.wait_send()
    kept.wait()


def exchange(
    partial,
    row_operands,
    vec_operands,
    row_function,
    own_widths,
    low_width,
    vec_width,
    sum_axis="chip",
    spread_axis="chip",
    all_space=ANY,
):
    blocks, rows, cols = partial.shape
    far = blocks // 2
    n_rows = len(row_operands)
    masks = axis_masks(sum_axis)
    square = sum_axis == "chip" and len(masks) == 3
    out_blocks = lax.axis_size("seq") if spread_axis == "chip" else 2 * lax.axis_size("dp")
    order = list(range(far - 1, 0, -1)) + [0]
    at_mask = [(0, 0)] + masks

    def run(ins, outs, scratch):
        ins, outs = list(ins), list(outs)
        partial_ref = ins.pop(0)
        row_refs, vec_refs = ins[:n_rows], ins[n_rows:]
        all_ref = outs.pop(0) if low_width else None
        vec_out = outs.pop(-1) if vec_width else None
        mine, beside, arrived, low, local_sem, sems, out_sems = scratch

        across, loads = {}, {}
        for j in order:
            block = axis_block(sum_axis, at_mask[j])
            other = axis_block(sum_axis, (at_mask[j][0] + 1, at_mask[j][1]))
            across[j] = remote(partial_ref.at[other], beside.at[j], sems.at[j], SIBLING)
            loads[j] = keep(partial_ref.at[block], mine.at[j], local_sem.at[j])
        yield
        sent = []

        def settle(j, low_row=0, high_row=rows, more=None):
            def add(at):
                total = mine[j, at, :].astype(jnp.float32) + beside[j, at, :].astype(jnp.float32)
                if more is not None:
                    total = total + arrived[more, at, :].astype(jnp.float32)
                mine[j, at, :] = total.astype(jnp.bfloat16)

            rows_loop(low_row, high_row, add)

        if square:
            middle = rows // 2
            first, second = pl.ds(0, middle), pl.ds(middle, middle)
            for j in (3, 1, 2):
                loads[j].wait()
                across[j].wait_recv()
                if j == 3:
                    settle(3)
                elif j == 1:
                    settle(1, 0, middle)
                else:
                    settle(2, middle, rows)
                base = far + 2 * (j - 1)
                if j in (3, 1):
                    sent.append(
                        remote(mine.at[j, first], arrived.at[j, first], sems.at[base], (2, 0))
                    )
                if j in (3, 2):
                    sent.append(
                        remote(mine.at[j, second], arrived.at[j, second], sems.at[base + 1], (4, 0))
                    )
            yield
            diagonal_x, diagonal_y = sent[0], sent[1]
            diagonal_x.wait_recv()
            settle(2, 0, middle, more=3)
            sent.append(
                remote(mine.at[2, first], arrived.at[2, first], sems.at[far + 2], (4, 0))
            )
            diagonal_y.wait_recv()
            settle(1, middle, rows, more=3)
            sent.append(
                remote(mine.at[1, second], arrived.at[1, second], sems.at[far + 1], (2, 0))
            )
            yield
            adds = [1, 2]
            landed = sent[2:]
        else:
            for j in order[:-1]:
                loads[j].wait()
                across[j].wait_recv()
                settle(j)
                sent.append(remote(mine.at[j], arrived.at[j], sems.at[far + j], at_mask[j]))
            yield
            adds = order[:-1]
            landed = sent
        loads[0].wait()
        across[0].wait_recv()
        for copy in landed:
            copy.wait_recv()
        if vec_width:
            vec_out[...] = jnp.zeros_like(vec_out)
        vecs = [v[...] for v in vec_refs]

        def finish(at):
            total = mine[0, at, :].astype(jnp.float32) + beside[0, at, :].astype(jnp.float32)
            for j in adds:
                total = total + arrived[j, at, :].astype(jnp.float32)
            low_now, own_now, vec_now = row_function(total, [r[at, :] for r in row_refs], vecs)
            if low_width:
                low[at, :] = low_now.astype(jnp.bfloat16)
            for ref, value in zip(outs, own_now, strict=True):
                ref[at, :] = value
            if vec_width:
                vec_out[...] += vec_now

        rows_loop(0, rows, finish)
        if low_width:
            yield from spread(spread_axis, low, all_ref, local_sem.at[0], out_sems)
        for copy in list(across.values()) + sent:
            copy.wait_send()

    outputs = []
    if low_width:
        shape = jax.ShapeDtypeStruct((out_blocks, rows, low_width), jnp.bfloat16)
        outputs.append((shape, all_space))
    outputs += [(jax.ShapeDtypeStruct((rows, width), jnp.float32), VMEM) for width in own_widths]
    if vec_width:
        outputs.append((jax.ShapeDtypeStruct((STEP, vec_width), jnp.float32), VMEM))
    return Task(
        [(partial, ANY)] + [(a, VMEM) for a in list(row_operands) + list(vec_operands)],
        outputs,
        [
            pltpu.VMEM((far, rows, cols), jnp.bfloat16),
            pltpu.VMEM((far, rows, cols), jnp.bfloat16),
            pltpu.VMEM((far, rows, cols), jnp.bfloat16),
            pltpu.VMEM((rows, max(low_width, 128)), jnp.bfloat16),
            pltpu.SemaphoreType.DMA((far,)),
            pltpu.SemaphoreType.DMA((far + max(6, far), 2)),
            pltpu.SemaphoreType.DMA((spread_sems(spread_axis), 2)),
        ],
        [SIBLING] + masks + (spread_masks(spread_axis) if low_width else []),
        run,
    )


def spread_sems(axis):
    if axis == "dp":
        return 1 + 4 * (lax.axis_size("dp") - 1)
    return 2 * lax.axis_size("seq")


def gather(low, axis, all_space=ANY):
    rows, cols = low.shape
    blocks = lax.axis_size("seq") if axis == "chip" else 2 * lax.axis_size("dp")

    def run(ins, outs, scratch):
        yield from spread(axis, ins[0], outs[0], scratch[0].at[0], scratch[1])

    return Task(
        [(low, ANY)],
        [(jax.ShapeDtypeStruct((blocks, rows, cols), low.dtype), all_space)],
        [pltpu.SemaphoreType.DMA((1,)), pltpu.SemaphoreType.DMA((spread_sems(axis), 2))],
        spread_masks(axis),
        run,
    )


def family(kind):
    parts, groups = lax.axis_size("seq"), lax.axis_size("dp")
    if kind == "seq":
        return [(m, 0) for m in range(1, parts)], lambda s, d: s
    if kind == "dp":
        return [(0, m) for m in range(1, groups)], lambda s, d: d
    return [(m % 2, m // 2) for m in range(1, 2 * groups)], lambda s, d: d * 2 + s % 2


def swap(array, kind, repeat=False):
    masks, index = family(kind)

    def run(ins, outs, scratch):
        own = index(*here())
        copies = [keep(ins[0] if repeat else ins[0].at[own], outs[0].at[own], scratch[0].at[0])]
        for i, mask in enumerate(masks):
            source = ins[0] if repeat else ins[0].at[index(*device(mask))]
            copies.append(remote(source, outs[0].at[own], scratch[1].at[i], mask))
        yield
        for copy in copies:
            copy.wait()

    shape = (len(masks) + 1,) + array.shape if repeat else array.shape
    return Task(
        [(array, ANY)],
        [(jax.ShapeDtypeStruct(shape, array.dtype), ANY)],
        [pltpu.SemaphoreType.DMA((1,)), pltpu.SemaphoreType.DMA((len(masks), 2))],
        masks,
        run,
    )


def gather_both(array):
    seq_masks, dp_masks = family("seq")[0], family("dp")[0]
    parts, groups = lax.axis_size("seq"), lax.axis_size("dp")

    def run(ins, outs, scratch):
        me, group = here()
        (small,), (everything, line) = ins, outs
        copies = [keep(small, line.at[group], scratch[0].at[0])]
        for i, mask in enumerate(dp_masks):
            copies.append(remote(small, line.at[group], scratch[1].at[i], mask))
        yield
        for copy in copies:
            copy.wait()
        copies = [keep(line, everything.at[me], scratch[0].at[1])]
        for i, mask in enumerate(seq_masks):
            at = scratch[1].at[len(dp_masks) + i]
            copies.append(remote(line, everything.at[me], at, mask))
        yield
        for copy in copies:
            copy.wait()

    return Task(
        [(array, VMEM)],
        [
            (jax.ShapeDtypeStruct((parts, groups) + array.shape, array.dtype), VMEM),
            (jax.ShapeDtypeStruct((groups,) + array.shape, array.dtype), VMEM),
        ],
        [
            pltpu.SemaphoreType.DMA((2,)),
            pltpu.SemaphoreType.DMA((len(seq_masks) + len(dp_masks), 2)),
        ],
        seq_masks + dp_masks,
        run,
    )


def sum_both(array):
    seq_masks, dp_masks = family("seq")[0], family("dp")[0]

    def run(ins, outs, scratch):
        me, group = here()
        stage_one, line, stage_two, local_sem, sems = scratch
        copies = [keep(ins[0].at[me], stage_one.at[me], local_sem.at[0])]
        for i, mask in enumerate(seq_masks):
            source = ins[0].at[flip(me, mask[0])]
            copies.append(remote(source, stage_one.at[me], sems.at[i], mask))
        yield
        for copy in copies:
            copy.wait()
        line[...] = jnp.sum(stage_one[...], axis=0)
        copies = [keep(line.at[group], stage_two.at[group], local_sem.at[1])]
        for i, mask in enumerate(dp_masks):
            at = sems.at[len(seq_masks) + i]
            copies.append(remote(line.at[flip(group, mask[1])], stage_two.at[group], at, mask))
        yield
        for copy in copies:
            copy.wait()
        outs[0][...] = jnp.sum(stage_two[...], axis=0)

    return Task(
        [(array, VMEM)],
        [(jax.ShapeDtypeStruct(array.shape[2:], array.dtype), VMEM)],
        [
            pltpu.VMEM(array.shape, array.dtype),
            pltpu.VMEM(array.shape[1:], array.dtype),
            pltpu.VMEM(array.shape[1:], array.dtype),
            pltpu.SemaphoreType.DMA((2,)),
            pltpu.SemaphoreType.DMA((len(seq_masks) + len(dp_masks), 2)),
        ],
        seq_masks + dp_masks,
        run,
    )


def tie(value, needs):
    def body(*refs):
        pass

    return pl.pallas_call(
        body,
        name="tie",
        out_shape=jax.ShapeDtypeStruct(value.shape, value.dtype),
        in_specs=[ANY] * (1 + len(needs)),
        out_specs=ANY,
        input_output_aliases={0: 0},
        cost_estimate=COST,
    )(value, *needs)


def gather_chips(low):
    rows, cols = low.shape
    masks = axis_masks("chip")
    square = len(masks) == 3

    def run(ins, outs, scratch):
        me, _ = here()
        low_ref, all_ref, (local_sem, sems) = ins[0], outs[0], scratch

        def block(mask):
            return all_ref.at[device(mask)[0] // 2]

        def half(mask, which):
            middle = rows // 2 // STEP * STEP
            part = pl.ds(middle, rows - middle) if which else pl.ds(0, middle)
            return all_ref.at[device(mask)[0] // 2, part]

        kept = keep(low_ref, block((0, 0)), local_sem.at[0])
        direct = [(2, 0), (4, 0)] if square else masks
        copies = [
            remote(low_ref, block((0, 0)), sems.at[i], mask) for i, mask in enumerate(direct)
        ]
        yield
        if square:
            for i, mask in enumerate(direct):
                copies[i].wait_recv()
                part = half(mask, i)
                copies.append(remote(part, part, sems.at[2 + i], direct[1 - i]))
            yield
            copies[0].wait_send()
            copies[1].wait_send()
            copies = copies[2:]
        for copy in copies:
            copy.wait()
        kept.wait()

    return Task(
        [(low, ANY)],
        [(jax.ShapeDtypeStruct((len(masks) + 1, rows, cols), low.dtype), ANY)],
        [pltpu.SemaphoreType.DMA((1,)), pltpu.SemaphoreType.DMA((max(4, len(masks)), 2))],
        masks,
        run,
    )


def lanes_of(sources, segments, tile, rows):
    lane = lax.broadcasted_iota(jnp.int32, (rows, 128), 1)
    out = jnp.zeros((rows, 128), jnp.float32)
    low = tile * 128
    for source, from_col, to_col, length in segments:
        first, last = max(low, to_col), min(low + 128, to_col + length)
        if first >= last:
            continue
        begin = from_col + first - to_col
        window = begin // 128 * 128
        wide = 128 if begin - window + last - first <= 128 else 256
        held = min(wide, sources[source].shape[1] - window)
        wide = pl.cdiv(held, 128) * 128
        piece = sources[source][:, window : window + held].astype(jnp.float32)
        if held < wide:
            blank = jnp.zeros((rows, wide - held), jnp.float32)
            piece = jnp.concatenate([piece, blank], axis=1)
        shift = (first - low - (begin - window)) % wide
        if shift:
            piece = pltpu.roll(piece, shift, axis=1)
        out = jnp.where((lane >= first - low) & (lane < last - low), piece[:, :128], out)
    return out


def fold(weights, chips, groups):
    rows, cols = weights[0].shape
    units = cols // (2 * chips * groups)
    width = 2 * chips * units

    def body(first_ref, second_ref, out_ref):
        sources = [first_ref, second_ref]
        for group in range(groups):
            for core in range(2):
                segments = [
                    (
                        which,
                        ((chip * 2 + core) * groups + group) * units,
                        (which * chips + chip) * units,
                        units,
                    )
                    for which in range(2)
                    for chip in range(chips)
                ]
                for tile in range(pl.cdiv(width, 128)):
                    value = lanes_of(sources, segments, tile, rows).astype(jnp.bfloat16)
                    stop = min(width, tile * 128 + 128)
                    out_ref[group * 2 + core, :, tile * 128 : stop] = value[:, : stop - tile * 128]

    return pl.pallas_call(
        body,
        name="fold",
        out_shape=jax.ShapeDtypeStruct((2 * groups, rows, width), jnp.bfloat16),
        in_specs=[VMEM, VMEM],
        out_specs=VMEM,
        compiler_params=pltpu.CompilerParams(vmem_limit_bytes=VMEM_LIMIT),
        cost_estimate=COST,
    )(*weights)


def unfold_pair(pieces, chips, groups):
    _, rows, width = pieces.shape
    units = width // (2 * chips)
    cols = units * 2 * chips * groups

    def body(in_ref, first_ref, second_ref):
        sources = [in_ref.at[i] for i in range(2 * groups)]
        for which, out_ref in enumerate([first_ref, second_ref]):
            segments = [
                (
                    group * 2 + core,
                    (which * chips + chip) * units,
                    ((chip * 2 + core) * groups + group) * units,
                    units,
                )
                for chip in range(chips)
                for core in range(2)
                for group in range(groups)
            ]
            for tile in range(cols // 128):
                out_ref[:, tile * 128 : tile * 128 + 128] = lanes_of(sources, segments, tile, rows)

    shape = jax.ShapeDtypeStruct((rows, cols), jnp.float32)
    return pl.pallas_call(
        body,
        name="unfold",
        out_shape=[shape, shape],
        in_specs=[VMEM],
        out_specs=[VMEM, VMEM],
        compiler_params=pltpu.CompilerParams(vmem_limit_bytes=VMEM_LIMIT),
        cost_estimate=COST,
    )(pieces)


def nt(left, right):
    return lax.dot_general(
        left, right, (((1,), (1,)), ((), ())), preferred_element_type=jnp.float32
    )


def tn(left, right):
    return lax.dot_general(
        left, right, (((0,), (0,)), ((), ())), preferred_element_type=jnp.float32
    )


def window_of(i, tokens):
    wide = tokens // 2 + QUERIES
    start = jnp.clip(i * QUERIES - tokens // 2, 0, tokens - wide)
    return pl.multiple_of(start, QUERIES), wide


def probabilities(queries, keys, i, start, seg_col, seg_row):
    scores = nt(queries, keys) * (1.0 / math.sqrt(E))
    row = i * QUERIES + lax.broadcasted_iota(jnp.int32, scores.shape, 0)
    col = start + lax.broadcasted_iota(jnp.int32, scores.shape, 1)
    scores = jnp.where((seg_col == seg_row) & (col <= row), scores, big_negative)
    shifted = jnp.exp(scores - jnp.max(scores, axis=-1, keepdims=True))
    return shifted / jnp.sum(shifted, axis=-1, keepdims=True)


def attend(gathered, qb_cols, cosine, sine_tab, seg_col, seg_rows):
    tokens, inner = gathered.shape
    rank, width = qb_cols.shape

    def run(ins, outs, scratch):
        in_ref, qb_ref, cos_ref, sin_ref, seg_ref, segs_ref = ins
        q_ref, out_ref = outs

        def block(i, carry):
            at = pl.ds(pl.multiple_of(i * QUERIES, QUERIES), QUERIES)
            start, wide = window_of(i, tokens)
            span = pl.ds(start, wide)
            query = dot(in_ref[at, :rank], qb_ref[...])
            keys, values = in_ref[span, rank : rank + E], in_ref[span, rank + E :]
            for head in range(width // E):
                lanes = slice(head * E, head * E + E)
                rotated = rotate(query[:, lanes], cos_ref[at, :], sin_ref[at, :])
                rotated = rotated.astype(jnp.bfloat16)
                q_ref[at, lanes] = rotated
                probs = probabilities(rotated, keys, i, start, seg_ref[at, :], segs_ref[i])
                out_ref[at, lanes] = dot(probs.astype(jnp.bfloat16), values).astype(jnp.bfloat16)
            return carry

        lax.fori_loop(0, tokens // QUERIES, block, 0)
        yield

    shape = jax.ShapeDtypeStruct((tokens, width), jnp.bfloat16)
    return Task(
        [(a, VMEM) for a in (gathered, qb_cols, cosine, sine_tab, seg_col, seg_rows)],
        [(shape, VMEM), (shape, VMEM)],
        [],
        [],
        run,
    )


def attend_back(
    gathered, queries, out_grad, o_rows, qb_cols, cosine, sine_tab, seg_col, seg_rows
):
    tokens, inner = gathered.shape
    rank, width = qb_cols.shape
    scale = 1.0 / math.sqrt(E)

    def run(ins, outs, scratch):
        in_ref, q_ref, grad_ref, o_ref, qb_ref, cos_ref, sin_ref, seg_ref, segs_ref = ins
        dq_ref, part_ref = outs
        key_sum, value_sum = scratch
        key_sum[...] = jnp.zeros_like(key_sum)
        value_sum[...] = jnp.zeros_like(value_sum)

        def block(i, carry):
            at = pl.ds(pl.multiple_of(i * QUERIES, QUERIES), QUERIES)
            start, wide = window_of(i, tokens)
            span = pl.ds(start, wide)
            per = QUERIES // grad_ref.shape[1]
            upstream = grad_ref[pl.ds(i * per, per)].reshape(QUERIES, grad_ref.shape[2])
            attended_grad = nt(upstream, o_ref[...]).astype(jnp.bfloat16)
            keys, values = in_ref[span, rank : rank + E], in_ref[span, rank + E :]
            for head in range(width // E):
                lanes = slice(head * E, head * E + E)
                query, upstream = q_ref[at, lanes], attended_grad[:, lanes]
                probs = probabilities(query, keys, i, start, seg_ref[at, :], segs_ref[i])
                value_sum[span, :] += tn(probs.astype(jnp.bfloat16), upstream)
                prob_grad = nt(upstream, values)
                delta = jnp.sum(probs * prob_grad, axis=-1, keepdims=True)
                score_grad = (probs * (prob_grad - delta)).astype(jnp.bfloat16)
                key_sum[span, :] += tn(score_grad, query)
                query_grad = dot(score_grad, keys) * scale
                query_grad = rotate_back(query_grad, cos_ref[at, :], sin_ref[at, :])
                dq_ref[at, lanes] = query_grad.astype(jnp.bfloat16)
            part_ref[at, :rank] = nt(dq_ref[at, :], qb_ref[...]).astype(jnp.bfloat16)
            return carry

        lax.fori_loop(0, tokens // QUERIES, block, 0)
        part_ref[:, rank : rank + E] = (key_sum[...] * scale).astype(jnp.bfloat16)
        part_ref[:, rank + E :] = value_sum[...].astype(jnp.bfloat16)
        yield

    return Task(
        [
            (a, VMEM)
            for a in (
                gathered,
                queries,
                out_grad,
                o_rows,
                qb_cols,
                cosine,
                sine_tab,
                seg_col,
                seg_rows,
            )
        ],
        [
            (jax.ShapeDtypeStruct((tokens, width), jnp.bfloat16), VMEM),
            (jax.ShapeDtypeStruct((tokens, inner), jnp.bfloat16), VMEM),
        ],
        [pltpu.VMEM((tokens, E), jnp.float32), pltpu.VMEM((tokens, E), jnp.float32)],
        [],
        run,
    )


def feed_forward(two_all, grad_all, both_cols, down_rows, mixed_rows, out_grad, gain_two):
    line, rows, cols = two_all.shape
    units = down_rows.shape[0]
    far = line // 2
    chips, groups = lax.axis_size("seq") // 2, lax.axis_size("dp")
    masks = axis_masks("dp")
    at_mask = [(0, 0)] + masks
    order = list(range(far - 1, 0, -1)) + [0]
    slab = cols // (2 * chips)
    piece = slab // groups

    def run(ins, outs, scratch):
        two_ref, grad_ref, both_ref, down_ref, mixed_ref, dy_ref, gain_ref = ins
        mixed_out, low_out, vec_out, y_out, down_out, both_out = outs
        mine, give, beside, arrived, hidden, pair_grad, stage, sems, stage_sem = scratch
        core = here()[0] % 2

        def produce(j):
            block = device(at_mask[j])[1] * 2
            both = pl.ds(block, 2)
            x = two_ref[both].reshape(2 * rows, cols)
            dy = grad_ref[both].reshape(2 * rows, cols)
            act = dot(x, both_ref[...])
            gate, up = act[:, :units], act[:, units:]
            sigmoid = jax.nn.sigmoid(gate)
            silu = gate * sigmoid
            hid = (silu * up).astype(jnp.bfloat16)
            hidden[both] = hid.reshape(2, rows, units)
            y_out[both] = dot(hid, down_ref[...]).astype(jnp.bfloat16).reshape(2, rows, cols)
            hid_grad = nt(dy, down_ref[...])
            gate_grad = hid_grad * up * (sigmoid * (1.0 + gate * (1.0 - sigmoid)))
            up_grad = hid_grad * silu
            pair = jnp.concatenate([gate_grad, up_grad], axis=1).astype(jnp.bfloat16)
            pair_grad[both] = pair.reshape(2, rows, 2 * units)
            part = nt(pair, both_ref[...]).astype(jnp.bfloat16)

            @pl.when(core == 0)
            def _():
                mine[j], give[j] = part[:rows], part[rows:]

            @pl.when(core == 1)
            def _():
                mine[j], give[j] = part[rows:], part[:rows]

        across, sent = {}, {}

        def settle(j):
            across[j].wait_recv()

            def add(at):
                total = mine[j, at, :].astype(jnp.float32) + beside[j, at, :].astype(jnp.float32)
                mine[j, at, :] = total.astype(jnp.bfloat16)

            rows_loop(0, rows, add)
            sent[j] = remote(mine.at[j], arrived.at[j], sems.at[far + j], at_mask[j])

        last = None
        for j in order:
            produce(j)
            across[j] = remote(give.at[j], beside.at[j], sems.at[j], SIBLING)
            if last is not None:
                settle(last)
            last = j
        yield

        down_out[...] = tn(
            hidden[...].reshape(line * rows, units), grad_ref[...].reshape(line * rows, cols)
        ).astype(jnp.bfloat16)
        moves = []
        for index in range(2 * chips):
            slot = index % 2
            if index >= 2:
                for move in moves[(index - 2) * groups : (index - 1) * groups]:
                    move.wait()
            x = two_ref[:, :, index * slab : (index + 1) * slab].reshape(line * rows, slab)
            value = tn(x, pair_grad[...].reshape(line * rows, 2 * units))
            stage[slot] = value.astype(jnp.bfloat16).reshape(groups, piece, 2 * units)
            for group in range(groups):
                place = ((index // 2) * groups + group) * 2 + index % 2
                moves.append(
                    keep(stage.at[slot, group], both_out.at[place], stage_sem.at[slot, group])
                )
        for move in moves[-2 * groups :]:
            move.wait()

        across[0].wait_recv()
        for j in order[:-1]:
            sent[j].wait_recv()
        vec_out[...] = jnp.zeros_like(vec_out)
        gain = gain_ref[...]

        def finish(at):
            total = mine[0, at, :].astype(jnp.float32) + beside[0, at, :].astype(jnp.float32)
            for j in order[:-1]:
                total = total + arrived[j, at, :].astype(jnp.float32)
            value_grad, gain_grad = back_rows(mixed_ref[at, :], gain, total)
            mixed_grad = dy_ref[at, :] + value_grad
            mixed_out[at, :] = mixed_grad
            low_out[at, :] = mixed_grad.astype(jnp.bfloat16)
            vec_out[...] += gain_grad

        rows_loop(0, rows, finish)
        for copy in list(across.values()) + list(sent.values()):
            copy.wait_send()

    def low(*shape):
        return jax.ShapeDtypeStruct(shape, jnp.bfloat16)

    blocks = pltpu.VMEM((far, rows, cols), jnp.bfloat16)
    return Task(
        [
            (a, VMEM)
            for a in (two_all, grad_all, both_cols, down_rows, mixed_rows, out_grad, gain_two)
        ],
        [
            (jax.ShapeDtypeStruct((rows, cols), jnp.float32), VMEM),
            (low(rows, cols), VMEM),
            (jax.ShapeDtypeStruct((STEP, cols), jnp.float32), VMEM),
            (low(line, rows, cols), VMEM),
            (low(units, cols), VMEM),
            (low(2 * chips * groups, piece, 2 * units), ANY),
        ],
        [
            blocks,
            blocks,
            blocks,
            blocks,
            pltpu.VMEM((line, rows, units), jnp.bfloat16),
            pltpu.VMEM((line, rows, 2 * units), jnp.bfloat16),
            pltpu.VMEM((2, groups, piece, 2 * units), jnp.bfloat16),
            pltpu.SemaphoreType.DMA((2 * far, 2)),
            pltpu.SemaphoreType.DMA((2, groups)),
        ],
        [SIBLING] + masks,
        run,
    )


def chip_sum(partial):
    chips, rows, cols = partial.shape
    masks = axis_masks("chip")
    square = chips == 4
    middle = rows // 2 // STEP * STEP

    def run(ins, outs, scratch):
        (in_ref,), (out_ref,) = ins, outs
        arrived, held, local_sem, sems = scratch

        def block(j):
            return device(([(0, 0)] + masks)[j])[0] // 2

        def add(target, start, stop, *terms):
            def one(at):
                total = terms[0][at, :].astype(jnp.float32)
                for term in terms[1:]:
                    total = total + term[at, :].astype(jnp.float32)
                target[at, :] = total.astype(jnp.bfloat16)

            rows_loop(start, stop, one)

        own = keep(in_ref.at[block(0)], held.at[0], local_sem.at[0])
        if not square:
            copies = [
                remote(in_ref.at[block(j)], arrived.at[j - 1], sems.at[j - 1], masks[j - 1])
                for j in range(1, chips)
            ]
            yield
            own.wait()
            for copy in copies:
                copy.wait_recv()
            add(out_ref, 0, rows, held.at[0], *[arrived.at[j] for j in range(chips - 1)])
            for copy in copies:
                copy.wait_send()
            return
        first, second = pl.ds(0, middle), pl.ds(middle, rows - middle)
        over_x, over_y = (2, 0), (4, 0)
        copies = [
            remote(in_ref.at[block(3), first], arrived.at[2, first], sems.at[0], over_x),
            remote(in_ref.at[block(3), second], arrived.at[2, second], sems.at[1], over_y),
            remote(in_ref.at[block(1), first], arrived.at[0, first], sems.at[2], over_x),
            remote(in_ref.at[block(2), second], arrived.at[1, second], sems.at[3], over_y),
        ]
        loads = [
            keep(in_ref.at[block(2), first], held.at[1, first], local_sem.at[1]),
            keep(in_ref.at[block(1), second], held.at[1, second], local_sem.at[2]),
        ]
        yield
        loads[0].wait()
        copies[0].wait_recv()
        add(held.at[1], 0, middle, held.at[1], arrived.at[2])
        copies.append(remote(held.at[1, first], arrived.at[1, first], sems.at[4], over_y))
        loads[1].wait()
        copies[1].wait_recv()
        add(held.at[1], middle, rows, held.at[1], arrived.at[2])
        copies.append(remote(held.at[1, second], arrived.at[0, second], sems.at[5], over_x))
        yield
        own.wait()
        for copy in copies[2:]:
            copy.wait_recv()
        add(out_ref, 0, rows, held.at[0], arrived.at[0], arrived.at[1])
        for copy in copies:
            copy.wait_send()

    return Task(
        [(partial, ANY)],
        [(jax.ShapeDtypeStruct((rows, cols), jnp.bfloat16), VMEM)],
        [
            pltpu.VMEM((chips - 1, rows, cols), jnp.bfloat16),
            pltpu.VMEM((2, rows, cols), jnp.bfloat16),
            pltpu.SemaphoreType.DMA((3,)),
            pltpu.SemaphoreType.DMA((max(6, chips), 2)),
        ],
        masks,
        run,
    )


def dot(left, right):
    return jnp.dot(left, right, preferred_element_type=jnp.float32)


def back_rows(values, gain, upstream):
    inverse = lax.rsqrt(jnp.mean(values * values, axis=-1, keepdims=True) + eps_norm)
    scaled = upstream * gain
    value_grad = inverse * scaled - values * (inverse * inverse * inverse) * jnp.mean(
        scaled * values, axis=-1, keepdims=True
    )
    return value_grad, upstream * values * inverse


def columns(weight, parts):
    rows, cols = weight.shape
    low = weight.astype(jnp.bfloat16).reshape(rows, parts, cols // parts)
    return jnp.transpose(low, (1, 0, 2))


def join(pieces):
    parts, rows, cols = pieces.shape
    full = lax.all_gather(pieces.reshape(parts * rows, cols), "dp", axis=0, tiled=True)
    full = full.reshape(-1, parts, rows, cols)
    return jnp.transpose(full, (1, 0, 2, 3)).reshape(-1, cols)


def scatter_columns(grad, parts, groups):
    rows, cols = grad.shape
    piece = rows // (parts * groups)
    low = grad.astype(jnp.bfloat16).reshape(parts, groups, piece, cols)
    low = jnp.transpose(low, (1, 0, 2, 3)).reshape(rows, cols)
    own = lax.psum_scatter(low, "dp", scatter_dimension=0, tiled=True)
    return own.reshape(parts, piece, cols), low


def scatter_rows(grad):
    low = grad.astype(jnp.bfloat16)
    return lax.psum_scatter(low, "dp", scatter_dimension=0, tiled=True), low


def unfold(pieces):
    parts, rows, cols = pieces.shape
    return jnp.transpose(pieces, (1, 0, 2)).reshape(rows, parts * cols).astype(jnp.float32)


def chip_groups(parts):
    return [[chip * 2 + core for chip in range(parts // 2)] for core in range(2)]


def chip_gather(rows, parts):
    return lax.all_gather(rows, "seq", axis=0, tiled=True, axis_index_groups=chip_groups(parts))


def chip_scatter(rows, parts):
    return lax.psum_scatter(
        rows, "seq", scatter_dimension=0, tiled=True, axis_index_groups=chip_groups(parts)
    )


def local(
    block_input,
    lengths,
    cotangent,
    attn_gain,
    w_qa,
    q_gain,
    w_qb,
    w_k,
    k_gain,
    w_v,
    w_o,
    mlp_gain,
    w_gate,
    w_up,
    w_down,
):
    tok_rows = block_input.shape[1]
    parts = lax.axis_size("seq")
    groups = lax.axis_size("dp")
    me = lax.axis_index("seq")
    heads = H // parts
    group_tokens = tok_rows * parts
    first_row = me * tok_rows
    segment, places, offsets = layout(lengths[0], group_tokens)
    cos_all, sin_all = rope_tables(offsets, E)
    cosine = lax.dynamic_slice_in_dim(cos_all, first_row, tok_rows, 0)
    sine_tab = lax.dynamic_slice_in_dim(sin_all, first_row, tok_rows, 0)
    score_scale = 1.0 / math.sqrt(E)
    flat_rows = block_input.reshape(tok_rows, D)
    out_grad = cotangent.reshape(tok_rows, D)
    rank = w_qa.shape[1]
    inner = rank + 2 * E
    width = D // parts

    own_gains = [attn_gain, q_gain, k_gain, mlp_gain]
    spans = [g.shape[0] for g in own_gains]
    gain_block = jnp.concatenate(
        [jnp.pad(g, (0, 128 - g.shape[0]))[None] for g in own_gains]
        + [jnp.zeros((4, 128), jnp.float32)],
        axis=0,
    )
    gain_block = lax.reduce_precision(gain_block, 8, 7)
    inverse_one = lax.rsqrt(jnp.mean(flat_rows * flat_rows, axis=-1, keepdims=True) + eps_norm)
    scaled_cols = jnp.transpose(
        (flat_rows * inverse_one).reshape(tok_rows, parts, width), (1, 0, 2)
    )
    w_in = jnp.concatenate([w_qa, w_k, w_v], axis=1).astype(jnp.bfloat16)
    (gains, gains_line), (scaled_cols,), (in_rows,), (qb_cols,), o_low = launch(
        "start",
        0,
        [
            gather_both(gain_block),
            swap(scaled_cols, "seq"),
            swap(w_in, "dp", repeat=True),
            swap(columns(w_qb, parts), "seq"),
        ],
        passes=[w_o.astype(jnp.bfloat16)],
    )
    gain_one = gains[:, :, 0, : spans[0]].reshape(1, -1)
    gain_latent = gains[:, :, 1, : spans[1]].reshape(1, -1)
    gain_key = gains[:, :, 2, : spans[2]].reshape(1, -1)
    gain_two = gains[:, :, 3, : spans[3]].reshape(1, -1)
    gain_mine = gains_line[:, 0, : spans[0]].reshape(1, -1)

    o_rows = lax.all_gather(o_low, "dp", axis=0, tiled=True)
    qb_cols = join(qb_cols)

    in_rows = in_rows.reshape(width, inner)
    normed = (scaled_cols.reshape(group_tokens, width) * gain_mine).astype(jnp.bfloat16)
    partial = dot(normed, in_rows).astype(jnp.bfloat16).reshape(parts, tok_rows, inner)

    def latent_rows(total, row, vec):
        latent, key, value = total[:, :rank], total[:, rank : rank + E], total[:, rank + E :]
        low = jnp.concatenate(
            [rms_scale(latent, vec[0]), rotate(rms_scale(key, vec[1]), row[0], row[1]), value],
            axis=1,
        )
        return low, [total], None

    chips = parts // 2
    both_cols = fold(list(lax.optimization_barrier((w_gate, w_up))), chips, groups)
    (gathered, inner_own), (both_cols,), (down_rows,) = launch(
        "latent",
        1,
        [
            exchange(
                partial,
                [cosine, sine_tab],
                [gain_latent, gain_key],
                latent_rows,
                [inner],
                inner,
                0,
            ),
            swap(both_cols, "line"),
            gather_chips(w_down.astype(jnp.bfloat16)),
        ],
    )
    gathered = gathered.reshape(group_tokens, inner)
    seg_col = segment[:, None]
    seg_rows = jnp.stack(
        [
            lax.slice_in_dim(segment, start, start + group_tokens // 2 + QUERIES)
            for start in [
                min(max(0, first - group_tokens // 2), group_tokens // 2 - QUERIES)
                for first in range(0, group_tokens, QUERIES)
            ]
        ]
    )[:, None, :]
    ((q_rot, attended_low),) = launch(
        "attend", 2, [attend(gathered, qb_cols, cos_all, sin_all, seg_col, seg_rows)]
    )
    down_rows = down_rows.reshape(-1, D)
    partial = dot(attended_low, o_rows).astype(jnp.bfloat16).reshape(parts, tok_rows, D)

    def mixed_function(total, row, vec):
        mixed = row[0] + total
        return rms_scale(mixed, vec[0]), [mixed], None

    (two_all, mixed_rows), (grad_all,) = launch(
        "mixed",
        3,
        [
            exchange(
                partial,
                [flat_rows],
                [gain_two],
                mixed_function,
                [D],
                D,
                0,
                spread_axis="dp",
            ),
            gather(out_grad.astype(jnp.bfloat16), "dp"),
        ],
    )
    wide = both_cols.shape[2]
    piece = both_cols.shape[1]
    both_cols = chip_gather(both_cols.reshape(-1, wide), parts)
    both_cols = both_cols.reshape(chips, groups, 2, piece, wide)
    both_cols = jnp.transpose(both_cols, (0, 2, 1, 3, 4)).reshape(D, wide)

    ((mixed_grad, mixed_low, gain_two_grad, out_part, down_low, both_low),) = launch(
        "feed_forward",
        9,
        [
            feed_forward(
                two_all, grad_all, both_cols, down_rows, mixed_rows, out_grad, gain_two
            )
        ],
    )
    both_shard = chip_scatter(both_low.reshape(D, wide), parts).reshape(2 * groups, piece, wide)

    def out_function(total, row, vec):
        return None, [row[0] + total], None

    mixed_task = gather(mixed_low, "chip", VMEM)
    back_task = attend_back(
        gathered,
        q_rot,
        jax.ShapeDtypeStruct((parts, tok_rows, D), jnp.bfloat16),
        o_rows,
        qb_cols,
        cos_all,
        sin_all,
        seg_col,
        seg_rows,
    )
    (output_rows,), (mixed_all, query_grad, partial) = launch(
        "attend_back",
        4,
        [
            exchange(out_part, [mixed_rows], [], out_function, [D], 0, 0, sum_axis="dp"),
            chain(mixed_task, back_task, {2: 0}),
        ],
    )
    mixed_all = tie(mixed_all, [both_shard]).reshape(group_tokens, D)
    o_shard, o_low = scatter_rows(
        jnp.einsum("tf,td->fd", attended_low, mixed_all, preferred_element_type=jnp.float32)
    )
    qb_shard, qb_low = scatter_columns(
        jnp.einsum("tr,tf->rf", gathered[:, :rank], query_grad, preferred_element_type=jnp.float32),
        parts,
        groups,
    )

    def inner_function(total, row, vec):
        latent_grad, latent_gain = back_rows(row[0][:, :rank], vec[0], total[:, :rank])
        key_back = rotate_back(total[:, rank : rank + E], row[1], row[2])
        key_grad, key_gain = back_rows(row[0][:, rank : rank + E], vec[1], key_back)
        low = jnp.concatenate([latent_grad, key_grad, total[:, rank + E :]], axis=1)
        return low, [], jnp.concatenate([latent_gain, key_gain], axis=1)

    (in_grad, inner_gain_grad), (both_shard,), (down_shard,) = launch(
        "inner_grad",
        5,
        [
            exchange(
                partial.reshape(parts, tok_rows, inner),
                [inner_own, cosine, sine_tab],
                [gain_latent, gain_key],
                inner_function,
                [],
                inner,
                rank + E,
            ),
            swap(both_shard, "line"),
            paused(chip_sum(down_low.reshape(chips, -1, D)), 2),
        ],
        needs=[o_low, qb_low],
    )
    in_grad = in_grad.reshape(group_tokens, inner)
    in_low = jnp.einsum("td,tr->dr", normed, in_grad, preferred_element_type=jnp.float32)
    in_low = in_low.astype(jnp.bfloat16).reshape(groups, -1, inner)
    normed_part = jnp.einsum("tr,dr->td", in_grad, in_rows, preferred_element_type=jnp.float32)
    normed_part = normed_part.astype(jnp.bfloat16).reshape(parts, tok_rows, width)

    (normed_grad,), (in_shard,) = launch(
        "normed_grad",
        6,
        [swap(normed_part, "seq"), swap(in_low, "dp")],
    )
    in_shard = jnp.sum(in_shard.astype(jnp.float32), axis=0)
    normed_grad = jnp.transpose(normed_grad.astype(jnp.float32), (1, 0, 2)).reshape(tok_rows, D)
    input_part, gain_one_grad = back_rows(flat_rows, gain_one, normed_grad)
    input_grad = mixed_grad + input_part

    gain_grads = [
        jnp.sum(gain_one_grad, axis=0),
        jnp.sum(inner_gain_grad[:, :rank], axis=0),
        jnp.sum(inner_gain_grad[:, rank:], axis=0),
        jnp.sum(gain_two_grad, axis=0),
    ]
    gain_grads = jnp.stack(
        [
            jnp.pad(g.reshape(parts, groups, n), ((0, 0), (0, 0), (0, 128 - n)))
            for g, n in zip(gain_grads, spans, strict=True)
        ]
        + [jnp.zeros((parts, groups, 128), jnp.float32)] * 4,
        axis=2,
    )
    (gain_own,), (qb_shard,) = launch("end", 7, [sum_both(gain_grads), swap(qb_shard, "seq")])
    gate_grad, up_grad = unfold_pair(both_shard, chips, groups)
    return (
        output_rows.reshape(1, tok_rows, D),
        input_grad.reshape(1, tok_rows, D),
        gain_own[0, : spans[0]],
        in_shard[:, :rank],
        gain_own[1, : spans[1]],
        unfold(qb_shard),
        in_shard[:, rank : rank + E],
        gain_own[2, : spans[2]],
        in_shard[:, rank + E :],
        o_shard.astype(jnp.float32),
        gain_own[3, : spans[3]],
        gate_grad,
        up_grad,
        down_shard.astype(jnp.float32),
    )


def solution(mesh):
    return jax.shard_map(
        local,
        mesh=mesh,
        in_specs=(
            P("dp", "seq", None),
            P("dp", None),
            P("dp", "seq", None),
            P(("seq", "dp")),
            P(("seq", "dp"), None),
            P(("seq", "dp")),
            P(("seq", "dp"), None),
            P(("seq", "dp"), None),
            P(("seq", "dp")),
            P(("seq", "dp"), None),
            P(("seq", "dp"), None),
            P(("seq", "dp")),
            P(("seq", "dp"), None),
            P(("seq", "dp"), None),
            P(("seq", "dp"), None),
        ),
        out_specs=(
            P("dp", "seq", None),
            P("dp", "seq", None),
            P(("seq", "dp")),
            P(("seq", "dp"), None),
            P(("seq", "dp")),
            P(("seq", "dp"), None),
            P(("seq", "dp"), None),
            P(("seq", "dp")),
            P(("seq", "dp"), None),
            P(("seq", "dp"), None),
            P(("seq", "dp")),
            P(("seq", "dp"), None),
            P(("seq", "dp"), None),
            P(("seq", "dp"), None),
        ),
        check_vma=False,
    )
```

```python
import math

import jax
import jax.numpy as jnp
from jax import lax
from jax.experimental import pallas as pl
from jax.experimental.pallas import tpu as pltpu
from jax.sharding import PartitionSpec as P

D = 2048
H = 16
E = 256


MESH = pl.DeviceIdType.MESH
STEP = 16
QUERIES = 256
VMEM_LIMIT = 60 * 1024 * 1024
COST = pl.CostEstimate(flops=0, transcendentals=0, bytes_accessed=1024)

eps_norm = 1e-06
big_negative = -1e30


def rms_scale(values, gain_vec):
    inverse = lax.rsqrt(jnp.mean(values * values, axis=-1, keepdims=True) + eps_norm)
    return values * inverse * gain_vec


def norm_back(values, gain_vec, upstream):
    inverse = lax.rsqrt(jnp.mean(values * values, axis=-1, keepdims=True) + eps_norm)
    gain_grad = jnp.sum(upstream * values * inverse, axis=0)
    scaled = upstream * gain_vec
    value_grad = inverse * scaled - values * (inverse * inverse * inverse) * jnp.mean(
        scaled * values, axis=-1, keepdims=True
    )
    return (value_grad, gain_grad)


def rotate(values, cosine, sine_tab):
    half_width = values.shape[-1] // 2
    turned = jnp.concatenate([-values[..., half_width:], values[..., :half_width]], axis=-1)
    return values * cosine + turned * sine_tab


def rotate_back(upstream, cosine, sine_tab):
    half_width = upstream.shape[-1] // 2
    weighted = upstream * sine_tab
    turned = jnp.concatenate([weighted[..., half_width:], -weighted[..., :half_width]], axis=-1)
    return upstream * cosine + turned


def layout(seq_lengths, group_tokens):
    seq_ends = jnp.cumsum(seq_lengths)
    places = jnp.arange(group_tokens, dtype=jnp.int32)
    passed = places[:, None] >= seq_ends[None, :]
    segment = jnp.sum(passed.astype(jnp.int32), axis=1)
    starts = jnp.sum(jnp.where(passed, seq_lengths[None, :], 0), axis=1)
    return (segment, places, places - starts)


def rope_tables(offsets, width):
    half_width = width // 2
    frequency = jnp.exp(
        jnp.arange(half_width, dtype=jnp.float32) * (-2.0 * math.log(10000.0) / width)
    )
    angles = offsets.astype(jnp.float32)[:, None] * frequency[None, :]
    angles = jnp.concatenate([angles, angles], axis=-1)
    return (jnp.cos(angles), jnp.sin(angles))


VMEM = pl.BlockSpec(memory_space=pltpu.VMEM)
ANY = pl.BlockSpec(memory_space=pl.ANY)
SIBLING = (1, 0)


def flip(index, bits):
    out, power = index, 1
    while power <= bits:
        if bits & power:
            out = out + power - 2 * power * ((index // power) % 2)
        power *= 2
    return out


def here():
    return lax.axis_index("seq"), lax.axis_index("dp")


def device(mask):
    me, group = here()
    return flip(me, mask[0]), flip(group, mask[1])


def copy_to(source, target, sems, seq_to, dp_to):
    return pltpu.make_async_remote_copy(
        src_ref=source,
        dst_ref=target,
        send_sem=sems.at[0],
        recv_sem=sems.at[1],
        device_id=(seq_to, dp_to),
        device_id_type=MESH,
    )


def remote(source, target, sems, mask):
    copy = copy_to(source, target, sems, *device(mask))
    copy.start()
    return copy


def keep(source, target, sem):
    copy = pltpu.make_async_copy(source, target, sem)
    copy.start()
    return copy


class Task:
    def __init__(self, inputs, outputs, scratch, masks, run):
        self.inputs, self.outputs, self.scratch = inputs, outputs, scratch
        self.masks, self.run = masks, run


def launch(name, collective_id, tasks, needs=(), passes=(), turns=()):
    masks = sorted({mask for task in tasks for mask in task.masks})
    n_in = sum(len(task.inputs) for task in tasks)
    n_out = sum(len(task.outputs) for task in tasks)

    def body(*refs):
        refs = list(refs)
        ins = refs[:n_in]
        refs = refs[n_in + len(needs) + len(passes) :]
        outs, scratch = refs[:n_out], refs[n_out + len(passes) :]
        if masks:
            barrier = pltpu.get_barrier_semaphore()
            for mask in masks:
                pl.semaphore_signal(barrier, inc=1, device_id=device(mask), device_id_type=MESH)
            pl.semaphore_wait(barrier, len(masks))
        running = []
        for task in tasks:
            a, b, c = len(task.inputs), len(task.outputs), len(task.scratch)
            running.append(task.run(ins[:a], outs[:b], scratch[:c]))
            ins, outs, scratch = ins[a:], outs[b:], scratch[c:]
        for turn in turns:
            next(running[turn], None)
        while running:
            for step in list(running):
                if next(step, "done") == "done":
                    running.remove(step)

    inputs = [pair for task in tasks for pair in task.inputs]
    outputs = [pair for task in tasks for pair in task.outputs]
    results = pl.pallas_call(
        body,
        name=name,
        out_shape=[shape for shape, _ in outputs]
        + [jax.ShapeDtypeStruct(a.shape, a.dtype) for a in passes],
        in_specs=[spec for _, spec in inputs] + [ANY] * (len(needs) + len(passes)),
        out_specs=[spec for _, spec in outputs] + [ANY] * len(passes),
        input_output_aliases={n_in + len(needs) + i: n_out + i for i in range(len(passes))},
        scratch_shapes=[shape for task in tasks for shape in task.scratch],
        compiler_params=pltpu.CompilerParams(
            collective_id=collective_id if masks else None,
            has_side_effects=bool(masks),
            vmem_limit_bytes=VMEM_LIMIT,
        ),
        cost_estimate=COST,
    )(*[array for array, _ in inputs], *needs, *passes)
    results, split = list(results), []
    for task in tasks:
        split.append(results[: len(task.outputs)])
        results = results[len(task.outputs) :]
    return split + results


def chain(first, second, links):
    inputs = [pair for i, pair in enumerate(second.inputs) if i not in links]
    a, b, c = len(first.inputs), len(first.outputs), len(first.scratch)

    def run(ins, outs, scratch):
        yield from first.run(ins[:a], outs[:b], scratch[:c])
        rest = list(ins[a:])
        joined = [outs[links[i]] if i in links else rest.pop(0) for i in range(len(second.inputs))]
        yield from second.run(joined, outs[b:], scratch[c:])

    return Task(
        first.inputs + inputs,
        first.outputs + second.outputs,
        first.scratch + second.scratch,
        first.masks + second.masks,
        run,
    )


def paused(task, pauses):
    def run(ins, outs, scratch):
        for _ in range(pauses):
            yield
        yield from task.run(ins, outs, scratch)

    return Task(task.inputs, task.outputs, task.scratch, task.masks, run)


def rows_loop(start, stop, step):
    def one(i, carry):
        step(pl.ds(pl.multiple_of(i * STEP, STEP), STEP))
        return carry

    lax.fori_loop(start // STEP, stop // STEP, one, 0)


def axis_masks(axis):
    if axis == "chip":
        return [(2 * j, 0) for j in range(1, lax.axis_size("seq") // 2)]
    return [(0, j) for j in range(1, lax.axis_size("dp"))]


def axis_block(axis, mask=(0, 0)):
    seq_at, dp_at = device(mask)
    return seq_at if axis == "chip" else dp_at * 2 + seq_at % 2


def line_masks():
    masks, power = [], 2
    while power <= lax.axis_size("dp"):
        masks.append((0, power - 1))
        power *= 2
    return masks


def spread_masks(axis):
    if axis == "dp":
        return [SIBLING] + line_masks()
    return [SIBLING] + axis_masks(axis)


def spread(axis, low, all_ref, keep_sem, sems):
    own = all_ref.at[axis_block(axis)]
    rows = low.shape[0]
    sends = []
    if axis == "dp":
        yield from spread_line(low, all_ref, keep_sem, sems)
        return
    masks = axis_masks(axis)
    square = len(masks) == 3
    direct = [(2, 0), (4, 0)] if square else masks
    for i, mask in enumerate(direct):
        sends.append(remote(low, own, sems.at[i], mask))
    beside = [remote(low, own, sems.at[len(masks)], SIBLING)]
    kept = keep(low, own, keep_sem)
    yield
    at, halves = len(masks) + 1, []

    def block(mask):
        return all_ref.at[axis_block(axis, mask)]

    def half(mask, which):
        return all_ref.at[axis_block(axis, mask), pl.ds(which * (rows // 2), rows // 2)]

    for i, mask in enumerate(direct):
        sends[i].wait_recv()
        if square:
            halves.append(remote(half(mask, i), half(mask, i), sems.at[at], direct[1 - i]))
            at += 1
        beside.append(remote(block(mask), block(mask), sems.at[at], SIBLING))
        at += 1
        yield
    for i, copy in enumerate(halves):
        copy.wait_recv()
        part = half((6, 0), i)
        beside.append(remote(part, part, sems.at[at], SIBLING))
        at += 1
        yield
    for copy in beside:
        copy.wait_recv()
    for copy in sends + halves + beside:
        copy.wait_send()
    kept.wait()


def spread_line(low, all_ref, keep_sem, sems):
    me, group = here()
    core, groups = me % 2, lax.axis_size("dp")
    own = all_ref.at[axis_block("dp")]
    kept = keep(low, own, keep_sem)
    beside = remote(low, own, sems.at[0], SIBLING)

    def at(way, k, kind):
        return sems.at[1 + (way * (groups - 1) + k) * 2 + kind]

    def hop(way, k):
        step = 1 - 2 * way
        block = all_ref.at[(group - step * k) * 2 + core]
        return copy_to(low if k == 0 else block, block, at(way, k, 0), me, group + step)

    def landed(way, k):
        block = all_ref.at[(group - (1 - 2 * way) * (k + 1)) * 2 + core]
        return copy_to(block, block, at(way, k, 0), *device(SIBLING))

    def aside(way, k):
        block = all_ref.at[(group - (1 - 2 * way) * (k + 1)) * 2 + core]
        return copy_to(block, block, at(way, k, 1), *device(SIBLING))

    def sends(way, k):
        if way == 0:
            return (group >= k) & (group < groups - 1)
        return (group + k < groups) & (group > 0)

    def lands(way, k):
        return (group >= k + 1) if way == 0 else (group + k + 1 < groups)

    for k in range(groups - 1):
        for way in range(2):

            @pl.when(sends(way, k))
            def _(way=way, k=k):
                hop(way, k).start()

        yield
        for way in range(2):

            @pl.when(lands(way, k))
            def _(way=way, k=k):
                landed(way, k).wait_recv()
                aside(way, k).start()

    yield
    beside.wait_recv()
    for k in range(groups - 1):
        for way in range(2):

            @pl.when(lands(way, k))
            def _(way=way, k=k):
                aside(way, k).wait()

            @pl.when(sends(way, k))
            def _(way=way, k=k):
                hop(way, k).wait_send()

    beside.wait_send()
    kept.wait()


def exchange(
    partial,
    row_operands,
    vec_operands,
    row_function,
    own_widths,
    low_width,
    vec_width,
    sum_axis="chip",
    spread_axis="chip",
    all_space=ANY,
):
    blocks, rows, cols = partial.shape
    far = blocks // 2
    n_rows = len(row_operands)
    masks = axis_masks(sum_axis)
    square = sum_axis == "chip" and len(masks) == 3
    out_blocks = lax.axis_size("seq") if spread_axis == "chip" else 2 * lax.axis_size("dp")
    order = list(range(far - 1, 0, -1)) + [0]
    at_mask = [(0, 0)] + masks

    def run(ins, outs, scratch):
        ins, outs = list(ins), list(outs)
        partial_ref = ins.pop(0)
        row_refs, vec_refs = ins[:n_rows], ins[n_rows:]
        all_ref = outs.pop(0) if low_width else None
        vec_out = outs.pop(-1) if vec_width else None
        mine, beside, arrived, low, local_sem, sems, out_sems = scratch

        across, loads = {}, {}
        for j in order:
            block = axis_block(sum_axis, at_mask[j])
            other = axis_block(sum_axis, (at_mask[j][0] + 1, at_mask[j][1]))
            across[j] = remote(partial_ref.at[other], beside.at[j], sems.at[j], SIBLING)
            loads[j] = keep(partial_ref.at[block], mine.at[j], local_sem.at[j])
        yield
        sent = []

        def settle(j, low_row=0, high_row=rows, more=None):
            def add(at):
                total = mine[j, at, :].astype(jnp.float32) + beside[j, at, :].astype(jnp.float32)
                if more is not None:
                    total = total + arrived[more, at, :].astype(jnp.float32)
                mine[j, at, :] = total.astype(jnp.bfloat16)

            rows_loop(low_row, high_row, add)

        if square:
            middle = rows // 2
            first, second = pl.ds(0, middle), pl.ds(middle, middle)
            for j in (3, 1, 2):
                loads[j].wait()
                across[j].wait_recv()
                if j == 3:
                    settle(3)
                elif j == 1:
                    settle(1, 0, middle)
                else:
                    settle(2, middle, rows)
                base = far + 2 * (j - 1)
                if j in (3, 1):
                    sent.append(
                        remote(mine.at[j, first], arrived.at[j, first], sems.at[base], (2, 0))
                    )
                if j in (3, 2):
                    sent.append(
                        remote(mine.at[j, second], arrived.at[j, second], sems.at[base + 1], (4, 0))
                    )
            yield
            diagonal_x, diagonal_y = sent[0], sent[1]
            diagonal_x.wait_recv()
            settle(2, 0, middle, more=3)
            sent.append(
                remote(mine.at[2, first], arrived.at[2, first], sems.at[far + 2], (4, 0))
            )
            diagonal_y.wait_recv()
            settle(1, middle, rows, more=3)
            sent.append(
                remote(mine.at[1, second], arrived.at[1, second], sems.at[far + 1], (2, 0))
            )
            yield
            adds = [1, 2]
            landed = sent[2:]
        else:
            for j in order[:-1]:
                loads[j].wait()
                across[j].wait_recv()
                settle(j)
                sent.append(remote(mine.at[j], arrived.at[j], sems.at[far + j], at_mask[j]))
            yield
            adds = order[:-1]
            landed = sent
        loads[0].wait()
        across[0].wait_recv()
        for copy in landed:
            copy.wait_recv()
        if vec_width:
            vec_out[...] = jnp.zeros_like(vec_out)
        vecs = [v[...] for v in vec_refs]

        def finish(at):
            total = mine[0, at, :].astype(jnp.float32) + beside[0, at, :].astype(jnp.float32)
            for j in adds:
                total = total + arrived[j, at, :].astype(jnp.float32)
            low_now, own_now, vec_now = row_function(total, [r[at, :] for r in row_refs], vecs)
            if low_width:
                low[at, :] = low_now.astype(jnp.bfloat16)
            for ref, value in zip(outs, own_now, strict=True):
                ref[at, :] = value
            if vec_width:
                vec_out[...] += vec_now

        rows_loop(0, rows, finish)
        if low_width:
            yield from spread(spread_axis, low, all_ref, local_sem.at[0], out_sems)
        for copy in list(across.values()) + sent:
            copy.wait_send()

    outputs = []
    if low_width:
        shape = jax.ShapeDtypeStruct((out_blocks, rows, low_width), jnp.bfloat16)
        outputs.append((shape, all_space))
    outputs += [(jax.ShapeDtypeStruct((rows, width), jnp.float32), VMEM) for width in own_widths]
    if vec_width:
        outputs.append((jax.ShapeDtypeStruct((STEP, vec_width), jnp.float32), VMEM))
    return Task(
        [(partial, ANY)] + [(a, VMEM) for a in list(row_operands) + list(vec_operands)],
        outputs,
        [
            pltpu.VMEM((far, rows, cols), jnp.bfloat16),
            pltpu.VMEM((far, rows, cols), jnp.bfloat16),
            pltpu.VMEM((far, rows, cols), jnp.bfloat16),
            pltpu.VMEM((rows, max(low_width, 128)), jnp.bfloat16),
            pltpu.SemaphoreType.DMA((far,)),
            pltpu.SemaphoreType.DMA((far + max(6, far), 2)),
            pltpu.SemaphoreType.DMA((spread_sems(spread_axis), 2)),
        ],
        [SIBLING] + masks + (spread_masks(spread_axis) if low_width else []),
        run,
    )


def spread_sems(axis):
    if axis == "dp":
        return 1 + 4 * (lax.axis_size("dp") - 1)
    return 2 * lax.axis_size("seq")


def gather(low, axis, all_space=ANY):
    rows, cols = low.shape
    blocks = lax.axis_size("seq") if axis == "chip" else 2 * lax.axis_size("dp")

    def run(ins, outs, scratch):
        yield from spread(axis, ins[0], outs[0], scratch[0].at[0], scratch[1])

    return Task(
        [(low, ANY)],
        [(jax.ShapeDtypeStruct((blocks, rows, cols), low.dtype), all_space)],
        [pltpu.SemaphoreType.DMA((1,)), pltpu.SemaphoreType.DMA((spread_sems(axis), 2))],
        spread_masks(axis),
        run,
    )


def family(kind):
    parts, groups = lax.axis_size("seq"), lax.axis_size("dp")
    if kind == "seq":
        return [(m, 0) for m in range(1, parts)], lambda s, d: s
    if kind == "dp":
        return [(0, m) for m in range(1, groups)], lambda s, d: d
    return [(m % 2, m // 2) for m in range(1, 2 * groups)], lambda s, d: d * 2 + s % 2


def swap(array, kind, repeat=False):
    masks, index = family(kind)

    def run(ins, outs, scratch):
        own = index(*here())
        copies = [keep(ins[0] if repeat else ins[0].at[own], outs[0].at[own], scratch[0].at[0])]
        for i, mask in enumerate(masks):
            source = ins[0] if repeat else ins[0].at[index(*device(mask))]
            copies.append(remote(source, outs[0].at[own], scratch[1].at[i], mask))
        yield
        for copy in copies:
            copy.wait()

    shape = (len(masks) + 1,) + array.shape if repeat else array.shape
    return Task(
        [(array, ANY)],
        [(jax.ShapeDtypeStruct(shape, array.dtype), ANY)],
        [pltpu.SemaphoreType.DMA((1,)), pltpu.SemaphoreType.DMA((len(masks), 2))],
        masks,
        run,
    )


def gather_both(array):
    seq_masks, dp_masks = family("seq")[0], family("dp")[0]
    parts, groups = lax.axis_size("seq"), lax.axis_size("dp")

    def run(ins, outs, scratch):
        me, group = here()
        (small,), (everything, line) = ins, outs
        copies = [keep(small, line.at[group], scratch[0].at[0])]
        for i, mask in enumerate(dp_masks):
            copies.append(remote(small, line.at[group], scratch[1].at[i], mask))
        yield
        for copy in copies:
            copy.wait()
        copies = [keep(line, everything.at[me], scratch[0].at[1])]
        for i, mask in enumerate(seq_masks):
            at = scratch[1].at[len(dp_masks) + i]
            copies.append(remote(line, everything.at[me], at, mask))
        yield
        for copy in copies:
            copy.wait()

    return Task(
        [(array, VMEM)],
        [
            (jax.ShapeDtypeStruct((parts, groups) + array.shape, array.dtype), VMEM),
            (jax.ShapeDtypeStruct((groups,) + array.shape, array.dtype), VMEM),
        ],
        [
            pltpu.SemaphoreType.DMA((2,)),
            pltpu.SemaphoreType.DMA((len(seq_masks) + len(dp_masks), 2)),
        ],
        seq_masks + dp_masks,
        run,
    )


def sum_both(array):
    seq_masks, dp_masks = family("seq")[0], family("dp")[0]

    def run(ins, outs, scratch):
        me, group = here()
        stage_one, line, stage_two, local_sem, sems = scratch
        copies = [keep(ins[0].at[me], stage_one.at[me], local_sem.at[0])]
        for i, mask in enumerate(seq_masks):
            source = ins[0].at[flip(me, mask[0])]
            copies.append(remote(source, stage_one.at[me], sems.at[i], mask))
        yield
        for copy in copies:
            copy.wait()
        line[...] = jnp.sum(stage_one[...], axis=0)
        copies = [keep(line.at[group], stage_two.at[group], local_sem.at[1])]
        for i, mask in enumerate(dp_masks):
            at = sems.at[len(seq_masks) + i]
            copies.append(remote(line.at[flip(group, mask[1])], stage_two.at[group], at, mask))
        yield
        for copy in copies:
            copy.wait()
        outs[0][...] = jnp.sum(stage_two[...], axis=0)

    return Task(
        [(array, VMEM)],
        [(jax.ShapeDtypeStruct(array.shape[2:], array.dtype), VMEM)],
        [
            pltpu.VMEM(array.shape, array.dtype),
            pltpu.VMEM(array.shape[1:], array.dtype),
            pltpu.VMEM(array.shape[1:], array.dtype),
            pltpu.SemaphoreType.DMA((2,)),
            pltpu.SemaphoreType.DMA((len(seq_masks) + len(dp_masks), 2)),
        ],
        seq_masks + dp_masks,
        run,
    )


def tie(value, needs):
    def body(*refs):
        pass

    return pl.pallas_call(
        body,
        name="tie",
        out_shape=jax.ShapeDtypeStruct(value.shape, value.dtype),
        in_specs=[ANY] * (1 + len(needs)),
        out_specs=ANY,
        input_output_aliases={0: 0},
        cost_estimate=COST,
    )(value, *needs)


def gather_chips(low):
    rows = low.shape[0]
    middle = rows // 2 // STEP * STEP if len(low.shape) == 2 else rows // 2
    masks = axis_masks("chip")
    square = len(masks) == 3

    def run(ins, outs, scratch):
        me, _ = here()
        low_ref, all_ref, (local_sem, sems) = ins[0], outs[0], scratch

        def block(mask):
            return all_ref.at[device(mask)[0] // 2]

        def half(mask, which):
            part = pl.ds(middle, rows - middle) if which else pl.ds(0, middle)
            return all_ref.at[device(mask)[0] // 2, part]

        kept = keep(low_ref, block((0, 0)), local_sem.at[0])
        direct = [(2, 0), (4, 0)] if square else masks
        copies = [
            remote(low_ref, block((0, 0)), sems.at[i], mask) for i, mask in enumerate(direct)
        ]
        yield
        if square:
            for i, mask in enumerate(direct):
                copies[i].wait_recv()
                part = half(mask, i)
                copies.append(remote(part, part, sems.at[2 + i], direct[1 - i]))
            yield
            copies[0].wait_send()
            copies[1].wait_send()
            copies = copies[2:]
        for copy in copies:
            copy.wait()
        kept.wait()

    return Task(
        [(low, ANY)],
        [(jax.ShapeDtypeStruct((len(masks) + 1,) + low.shape, low.dtype), ANY)],
        [pltpu.SemaphoreType.DMA((1,)), pltpu.SemaphoreType.DMA((max(4, len(masks)), 2))],
        masks,
        run,
    )


def lanes_of(sources, segments, tile, rows):
    lane = lax.broadcasted_iota(jnp.int32, (rows, 128), 1)
    out = jnp.zeros((rows, 128), jnp.float32)
    low = tile * 128
    for source, from_col, to_col, length in segments:
        first, last = max(low, to_col), min(low + 128, to_col + length)
        if first >= last:
            continue
        begin = from_col + first - to_col
        window = begin // 128 * 128
        wide = 128 if begin - window + last - first <= 128 else 256
        held = min(wide, sources[source].shape[1] - window)
        wide = pl.cdiv(held, 128) * 128
        piece = sources[source][:, window : window + held].astype(jnp.float32)
        if held < wide:
            blank = jnp.zeros((rows, wide - held), jnp.float32)
            piece = jnp.concatenate([piece, blank], axis=1)
        shift = (first - low - (begin - window)) % wide
        if shift:
            piece = pltpu.roll(piece, shift, axis=1)
        out = jnp.where((lane >= first - low) & (lane < last - low), piece[:, :128], out)
    return out


def fold(weights, chips, groups):
    rows, cols = weights[0].shape
    units = cols // (2 * chips * groups)
    width = 2 * chips * units

    def body(first_ref, second_ref, out_ref):
        sources = [first_ref, second_ref]
        for group in range(groups):
            for core in range(2):
                segments = [
                    (
                        which,
                        ((chip * 2 + core) * groups + group) * units,
                        (which * chips + chip) * units,
                        units,
                    )
                    for which in range(2)
                    for chip in range(chips)
                ]
                for tile in range(pl.cdiv(width, 128)):
                    value = lanes_of(sources, segments, tile, rows).astype(jnp.bfloat16)
                    stop = min(width, tile * 128 + 128)
                    out_ref[group * 2 + core, :, tile * 128 : stop] = value[:, : stop - tile * 128]

    return pl.pallas_call(
        body,
        name="fold",
        out_shape=jax.ShapeDtypeStruct((2 * groups, rows, width), jnp.bfloat16),
        in_specs=[VMEM, VMEM],
        out_specs=VMEM,
        compiler_params=pltpu.CompilerParams(vmem_limit_bytes=VMEM_LIMIT),
        cost_estimate=COST,
    )(*weights)


def unfold_pair(pieces, chips, groups):
    _, rows, width = pieces.shape
    units = width // (2 * chips)
    cols = units * 2 * chips * groups

    def body(in_ref, first_ref, second_ref):
        sources = [in_ref.at[i] for i in range(2 * groups)]
        for which, out_ref in enumerate([first_ref, second_ref]):
            segments = [
                (
                    group * 2 + core,
                    (which * chips + chip) * units,
                    ((chip * 2 + core) * groups + group) * units,
                    units,
                )
                for chip in range(chips)
                for core in range(2)
                for group in range(groups)
            ]
            for tile in range(cols // 128):
                out_ref[:, tile * 128 : tile * 128 + 128] = lanes_of(sources, segments, tile, rows)

    shape = jax.ShapeDtypeStruct((rows, cols), jnp.float32)
    return pl.pallas_call(
        body,
        name="unfold",
        out_shape=[shape, shape],
        in_specs=[VMEM],
        out_specs=[VMEM, VMEM],
        compiler_params=pltpu.CompilerParams(vmem_limit_bytes=VMEM_LIMIT),
        cost_estimate=COST,
    )(pieces)


def nt(left, right):
    return lax.dot_general(
        left, right, (((1,), (1,)), ((), ())), preferred_element_type=jnp.float32
    )


def tn(left, right):
    return lax.dot_general(
        left, right, (((0,), (0,)), ((), ())), preferred_element_type=jnp.float32
    )


def window_of(i, tokens):
    wide = tokens // 2 + QUERIES
    start = jnp.clip(i * QUERIES - tokens // 2, 0, tokens - wide)
    return pl.multiple_of(start, QUERIES), wide


def probabilities(queries, keys, i, start, seg_col, seg_row):
    scores = nt(queries, keys) * (1.0 / math.sqrt(E))
    row = i * QUERIES + lax.broadcasted_iota(jnp.int32, scores.shape, 0)
    col = start + lax.broadcasted_iota(jnp.int32, scores.shape, 1)
    scores = jnp.where((seg_col == seg_row) & (col <= row), scores, big_negative)
    shifted = jnp.exp(scores - jnp.max(scores, axis=-1, keepdims=True))
    return shifted / jnp.sum(shifted, axis=-1, keepdims=True)


def attend(gathered, qb_cols, o_rows, cosine, sine_tab, seg_col, seg_rows, parts):
    tokens, inner = gathered.shape
    rank, width = qb_cols.shape
    rows, cols = tokens // parts, o_rows.shape[1]
    per = QUERIES // rows

    def run(ins, outs, scratch):
        in_ref, qb_ref, o_ref, cos_ref, sin_ref, seg_ref, segs_ref = ins
        part_ref, q_ref, out_ref = outs

        def block(i, carry):
            at = pl.ds(pl.multiple_of(i * QUERIES, QUERIES), QUERIES)
            start, wide = window_of(i, tokens)
            span = pl.ds(start, wide)
            query = dot(in_ref[at, :rank], qb_ref[...])
            keys, values = in_ref[span, rank : rank + E], in_ref[span, rank + E :]
            for head in range(width // E):
                lanes = slice(head * E, head * E + E)
                rotated = rotate(query[:, lanes], cos_ref[at, :], sin_ref[at, :])
                rotated = rotated.astype(jnp.bfloat16)
                q_ref[at, lanes] = rotated
                probs = probabilities(rotated, keys, i, start, seg_ref[at, :], segs_ref[i])
                out_ref[at, lanes] = dot(probs.astype(jnp.bfloat16), values).astype(jnp.bfloat16)
            part = dot(out_ref[at, :], o_ref[...]).astype(jnp.bfloat16)
            part_ref[pl.ds(i * per, per)] = part.reshape(per, rows, cols)
            return carry

        lax.fori_loop(0, tokens // QUERIES, block, 0)
        yield

    shape = jax.ShapeDtypeStruct((tokens, width), jnp.bfloat16)
    return Task(
        [(a, VMEM) for a in (gathered, qb_cols, o_rows, cosine, sine_tab, seg_col, seg_rows)],
        [
            (jax.ShapeDtypeStruct((parts, rows, cols), jnp.bfloat16), VMEM),
            (shape, VMEM),
            (shape, VMEM),
        ],
        [],
        [],
        run,
    )


def attend_back(
    gathered, queries, out_grad, o_rows, qb_cols, cosine, sine_tab, seg_col, seg_rows
):
    tokens, inner = gathered.shape
    rank, width = qb_cols.shape
    scale = 1.0 / math.sqrt(E)

    def run(ins, outs, scratch):
        in_ref, q_ref, grad_ref, o_ref, qb_ref, cos_ref, sin_ref, seg_ref, segs_ref = ins
        dq_ref, part_ref = outs
        key_sum, value_sum = scratch
        key_sum[...] = jnp.zeros_like(key_sum)
        value_sum[...] = jnp.zeros_like(value_sum)

        def block(i, carry):
            at = pl.ds(pl.multiple_of(i * QUERIES, QUERIES), QUERIES)
            start, wide = window_of(i, tokens)
            span = pl.ds(start, wide)
            per = QUERIES // grad_ref.shape[1]
            upstream = grad_ref[pl.ds(i * per, per)].reshape(QUERIES, grad_ref.shape[2])
            attended_grad = nt(upstream, o_ref[...]).astype(jnp.bfloat16)
            keys, values = in_ref[span, rank : rank + E], in_ref[span, rank + E :]
            for head in range(width // E):
                lanes = slice(head * E, head * E + E)
                query, upstream = q_ref[at, lanes], attended_grad[:, lanes]
                probs = probabilities(query, keys, i, start, seg_ref[at, :], segs_ref[i])
                value_sum[span, :] += tn(probs.astype(jnp.bfloat16), upstream)
                prob_grad = nt(upstream, values)
                delta = jnp.sum(probs * prob_grad, axis=-1, keepdims=True)
                score_grad = (probs * (prob_grad - delta)).astype(jnp.bfloat16)
                key_sum[span, :] += tn(score_grad, query)
                query_grad = dot(score_grad, keys) * scale
                query_grad = rotate_back(query_grad, cos_ref[at, :], sin_ref[at, :])
                dq_ref[at, lanes] = query_grad.astype(jnp.bfloat16)
            part_ref[at, :rank] = nt(dq_ref[at, :], qb_ref[...]).astype(jnp.bfloat16)
            return carry

        lax.fori_loop(0, tokens // QUERIES, block, 0)
        part_ref[:, rank : rank + E] = (key_sum[...] * scale).astype(jnp.bfloat16)
        part_ref[:, rank + E :] = value_sum[...].astype(jnp.bfloat16)
        yield

    return Task(
        [
            (a, VMEM)
            for a in (
                gathered,
                queries,
                out_grad,
                o_rows,
                qb_cols,
                cosine,
                sine_tab,
                seg_col,
                seg_rows,
            )
        ],
        [
            (jax.ShapeDtypeStruct((tokens, width), jnp.bfloat16), VMEM),
            (jax.ShapeDtypeStruct((tokens, inner), jnp.bfloat16), VMEM),
        ],
        [pltpu.VMEM((tokens, E), jnp.float32), pltpu.VMEM((tokens, E), jnp.float32)],
        [],
        run,
    )


def feed_forward(two_all, grad_all, both_cols, down_rows, mixed_rows, out_grad, gain_two):
    line, rows, cols = two_all.shape
    units = down_rows.shape[0]
    far = line // 2
    chips, groups = lax.axis_size("seq") // 2, lax.axis_size("dp")
    masks = axis_masks("dp")
    at_mask = [(0, 0)] + masks
    order = list(range(far - 1, 0, -1)) + [0]
    slab = cols // (2 * chips)
    piece = slab // groups

    def run(ins, outs, scratch):
        two_ref, grad_ref, both_ref, down_ref, mixed_ref, dy_ref, gain_ref = ins
        mixed_out, low_out, vec_out, y_out, down_out, both_out = outs
        mine, give, beside, arrived, hidden, pair_grad, stage, sems, stage_sem = scratch
        core = here()[0] % 2

        def produce(j):
            block = device(at_mask[j])[1] * 2
            both = pl.ds(block, 2)
            x = two_ref[both].reshape(2 * rows, cols)
            dy = grad_ref[both].reshape(2 * rows, cols)
            act = dot(x, both_ref[...])
            gate, up = act[:, :units], act[:, units:]
            sigmoid = jax.nn.sigmoid(gate)
            silu = gate * sigmoid
            hid = (silu * up).astype(jnp.bfloat16)
            hidden[both] = hid.reshape(2, rows, units)
            y_out[both] = dot(hid, down_ref[...]).astype(jnp.bfloat16).reshape(2, rows, cols)
            hid_grad = nt(dy, down_ref[...])
            gate_grad = hid_grad * up * (sigmoid * (1.0 + gate * (1.0 - sigmoid)))
            up_grad = hid_grad * silu
            pair = jnp.concatenate([gate_grad, up_grad], axis=1).astype(jnp.bfloat16)
            pair_grad[both] = pair.reshape(2, rows, 2 * units)
            part = nt(pair, both_ref[...]).astype(jnp.bfloat16)

            @pl.when(core == 0)
            def _():
                mine[j], give[j] = part[:rows], part[rows:]

            @pl.when(core == 1)
            def _():
                mine[j], give[j] = part[rows:], part[:rows]

        across, sent = {}, {}

        def settle(j):
            across[j].wait_recv()

            def add(at):
                total = mine[j, at, :].astype(jnp.float32) + beside[j, at, :].astype(jnp.float32)
                mine[j, at, :] = total.astype(jnp.bfloat16)

            rows_loop(0, rows, add)
            sent[j] = remote(mine.at[j], arrived.at[j], sems.at[far + j], at_mask[j])

        last = None
        for j in order:
            produce(j)
            across[j] = remote(give.at[j], beside.at[j], sems.at[j], SIBLING)
            if last is not None:
                settle(last)
            last = j
        yield

        down_out[...] = tn(
            hidden[...].reshape(line * rows, units), grad_ref[...].reshape(line * rows, cols)
        ).astype(jnp.bfloat16)
        moves = []
        for index in range(2 * chips):
            slot = index % 2
            if index >= 2:
                for move in moves[(index - 2) * groups : (index - 1) * groups]:
                    move.wait()
            x = two_ref[:, :, index * slab : (index + 1) * slab].reshape(line * rows, slab)
            value = tn(x, pair_grad[...].reshape(line * rows, 2 * units))
            stage[slot] = value.astype(jnp.bfloat16).reshape(groups, piece, 2 * units)
            for group in range(groups):
                place = ((index // 2) * groups + group) * 2 + index % 2
                moves.append(
                    keep(stage.at[slot, group], both_out.at[place], stage_sem.at[slot, group])
                )
        for move in moves[-2 * groups :]:
            move.wait()

        across[0].wait_recv()
        for j in order[:-1]:
            sent[j].wait_recv()
        vec_out[...] = jnp.zeros_like(vec_out)
        gain = gain_ref[...]

        def finish(at):
            total = mine[0, at, :].astype(jnp.float32) + beside[0, at, :].astype(jnp.float32)
            for j in order[:-1]:
                total = total + arrived[j, at, :].astype(jnp.float32)
            value_grad, gain_grad = back_rows(mixed_ref[at, :], gain, total)
            mixed_grad = dy_ref[at, :] + value_grad
            mixed_out[at, :] = mixed_grad
            low_out[at, :] = mixed_grad.astype(jnp.bfloat16)
            vec_out[...] += gain_grad

        rows_loop(0, rows, finish)
        for copy in list(across.values()) + list(sent.values()):
            copy.wait_send()

    def low(*shape):
        return jax.ShapeDtypeStruct(shape, jnp.bfloat16)

    blocks = pltpu.VMEM((far, rows, cols), jnp.bfloat16)
    return Task(
        [
            (a, VMEM)
            for a in (two_all, grad_all, both_cols, down_rows, mixed_rows, out_grad, gain_two)
        ],
        [
            (jax.ShapeDtypeStruct((rows, cols), jnp.float32), VMEM),
            (low(rows, cols), VMEM),
            (jax.ShapeDtypeStruct((STEP, cols), jnp.float32), VMEM),
            (low(line, rows, cols), VMEM),
            (low(units, cols), VMEM),
            (low(2 * chips * groups, piece, 2 * units), ANY),
        ],
        [
            blocks,
            blocks,
            blocks,
            blocks,
            pltpu.VMEM((line, rows, units), jnp.bfloat16),
            pltpu.VMEM((line, rows, 2 * units), jnp.bfloat16),
            pltpu.VMEM((2, groups, piece, 2 * units), jnp.bfloat16),
            pltpu.SemaphoreType.DMA((2 * far, 2)),
            pltpu.SemaphoreType.DMA((2, groups)),
        ],
        [SIBLING] + masks,
        run,
    )


def chip_sum(partial):
    chips, rows, cols = partial.shape
    masks = axis_masks("chip")
    square = chips == 4
    middle = rows // 2 // STEP * STEP

    def run(ins, outs, scratch):
        (in_ref,), (out_ref,) = ins, outs
        arrived, held, local_sem, sems = scratch

        def block(j):
            return device(([(0, 0)] + masks)[j])[0] // 2

        def add(target, start, stop, *terms):
            def one(at):
                total = terms[0][at, :].astype(jnp.float32)
                for term in terms[1:]:
                    total = total + term[at, :].astype(jnp.float32)
                target[at, :] = total.astype(jnp.bfloat16)

            rows_loop(start, stop, one)

        own = keep(in_ref.at[block(0)], held.at[0], local_sem.at[0])
        if not square:
            copies = [
                remote(in_ref.at[block(j)], arrived.at[j - 1], sems.at[j - 1], masks[j - 1])
                for j in range(1, chips)
            ]
            yield
            own.wait()
            for copy in copies:
                copy.wait_recv()
            add(out_ref, 0, rows, held.at[0], *[arrived.at[j] for j in range(chips - 1)])
            for copy in copies:
                copy.wait_send()
            return
        first, second = pl.ds(0, middle), pl.ds(middle, rows - middle)
        over_x, over_y = (2, 0), (4, 0)
        copies = [
            remote(in_ref.at[block(3), first], arrived.at[2, first], sems.at[0], over_x),
            remote(in_ref.at[block(3), second], arrived.at[2, second], sems.at[1], over_y),
            remote(in_ref.at[block(1), first], arrived.at[0, first], sems.at[2], over_x),
            remote(in_ref.at[block(2), second], arrived.at[1, second], sems.at[3], over_y),
        ]
        loads = [
            keep(in_ref.at[block(2), first], held.at[1, first], local_sem.at[1]),
            keep(in_ref.at[block(1), second], held.at[1, second], local_sem.at[2]),
        ]
        yield
        loads[0].wait()
        copies[0].wait_recv()
        add(held.at[1], 0, middle, held.at[1], arrived.at[2])
        copies.append(remote(held.at[1, first], arrived.at[1, first], sems.at[4], over_y))
        loads[1].wait()
        copies[1].wait_recv()
        add(held.at[1], middle, rows, held.at[1], arrived.at[2])
        copies.append(remote(held.at[1, second], arrived.at[0, second], sems.at[5], over_x))
        yield
        own.wait()
        for copy in copies[2:]:
            copy.wait_recv()
        add(out_ref, 0, rows, held.at[0], arrived.at[0], arrived.at[1])
        for copy in copies:
            copy.wait_send()

    return Task(
        [(partial, ANY)],
        [(jax.ShapeDtypeStruct((rows, cols), jnp.bfloat16), VMEM)],
        [
            pltpu.VMEM((chips - 1, rows, cols), jnp.bfloat16),
            pltpu.VMEM((2, rows, cols), jnp.bfloat16),
            pltpu.SemaphoreType.DMA((3,)),
            pltpu.SemaphoreType.DMA((max(6, chips), 2)),
        ],
        masks,
        run,
    )


def dot(left, right):
    return jnp.dot(left, right, preferred_element_type=jnp.float32)


def back_rows(values, gain, upstream):
    inverse = lax.rsqrt(jnp.mean(values * values, axis=-1, keepdims=True) + eps_norm)
    scaled = upstream * gain
    value_grad = inverse * scaled - values * (inverse * inverse * inverse) * jnp.mean(
        scaled * values, axis=-1, keepdims=True
    )
    return value_grad, upstream * values * inverse


def columns(weight, parts):
    rows, cols = weight.shape
    low = weight.astype(jnp.bfloat16).reshape(rows, parts, cols // parts)
    return jnp.transpose(low, (1, 0, 2))


def join(pieces):
    parts, rows, cols = pieces.shape
    full = lax.all_gather(pieces.reshape(parts * rows, cols), "dp", axis=0, tiled=True)
    full = full.reshape(-1, parts, rows, cols)
    return jnp.transpose(full, (1, 0, 2, 3)).reshape(-1, cols)


def scatter_columns(grad, parts, groups):
    rows, cols = grad.shape
    piece = rows // (parts * groups)
    low = grad.astype(jnp.bfloat16).reshape(parts, groups, piece, cols)
    low = jnp.transpose(low, (1, 0, 2, 3)).reshape(rows, cols)
    own = lax.psum_scatter(low, "dp", scatter_dimension=0, tiled=True)
    return own.reshape(parts, piece, cols), low


def scatter_rows(grad):
    low = grad.astype(jnp.bfloat16)
    return lax.psum_scatter(low, "dp", scatter_dimension=0, tiled=True), low


def unfold(pieces):
    parts, rows, cols = pieces.shape
    return jnp.transpose(pieces, (1, 0, 2)).reshape(rows, parts * cols).astype(jnp.float32)


def chip_groups(parts):
    return [[chip * 2 + core for chip in range(parts // 2)] for core in range(2)]


def chip_gather(rows, parts):
    return lax.all_gather(rows, "seq", axis=0, tiled=True, axis_index_groups=chip_groups(parts))


def chip_scatter(rows, parts):
    return lax.psum_scatter(
        rows, "seq", scatter_dimension=0, tiled=True, axis_index_groups=chip_groups(parts)
    )


def local(
    block_input,
    lengths,
    cotangent,
    attn_gain,
    w_qa,
    q_gain,
    w_qb,
    w_k,
    k_gain,
    w_v,
    w_o,
    mlp_gain,
    w_gate,
    w_up,
    w_down,
):
    tok_rows = block_input.shape[1]
    parts = lax.axis_size("seq")
    groups = lax.axis_size("dp")
    me = lax.axis_index("seq")
    heads = H // parts
    group_tokens = tok_rows * parts
    first_row = me * tok_rows
    segment, places, offsets = layout(lengths[0], group_tokens)
    cos_all, sin_all = rope_tables(offsets, E)
    cosine = lax.dynamic_slice_in_dim(cos_all, first_row, tok_rows, 0)
    sine_tab = lax.dynamic_slice_in_dim(sin_all, first_row, tok_rows, 0)
    score_scale = 1.0 / math.sqrt(E)
    flat_rows = block_input.reshape(tok_rows, D)
    out_grad = cotangent.reshape(tok_rows, D)
    rank = w_qa.shape[1]
    inner = rank + 2 * E
    width = D // parts

    own_gains = [attn_gain, q_gain, k_gain, mlp_gain]
    spans = [g.shape[0] for g in own_gains]
    gain_block = jnp.concatenate(
        [jnp.pad(g, (0, 128 - g.shape[0]))[None] for g in own_gains]
        + [jnp.zeros((4, 128), jnp.float32)],
        axis=0,
    )
    gain_block = lax.reduce_precision(gain_block, 8, 7)
    inverse_one = lax.rsqrt(jnp.mean(flat_rows * flat_rows, axis=-1, keepdims=True) + eps_norm)
    scaled_cols = jnp.transpose(
        (flat_rows * inverse_one).reshape(tok_rows, parts, width), (1, 0, 2)
    )
    w_in = jnp.concatenate([w_qa, w_k, w_v], axis=1).astype(jnp.bfloat16)
    (gains, gains_line), (scaled_cols,), (in_rows,), (qb_cols,), o_low = launch(
        "start",
        0,
        [
            gather_both(gain_block),
            swap(scaled_cols, "seq"),
            swap(w_in, "dp", repeat=True),
            swap(columns(w_qb, parts), "seq"),
        ],
        passes=[w_o.astype(jnp.bfloat16)],
    )
    gain_one = gains[:, :, 0, : spans[0]].reshape(1, -1)
    gain_latent = gains[:, :, 1, : spans[1]].reshape(1, -1)
    gain_key = gains[:, :, 2, : spans[2]].reshape(1, -1)
    gain_two = gains[:, :, 3, : spans[3]].reshape(1, -1)
    gain_mine = gains_line[:, 0, : spans[0]].reshape(1, -1)

    o_rows = lax.all_gather(o_low, "dp", axis=0, tiled=True)
    qb_cols = join(qb_cols)

    in_rows = in_rows.reshape(width, inner)
    normed = (scaled_cols.reshape(group_tokens, width) * gain_mine).astype(jnp.bfloat16)
    partial = dot(normed, in_rows).astype(jnp.bfloat16).reshape(parts, tok_rows, inner)

    def latent_rows(total, row, vec):
        latent, key, value = total[:, :rank], total[:, rank : rank + E], total[:, rank + E :]
        low = jnp.concatenate(
            [rms_scale(latent, vec[0]), rotate(rms_scale(key, vec[1]), row[0], row[1]), value],
            axis=1,
        )
        return low, [total], None

    chips = parts // 2
    both_cols = fold(list(lax.optimization_barrier((w_gate, w_up))), chips, groups)
    (gathered, inner_own), (down_rows,) = launch(
        "latent",
        1,
        [
            exchange(
                partial,
                [cosine, sine_tab],
                [gain_latent, gain_key],
                latent_rows,
                [inner],
                inner,
                0,
            ),
            gather_chips(w_down.astype(jnp.bfloat16)),
        ],
        turns=[0, 0, 1, 0, 0, 0, 0, 1, 0, 0, 0],
    )
    gathered = gathered.reshape(group_tokens, inner)
    seg_col = segment[:, None]
    seg_rows = jnp.stack(
        [
            lax.slice_in_dim(segment, start, start + group_tokens // 2 + QUERIES)
            for start in [
                min(max(0, first - group_tokens // 2), group_tokens // 2 - QUERIES)
                for first in range(0, group_tokens, QUERIES)
            ]
        ]
    )[:, None, :]
    def mixed_function(total, row, vec):
        mixed = row[0] + total
        return rms_scale(mixed, vec[0]), [mixed], None

    down_rows = down_rows.reshape(-1, D)
    piece, wide = both_cols.shape[1:]
    attend_task = attend(
        gathered, qb_cols, o_rows, cos_all, sin_all, seg_col, seg_rows, parts
    )
    mixed_task = exchange(
        jax.ShapeDtypeStruct((parts, tok_rows, D), jnp.bfloat16),
        [flat_rows],
        [gain_two],
        mixed_function,
        [D],
        D,
        0,
        spread_axis="dp",
    )
    (_, q_rot, attended_low, two_all, mixed_rows), (grad_all,), (_, both_cols) = launch(
        "mixed",
        3,
        [
            chain(attend_task, mixed_task, {0: 0}),
            gather(out_grad.astype(jnp.bfloat16), "dp"),
            chain(swap(both_cols, "line"), gather_chips(both_cols), {0: 0}),
        ],
        turns=[2, 0, 0, 0, 0, 2, 1, 0, 1, 0, 2, 1, 0],
    )
    both_cols = both_cols.reshape(chips, groups, 2, piece, wide)
    both_cols = jnp.transpose(both_cols, (0, 2, 1, 3, 4)).reshape(D, wide)
    ((mixed_grad, mixed_low, gain_two_grad, out_part, down_low, both_low),) = launch(
        "feed_forward",
        9,
        [
            feed_forward(
                two_all, grad_all, both_cols, down_rows, mixed_rows, out_grad, gain_two
            )
        ],
    )
    both_shard = chip_scatter(both_low.reshape(D, wide), parts).reshape(2 * groups, piece, wide)

    def out_function(total, row, vec):
        return None, [row[0] + total], None

    mixed_task = gather(mixed_low, "chip", VMEM)
    back_task = attend_back(
        gathered,
        q_rot,
        jax.ShapeDtypeStruct((parts, tok_rows, D), jnp.bfloat16),
        o_rows,
        qb_cols,
        cos_all,
        sin_all,
        seg_col,
        seg_rows,
    )
    (output_rows,), (mixed_all, query_grad, partial) = launch(
        "attend_back",
        4,
        [
            exchange(out_part, [mixed_rows], [], out_function, [D], 0, 0, sum_axis="dp"),
            chain(mixed_task, back_task, {2: 0}),
        ],
        turns=[1, 0, 0, 1, 1, 1, 1, 1],
    )
    mixed_all = tie(mixed_all, [both_shard]).reshape(group_tokens, D)
    o_shard, o_low = scatter_rows(
        jnp.einsum("tf,td->fd", attended_low, mixed_all, preferred_element_type=jnp.float32)
    )
    qb_shard, qb_low = scatter_columns(
        jnp.einsum("tr,tf->rf", gathered[:, :rank], query_grad, preferred_element_type=jnp.float32),
        parts,
        groups,
    )

    def inner_function(total, row, vec):
        latent_grad, latent_gain = back_rows(row[0][:, :rank], vec[0], total[:, :rank])
        key_back = rotate_back(total[:, rank : rank + E], row[1], row[2])
        key_grad, key_gain = back_rows(row[0][:, rank : rank + E], vec[1], key_back)
        low = jnp.concatenate([latent_grad, key_grad, total[:, rank + E :]], axis=1)
        return low, [], jnp.concatenate([latent_gain, key_gain], axis=1)

    (in_grad, inner_gain_grad), (both_shard,) = launch(
        "inner_grad",
        5,
        [
            exchange(
                partial.reshape(parts, tok_rows, inner),
                [inner_own, cosine, sine_tab],
                [gain_latent, gain_key],
                inner_function,
                [],
                inner,
                rank + E,
            ),
            swap(both_shard, "line"),
        ],
        turns=[1, 0, 0, 0, 0, 0, 0, 0, 0, 0],
        needs=[o_low, qb_low],
    )
    in_grad = in_grad.reshape(group_tokens, inner)
    in_low = jnp.einsum("td,tr->dr", normed, in_grad, preferred_element_type=jnp.float32)
    in_low = in_low.astype(jnp.bfloat16).reshape(groups, -1, inner)
    normed_part = jnp.einsum("tr,dr->td", in_grad, in_rows, preferred_element_type=jnp.float32)
    normed_part = normed_part.astype(jnp.bfloat16).reshape(parts, tok_rows, width)

    (normed_grad,), (in_shard,), (down_shard,) = launch(
        "normed_grad",
        6,
        [
            swap(normed_part, "seq"),
            swap(in_low, "dp"),
            chip_sum(down_low.reshape(chips, -1, D)),
        ],
        turns=[0, 1, 2, 2],
    )
    in_shard = jnp.sum(in_shard.astype(jnp.float32), axis=0)
    normed_grad = jnp.transpose(normed_grad.astype(jnp.float32), (1, 0, 2)).reshape(tok_rows, D)
    input_part, gain_one_grad = back_rows(flat_rows, gain_one, normed_grad)
    input_grad = mixed_grad + input_part

    gain_grads = [
        jnp.sum(gain_one_grad, axis=0),
        jnp.sum(inner_gain_grad[:, :rank], axis=0),
        jnp.sum(inner_gain_grad[:, rank:], axis=0),
        jnp.sum(gain_two_grad, axis=0),
    ]
    gain_grads = jnp.stack(
        [
            jnp.pad(g.reshape(parts, groups, n), ((0, 0), (0, 0), (0, 128 - n)))
            for g, n in zip(gain_grads, spans, strict=True)
        ]
        + [jnp.zeros((parts, groups, 128), jnp.float32)] * 4,
        axis=2,
    )
    (gain_own,), (qb_shard,) = launch("end", 7, [sum_both(gain_grads), swap(qb_shard, "seq")])
    gate_grad, up_grad = unfold_pair(both_shard, chips, groups)
    return (
        output_rows.reshape(1, tok_rows, D),
        input_grad.reshape(1, tok_rows, D),
        gain_own[0, : spans[0]],
        in_shard[:, :rank],
        gain_own[1, : spans[1]],
        unfold(qb_shard),
        in_shard[:, rank : rank + E],
        gain_own[2, : spans[2]],
        in_shard[:, rank + E :],
        o_shard.astype(jnp.float32),
        gain_own[3, : spans[3]],
        gate_grad,
        up_grad,
        down_shard.astype(jnp.float32),
    )


def solution(mesh):
    return jax.shard_map(
        local,
        mesh=mesh,
        in_specs=(
            P("dp", "seq", None),
            P("dp", None),
            P("dp", "seq", None),
            P(("seq", "dp")),
            P(("seq", "dp"), None),
            P(("seq", "dp")),
            P(("seq", "dp"), None),
            P(("seq", "dp"), None),
            P(("seq", "dp")),
            P(("seq", "dp"), None),
            P(("seq", "dp"), None),
            P(("seq", "dp")),
            P(("seq", "dp"), None),
            P(("seq", "dp"), None),
            P(("seq", "dp"), None),
        ),
        out_specs=(
            P("dp", "seq", None),
            P("dp", "seq", None),
            P(("seq", "dp")),
            P(("seq", "dp"), None),
            P(("seq", "dp")),
            P(("seq", "dp"), None),
            P(("seq", "dp"), None),
            P(("seq", "dp")),
            P(("seq", "dp"), None),
            P(("seq", "dp"), None),
            P(("seq", "dp")),
            P(("seq", "dp"), None),
            P(("seq", "dp"), None),
            P(("seq", "dp"), None),
        ),
        check_vma=False,
    )
```

```python
import math

import jax
import jax.numpy as jnp
from jax import lax
from jax.experimental import pallas as pl
from jax.experimental.pallas import tpu as pltpu
from jax.sharding import PartitionSpec as P

D = 2048
H = 16
E = 256


MESH = pl.DeviceIdType.MESH
STEP = 16
QUERIES = 256
VMEM_LIMIT = 60 * 1024 * 1024
COST = pl.CostEstimate(flops=0, transcendentals=0, bytes_accessed=1024)

eps_norm = 1e-06
big_negative = -1e30


def rms_scale(values, gain_vec):
    inverse = lax.rsqrt(jnp.mean(values * values, axis=-1, keepdims=True) + eps_norm)
    return values * inverse * gain_vec


def norm_back(values, gain_vec, upstream):
    inverse = lax.rsqrt(jnp.mean(values * values, axis=-1, keepdims=True) + eps_norm)
    gain_grad = jnp.sum(upstream * values * inverse, axis=0)
    scaled = upstream * gain_vec
    value_grad = inverse * scaled - values * (inverse * inverse * inverse) * jnp.mean(
        scaled * values, axis=-1, keepdims=True
    )
    return (value_grad, gain_grad)


def rotate(values, cosine, sine_tab):
    half_width = values.shape[-1] // 2
    turned = jnp.concatenate([-values[..., half_width:], values[..., :half_width]], axis=-1)
    return values * cosine + turned * sine_tab


def rotate_back(upstream, cosine, sine_tab):
    half_width = upstream.shape[-1] // 2
    weighted = upstream * sine_tab
    turned = jnp.concatenate([weighted[..., half_width:], -weighted[..., :half_width]], axis=-1)
    return upstream * cosine + turned


def layout(seq_lengths, group_tokens):
    seq_ends = jnp.cumsum(seq_lengths)
    places = jnp.arange(group_tokens, dtype=jnp.int32)
    passed = places[:, None] >= seq_ends[None, :]
    segment = jnp.sum(passed.astype(jnp.int32), axis=1)
    starts = jnp.sum(jnp.where(passed, seq_lengths[None, :], 0), axis=1)
    return (segment, places, places - starts)


def rope_tables(offsets, width):
    half_width = width // 2
    frequency = jnp.exp(
        jnp.arange(half_width, dtype=jnp.float32) * (-2.0 * math.log(10000.0) / width)
    )
    angles = offsets.astype(jnp.float32)[:, None] * frequency[None, :]
    angles = jnp.concatenate([angles, angles], axis=-1)
    return (jnp.cos(angles), jnp.sin(angles))


VMEM = pl.BlockSpec(memory_space=pltpu.VMEM)
ANY = pl.BlockSpec(memory_space=pl.ANY)
SIBLING = (1, 0)


def flip(index, bits):
    out, power = index, 1
    while power <= bits:
        if bits & power:
            out = out + power - 2 * power * ((index // power) % 2)
        power *= 2
    return out


def here():
    return lax.axis_index("seq"), lax.axis_index("dp")


def device(mask):
    me, group = here()
    return flip(me, mask[0]), flip(group, mask[1])


def copy_to(source, target, sems, seq_to, dp_to):
    return pltpu.make_async_remote_copy(
        src_ref=source,
        dst_ref=target,
        send_sem=sems.at[0],
        recv_sem=sems.at[1],
        device_id=(seq_to, dp_to),
        device_id_type=MESH,
    )


def remote(source, target, sems, mask):
    copy = copy_to(source, target, sems, *device(mask))
    copy.start()
    return copy


def keep(source, target, sem):
    copy = pltpu.make_async_copy(source, target, sem)
    copy.start()
    return copy


class Task:
    def __init__(self, inputs, outputs, scratch, masks, run):
        self.inputs, self.outputs, self.scratch = inputs, outputs, scratch
        self.masks, self.run = masks, run


def launch(name, collective_id, tasks, needs=(), passes=(), turns=()):
    masks = sorted({mask for task in tasks for mask in task.masks})
    n_in = sum(len(task.inputs) for task in tasks)
    n_out = sum(len(task.outputs) for task in tasks)

    def body(*refs):
        refs = list(refs)
        ins = refs[:n_in]
        refs = refs[n_in + len(needs) + len(passes) :]
        outs, scratch = refs[:n_out], refs[n_out + len(passes) :]
        if masks:
            barrier = pltpu.get_barrier_semaphore()
            for mask in masks:
                pl.semaphore_signal(barrier, inc=1, device_id=device(mask), device_id_type=MESH)
            pl.semaphore_wait(barrier, len(masks))
        running = []
        for task in tasks:
            a, b, c = len(task.inputs), len(task.outputs), len(task.scratch)
            running.append(task.run(ins[:a], outs[:b], scratch[:c]))
            ins, outs, scratch = ins[a:], outs[b:], scratch[c:]
        for turn in turns:
            next(running[turn], None)
        while running:
            for step in list(running):
                if next(step, "done") == "done":
                    running.remove(step)

    inputs = [pair for task in tasks for pair in task.inputs]
    outputs = [pair for task in tasks for pair in task.outputs]
    results = pl.pallas_call(
        body,
        name=name,
        out_shape=[shape for shape, _ in outputs]
        + [jax.ShapeDtypeStruct(a.shape, a.dtype) for a in passes],
        in_specs=[spec for _, spec in inputs] + [ANY] * (len(needs) + len(passes)),
        out_specs=[spec for _, spec in outputs] + [ANY] * len(passes),
        input_output_aliases={n_in + len(needs) + i: n_out + i for i in range(len(passes))},
        scratch_shapes=[shape for task in tasks for shape in task.scratch],
        compiler_params=pltpu.CompilerParams(
            collective_id=collective_id if masks else None,
            has_side_effects=bool(masks),
            vmem_limit_bytes=VMEM_LIMIT,
        ),
        cost_estimate=COST,
    )(*[array for array, _ in inputs], *needs, *passes)
    results, split = list(results), []
    for task in tasks:
        split.append(results[: len(task.outputs)])
        results = results[len(task.outputs) :]
    return split + results


def chain(first, second, links):
    inputs = [pair for i, pair in enumerate(second.inputs) if i not in links]
    a, b, c = len(first.inputs), len(first.outputs), len(first.scratch)

    def run(ins, outs, scratch):
        yield from first.run(ins[:a], outs[:b], scratch[:c])
        rest = list(ins[a:])
        joined = [outs[links[i]] if i in links else rest.pop(0) for i in range(len(second.inputs))]
        yield from second.run(joined, outs[b:], scratch[c:])

    return Task(
        first.inputs + inputs,
        first.outputs + second.outputs,
        first.scratch + second.scratch,
        first.masks + second.masks,
        run,
    )


def paused(task, pauses):
    def run(ins, outs, scratch):
        for _ in range(pauses):
            yield
        yield from task.run(ins, outs, scratch)

    return Task(task.inputs, task.outputs, task.scratch, task.masks, run)


def rows_loop(start, stop, step):
    def one(i, carry):
        step(pl.ds(pl.multiple_of(i * STEP, STEP), STEP))
        return carry

    lax.fori_loop(start // STEP, stop // STEP, one, 0)


def axis_masks(axis):
    if axis == "chip":
        return [(2 * j, 0) for j in range(1, lax.axis_size("seq") // 2)]
    return [(0, j) for j in range(1, lax.axis_size("dp"))]


def axis_block(axis, mask=(0, 0)):
    seq_at, dp_at = device(mask)
    return seq_at if axis == "chip" else dp_at * 2 + seq_at % 2


def line_masks():
    masks, power = [], 2
    while power <= lax.axis_size("dp"):
        masks.append((0, power - 1))
        power *= 2
    return masks


def spread_masks(axis):
    if axis == "dp":
        return [SIBLING] + line_masks()
    return [SIBLING] + axis_masks(axis)


def spread(axis, low, all_ref, keep_sem, sems):
    own = all_ref.at[axis_block(axis)]
    rows = low.shape[0]
    sends = []
    if axis == "dp":
        yield from spread_line(low, all_ref, keep_sem, sems)
        return
    masks = axis_masks(axis)
    square = len(masks) == 3
    direct = [(2, 0), (4, 0)] if square else masks
    for i, mask in enumerate(direct):
        sends.append(remote(low, own, sems.at[i], mask))
    beside = [remote(low, own, sems.at[len(masks)], SIBLING)]
    kept = keep(low, own, keep_sem)
    yield
    at, halves = len(masks) + 1, []

    def block(mask):
        return all_ref.at[axis_block(axis, mask)]

    def half(mask, which):
        return all_ref.at[axis_block(axis, mask), pl.ds(which * (rows // 2), rows // 2)]

    for i, mask in enumerate(direct):
        sends[i].wait_recv()
        if square:
            halves.append(remote(half(mask, i), half(mask, i), sems.at[at], direct[1 - i]))
            at += 1
        beside.append(remote(block(mask), block(mask), sems.at[at], SIBLING))
        at += 1
        yield
    for i, copy in enumerate(halves):
        copy.wait_recv()
        part = half((6, 0), i)
        beside.append(remote(part, part, sems.at[at], SIBLING))
        at += 1
        yield
    for copy in beside:
        copy.wait_recv()
    for copy in sends + halves + beside:
        copy.wait_send()
    kept.wait()


def spread_line(low, all_ref, keep_sem, sems):
    me, group = here()
    core, groups = me % 2, lax.axis_size("dp")
    own = all_ref.at[axis_block("dp")]
    kept = keep(low, own, keep_sem)
    beside = remote(low, own, sems.at[0], SIBLING)

    def at(way, k, kind):
        return sems.at[1 + (way * (groups - 1) + k) * 2 + kind]

    def hop(way, k):
        step = 1 - 2 * way
        block = all_ref.at[(group - step * k) * 2 + core]
        return copy_to(low if k == 0 else block, block, at(way, k, 0), me, group + step)

    def landed(way, k):
        block = all_ref.at[(group - (1 - 2 * way) * (k + 1)) * 2 + core]
        return copy_to(block, block, at(way, k, 0), *device(SIBLING))

    def aside(way, k):
        block = all_ref.at[(group - (1 - 2 * way) * (k + 1)) * 2 + core]
        return copy_to(block, block, at(way, k, 1), *device(SIBLING))

    def sends(way, k):
        if way == 0:
            return (group >= k) & (group < groups - 1)
        return (group + k < groups) & (group > 0)

    def lands(way, k):
        return (group >= k + 1) if way == 0 else (group + k + 1 < groups)

    for k in range(groups - 1):
        for way in range(2):

            @pl.when(sends(way, k))
            def _(way=way, k=k):
                hop(way, k).start()

        yield
        for way in range(2):

            @pl.when(lands(way, k))
            def _(way=way, k=k):
                landed(way, k).wait_recv()
                aside(way, k).start()

    yield
    beside.wait_recv()
    for k in range(groups - 1):
        for way in range(2):

            @pl.when(lands(way, k))
            def _(way=way, k=k):
                aside(way, k).wait()

            @pl.when(sends(way, k))
            def _(way=way, k=k):
                hop(way, k).wait_send()

    beside.wait_send()
    kept.wait()


def exchange(
    partial,
    row_operands,
    vec_operands,
    row_function,
    own_widths,
    low_width,
    vec_width,
    sum_axis="chip",
    spread_axis="chip",
    all_space=ANY,
):
    blocks, rows, cols = partial.shape
    far = blocks // 2
    n_rows = len(row_operands)
    masks = axis_masks(sum_axis)
    square = sum_axis == "chip" and len(masks) == 3
    out_blocks = lax.axis_size("seq") if spread_axis == "chip" else 2 * lax.axis_size("dp")
    order = list(range(far - 1, 0, -1)) + [0]
    at_mask = [(0, 0)] + masks

    def run(ins, outs, scratch):
        ins, outs = list(ins), list(outs)
        partial_ref = ins.pop(0)
        row_refs, vec_refs = ins[:n_rows], ins[n_rows:]
        all_ref = outs.pop(0) if low_width else None
        vec_out = outs.pop(-1) if vec_width else None
        mine, beside, arrived, low, local_sem, sems, out_sems = scratch

        across, loads = {}, {}
        for j in order:
            block = axis_block(sum_axis, at_mask[j])
            other = axis_block(sum_axis, (at_mask[j][0] + 1, at_mask[j][1]))
            across[j] = remote(partial_ref.at[other], beside.at[j], sems.at[j], SIBLING)
            loads[j] = keep(partial_ref.at[block], mine.at[j], local_sem.at[j])
        yield
        sent = []

        def settle(j, low_row=0, high_row=rows, more=None):
            def add(at):
                total = mine[j, at, :].astype(jnp.float32) + beside[j, at, :].astype(jnp.float32)
                if more is not None:
                    total = total + arrived[more, at, :].astype(jnp.float32)
                mine[j, at, :] = total.astype(jnp.bfloat16)

            rows_loop(low_row, high_row, add)

        if square:
            middle = rows // 2
            first, second = pl.ds(0, middle), pl.ds(middle, middle)
            for j in (3, 1, 2):
                loads[j].wait()
                across[j].wait_recv()
                if j == 3:
                    settle(3)
                elif j == 1:
                    settle(1, 0, middle)
                else:
                    settle(2, middle, rows)
                base = far + 2 * (j - 1)
                if j in (3, 1):
                    sent.append(
                        remote(mine.at[j, first], arrived.at[j, first], sems.at[base], (2, 0))
                    )
                if j in (3, 2):
                    sent.append(
                        remote(mine.at[j, second], arrived.at[j, second], sems.at[base + 1], (4, 0))
                    )
            yield
            diagonal_x, diagonal_y = sent[0], sent[1]
            diagonal_x.wait_recv()
            settle(2, 0, middle, more=3)
            sent.append(
                remote(mine.at[2, first], arrived.at[2, first], sems.at[far + 2], (4, 0))
            )
            diagonal_y.wait_recv()
            settle(1, middle, rows, more=3)
            sent.append(
                remote(mine.at[1, second], arrived.at[1, second], sems.at[far + 1], (2, 0))
            )
            yield
            adds = [1, 2]
            landed = sent[2:]
        else:
            for j in order[:-1]:
                loads[j].wait()
                across[j].wait_recv()
                settle(j)
                sent.append(remote(mine.at[j], arrived.at[j], sems.at[far + j], at_mask[j]))
            yield
            adds = order[:-1]
            landed = sent
        loads[0].wait()
        across[0].wait_recv()
        for copy in landed:
            copy.wait_recv()
        if vec_width:
            vec_out[...] = jnp.zeros_like(vec_out)
        vecs = [v[...] for v in vec_refs]

        def finish(at):
            total = mine[0, at, :].astype(jnp.float32) + beside[0, at, :].astype(jnp.float32)
            for j in adds:
                total = total + arrived[j, at, :].astype(jnp.float32)
            low_now, own_now, vec_now = row_function(total, [r[at, :] for r in row_refs], vecs)
            if low_width:
                low[at, :] = low_now.astype(jnp.bfloat16)
            for ref, value in zip(outs, own_now, strict=True):
                ref[at, :] = value
            if vec_width:
                vec_out[...] += vec_now

        rows_loop(0, rows, finish)
        if low_width:
            yield from spread(spread_axis, low, all_ref, local_sem.at[0], out_sems)
        for copy in list(across.values()) + sent:
            copy.wait_send()

    outputs = []
    if low_width:
        shape = jax.ShapeDtypeStruct((out_blocks, rows, low_width), jnp.bfloat16)
        outputs.append((shape, all_space))
    outputs += [(jax.ShapeDtypeStruct((rows, width), jnp.float32), VMEM) for width in own_widths]
    if vec_width:
        outputs.append((jax.ShapeDtypeStruct((STEP, vec_width), jnp.float32), VMEM))
    return Task(
        [(partial, ANY)] + [(a, VMEM) for a in list(row_operands) + list(vec_operands)],
        outputs,
        [
            pltpu.VMEM((far, rows, cols), jnp.bfloat16),
            pltpu.VMEM((far, rows, cols), jnp.bfloat16),
            pltpu.VMEM((far, rows, cols), jnp.bfloat16),
            pltpu.VMEM((rows, max(low_width, 128)), jnp.bfloat16),
            pltpu.SemaphoreType.DMA((far,)),
            pltpu.SemaphoreType.DMA((far + max(6, far), 2)),
            pltpu.SemaphoreType.DMA((spread_sems(spread_axis), 2)),
        ],
        [SIBLING] + masks + (spread_masks(spread_axis) if low_width else []),
        run,
    )


def spread_sems(axis):
    if axis == "dp":
        return 1 + 4 * (lax.axis_size("dp") - 1)
    return 2 * lax.axis_size("seq")


def gather(low, axis, all_space=ANY):
    rows, cols = low.shape
    blocks = lax.axis_size("seq") if axis == "chip" else 2 * lax.axis_size("dp")

    def run(ins, outs, scratch):
        yield from spread(axis, ins[0], outs[0], scratch[0].at[0], scratch[1])

    return Task(
        [(low, ANY)],
        [(jax.ShapeDtypeStruct((blocks, rows, cols), low.dtype), all_space)],
        [pltpu.SemaphoreType.DMA((1,)), pltpu.SemaphoreType.DMA((spread_sems(axis), 2))],
        spread_masks(axis),
        run,
    )


def family(kind):
    parts, groups = lax.axis_size("seq"), lax.axis_size("dp")
    if kind == "seq":
        return [(m, 0) for m in range(1, parts)], lambda s, d: s
    if kind == "dp":
        return [(0, m) for m in range(1, groups)], lambda s, d: d
    return [(m % 2, m // 2) for m in range(1, 2 * groups)], lambda s, d: s % 2 * groups + d


def swap(array, kind, repeat=False):
    masks, index = family(kind)

    def run(ins, outs, scratch):
        own = index(*here())
        copies = [keep(ins[0] if repeat else ins[0].at[own], outs[0].at[own], scratch[0].at[0])]
        for i, mask in enumerate(masks):
            source = ins[0] if repeat else ins[0].at[index(*device(mask))]
            copies.append(remote(source, outs[0].at[own], scratch[1].at[i], mask))
        yield
        for copy in copies:
            copy.wait()

    shape = (len(masks) + 1,) + array.shape if repeat else array.shape
    return Task(
        [(array, ANY)],
        [(jax.ShapeDtypeStruct(shape, array.dtype), ANY)],
        [pltpu.SemaphoreType.DMA((1,)), pltpu.SemaphoreType.DMA((len(masks), 2))],
        masks,
        run,
    )


def gather_both(array):
    seq_masks, dp_masks = family("seq")[0], family("dp")[0]
    parts, groups = lax.axis_size("seq"), lax.axis_size("dp")

    def run(ins, outs, scratch):
        me, group = here()
        (small,), (everything, line) = ins, outs
        copies = [keep(small, line.at[group], scratch[0].at[0])]
        for i, mask in enumerate(dp_masks):
            copies.append(remote(small, line.at[group], scratch[1].at[i], mask))
        yield
        for copy in copies:
            copy.wait()
        copies = [keep(line, everything.at[me], scratch[0].at[1])]
        for i, mask in enumerate(seq_masks):
            at = scratch[1].at[len(dp_masks) + i]
            copies.append(remote(line, everything.at[me], at, mask))
        yield
        for copy in copies:
            copy.wait()

    return Task(
        [(array, VMEM)],
        [
            (jax.ShapeDtypeStruct((parts, groups) + array.shape, array.dtype), VMEM),
            (jax.ShapeDtypeStruct((groups,) + array.shape, array.dtype), VMEM),
        ],
        [
            pltpu.SemaphoreType.DMA((2,)),
            pltpu.SemaphoreType.DMA((len(seq_masks) + len(dp_masks), 2)),
        ],
        seq_masks + dp_masks,
        run,
    )


def sum_both(array):
    seq_masks, dp_masks = family("seq")[0], family("dp")[0]

    def run(ins, outs, scratch):
        me, group = here()
        stage_one, line, stage_two, local_sem, sems = scratch
        copies = [keep(ins[0].at[me], stage_one.at[me], local_sem.at[0])]
        for i, mask in enumerate(seq_masks):
            source = ins[0].at[flip(me, mask[0])]
            copies.append(remote(source, stage_one.at[me], sems.at[i], mask))
        yield
        for copy in copies:
            copy.wait()
        line[...] = jnp.sum(stage_one[...], axis=0)
        copies = [keep(line.at[group], stage_two.at[group], local_sem.at[1])]
        for i, mask in enumerate(dp_masks):
            at = sems.at[len(seq_masks) + i]
            copies.append(remote(line.at[flip(group, mask[1])], stage_two.at[group], at, mask))
        yield
        for copy in copies:
            copy.wait()
        outs[0][...] = jnp.sum(stage_two[...], axis=0)

    return Task(
        [(array, VMEM)],
        [(jax.ShapeDtypeStruct(array.shape[2:], array.dtype), VMEM)],
        [
            pltpu.VMEM(array.shape, array.dtype),
            pltpu.VMEM(array.shape[1:], array.dtype),
            pltpu.VMEM(array.shape[1:], array.dtype),
            pltpu.SemaphoreType.DMA((2,)),
            pltpu.SemaphoreType.DMA((len(seq_masks) + len(dp_masks), 2)),
        ],
        seq_masks + dp_masks,
        run,
    )


def tie(value, needs):
    def body(*refs):
        pass

    return pl.pallas_call(
        body,
        name="tie",
        out_shape=jax.ShapeDtypeStruct(value.shape, value.dtype),
        in_specs=[ANY] * (1 + len(needs)),
        out_specs=ANY,
        input_output_aliases={0: 0},
        cost_estimate=COST,
    )(value, *needs)


def gather_chips(low):
    rows = low.shape[0]
    middle = rows // 2 // STEP * STEP if len(low.shape) == 2 else rows // 2
    masks = axis_masks("chip")
    square = len(masks) == 3

    def run(ins, outs, scratch):
        me, _ = here()
        low_ref, all_ref, (local_sem, sems) = ins[0], outs[0], scratch

        def block(mask):
            return all_ref.at[device(mask)[0] // 2]

        def half(mask, which):
            part = pl.ds(middle, rows - middle) if which else pl.ds(0, middle)
            return all_ref.at[device(mask)[0] // 2, part]

        kept = keep(low_ref, block((0, 0)), local_sem.at[0])
        direct = [(2, 0), (4, 0)] if square else masks
        copies = [
            remote(low_ref, block((0, 0)), sems.at[i], mask) for i, mask in enumerate(direct)
        ]
        yield
        if square:
            for i, mask in enumerate(direct):
                copies[i].wait_recv()
                part = half(mask, i)
                copies.append(remote(part, part, sems.at[2 + i], direct[1 - i]))
            yield
            copies[0].wait_send()
            copies[1].wait_send()
            copies = copies[2:]
        for copy in copies:
            copy.wait()
        kept.wait()

    return Task(
        [(low, ANY)],
        [(jax.ShapeDtypeStruct((len(masks) + 1,) + low.shape, low.dtype), ANY)],
        [pltpu.SemaphoreType.DMA((1,)), pltpu.SemaphoreType.DMA((max(4, len(masks)), 2))],
        masks,
        run,
    )


def lanes_of(sources, segments, tile, rows):
    lane = lax.broadcasted_iota(jnp.int32, (rows, 128), 1)
    out = jnp.zeros((rows, 128), jnp.float32)
    low = tile * 128
    for source, from_col, to_col, length in segments:
        first, last = max(low, to_col), min(low + 128, to_col + length)
        if first >= last:
            continue
        begin = from_col + first - to_col
        window = begin // 128 * 128
        wide = 128 if begin - window + last - first <= 128 else 256
        held = min(wide, sources[source].shape[1] - window)
        wide = pl.cdiv(held, 128) * 128
        piece = sources[source][:, window : window + held].astype(jnp.float32)
        if held < wide:
            blank = jnp.zeros((rows, wide - held), jnp.float32)
            piece = jnp.concatenate([piece, blank], axis=1)
        shift = (first - low - (begin - window)) % wide
        if shift:
            piece = pltpu.roll(piece, shift, axis=1)
        out = jnp.where((lane >= first - low) & (lane < last - low), piece[:, :128], out)
    return out


def fold(weights, chips, groups):
    rows, cols = weights[0].shape
    units = cols // (2 * chips * groups)
    width = 2 * chips * units

    def body(first_ref, second_ref, out_ref):
        sources = [first_ref, second_ref]
        for group in range(groups):
            for core in range(2):
                segments = [
                    (
                        which,
                        ((chip * 2 + core) * groups + group) * units,
                        (which * chips + chip) * units,
                        units,
                    )
                    for which in range(2)
                    for chip in range(chips)
                ]
                for tile in range(pl.cdiv(width, 128)):
                    value = lanes_of(sources, segments, tile, rows).astype(jnp.bfloat16)
                    stop = min(width, tile * 128 + 128)
                    out_ref[core * groups + group, :, tile * 128 : stop] = value[:, : stop - tile * 128]

    return pl.pallas_call(
        body,
        name="fold",
        out_shape=jax.ShapeDtypeStruct((2 * groups, rows, width), jnp.bfloat16),
        in_specs=[VMEM, VMEM],
        out_specs=VMEM,
        compiler_params=pltpu.CompilerParams(vmem_limit_bytes=VMEM_LIMIT),
        cost_estimate=COST,
    )(*weights)


def unfold_pair(pieces, chips, groups):
    _, rows, width = pieces.shape
    units = width // (2 * chips)
    cols = units * 2 * chips * groups

    def body(in_ref, first_ref, second_ref):
        sources = [in_ref.at[i] for i in range(2 * groups)]
        for which, out_ref in enumerate([first_ref, second_ref]):
            segments = [
                (
                    core * groups + group,
                    (which * chips + chip) * units,
                    ((chip * 2 + core) * groups + group) * units,
                    units,
                )
                for chip in range(chips)
                for core in range(2)
                for group in range(groups)
            ]
            for tile in range(cols // 128):
                out_ref[:, tile * 128 : tile * 128 + 128] = lanes_of(sources, segments, tile, rows)

    shape = jax.ShapeDtypeStruct((rows, cols), jnp.float32)
    return pl.pallas_call(
        body,
        name="unfold",
        out_shape=[shape, shape],
        in_specs=[VMEM],
        out_specs=[VMEM, VMEM],
        compiler_params=pltpu.CompilerParams(vmem_limit_bytes=VMEM_LIMIT),
        cost_estimate=COST,
    )(pieces)


def nt(left, right):
    return lax.dot_general(
        left, right, (((1,), (1,)), ((), ())), preferred_element_type=jnp.float32
    )


def tn(left, right):
    return lax.dot_general(
        left, right, (((0,), (0,)), ((), ())), preferred_element_type=jnp.float32
    )


def window_of(i, tokens):
    wide = tokens // 2 + QUERIES
    start = jnp.clip(i * QUERIES - tokens // 2, 0, tokens - wide)
    return pl.multiple_of(start, QUERIES), wide


def probabilities(queries, keys, i, start, seg_col, seg_row):
    scores = nt(queries, keys) * (1.0 / math.sqrt(E))
    row = i * QUERIES + lax.broadcasted_iota(jnp.int32, scores.shape, 0)
    col = start + lax.broadcasted_iota(jnp.int32, scores.shape, 1)
    scores = jnp.where((seg_col == seg_row) & (col <= row), scores, big_negative)
    shifted = jnp.exp(scores - jnp.max(scores, axis=-1, keepdims=True))
    return shifted / jnp.sum(shifted, axis=-1, keepdims=True)


def attend(gathered, qb_cols, o_rows, cosine, sine_tab, seg_col, seg_rows, parts):
    tokens, inner = gathered.shape
    rank, width = qb_cols.shape
    rows, cols = tokens // parts, o_rows.shape[1]
    per = QUERIES // rows

    def run(ins, outs, scratch):
        in_ref, qb_ref, o_ref, cos_ref, sin_ref, seg_ref, segs_ref = ins
        part_ref, q_ref, out_ref = outs

        def block(i, carry):
            at = pl.ds(pl.multiple_of(i * QUERIES, QUERIES), QUERIES)
            start, wide = window_of(i, tokens)
            span = pl.ds(start, wide)
            query = dot(in_ref[at, :rank], qb_ref[...])
            keys, values = in_ref[span, rank : rank + E], in_ref[span, rank + E :]
            for head in range(width // E):
                lanes = slice(head * E, head * E + E)
                rotated = rotate(query[:, lanes], cos_ref[at, :], sin_ref[at, :])
                rotated = rotated.astype(jnp.bfloat16)
                q_ref[at, lanes] = rotated
                probs = probabilities(rotated, keys, i, start, seg_ref[at, :], segs_ref[i])
                out_ref[at, lanes] = dot(probs.astype(jnp.bfloat16), values).astype(jnp.bfloat16)
            part = dot(out_ref[at, :], o_ref[...]).astype(jnp.bfloat16)
            part_ref[pl.ds(i * per, per)] = part.reshape(per, rows, cols)
            return carry

        lax.fori_loop(0, tokens // QUERIES, block, 0)
        yield

    shape = jax.ShapeDtypeStruct((tokens, width), jnp.bfloat16)
    return Task(
        [(a, VMEM) for a in (gathered, qb_cols, o_rows, cosine, sine_tab, seg_col, seg_rows)],
        [
            (jax.ShapeDtypeStruct((parts, rows, cols), jnp.bfloat16), VMEM),
            (shape, VMEM),
            (shape, VMEM),
        ],
        [],
        [],
        run,
    )


def attend_back(
    gathered, queries, out_grad, o_rows, qb_cols, cosine, sine_tab, seg_col, seg_rows
):
    tokens, inner = gathered.shape
    rank, width = qb_cols.shape
    scale = 1.0 / math.sqrt(E)

    def run(ins, outs, scratch):
        in_ref, q_ref, grad_ref, o_ref, qb_ref, cos_ref, sin_ref, seg_ref, segs_ref = ins
        dq_ref, part_ref = outs
        key_sum, value_sum = scratch
        key_sum[...] = jnp.zeros_like(key_sum)
        value_sum[...] = jnp.zeros_like(value_sum)

        def block(i, carry):
            at = pl.ds(pl.multiple_of(i * QUERIES, QUERIES), QUERIES)
            start, wide = window_of(i, tokens)
            span = pl.ds(start, wide)
            per = QUERIES // grad_ref.shape[1]
            upstream = grad_ref[pl.ds(i * per, per)].reshape(QUERIES, grad_ref.shape[2])
            attended_grad = nt(upstream, o_ref[...]).astype(jnp.bfloat16)
            keys, values = in_ref[span, rank : rank + E], in_ref[span, rank + E :]
            for head in range(width // E):
                lanes = slice(head * E, head * E + E)
                query, upstream = q_ref[at, lanes], attended_grad[:, lanes]
                probs = probabilities(query, keys, i, start, seg_ref[at, :], segs_ref[i])
                value_sum[span, :] += tn(probs.astype(jnp.bfloat16), upstream)
                prob_grad = nt(upstream, values)
                delta = jnp.sum(probs * prob_grad, axis=-1, keepdims=True)
                score_grad = (probs * (prob_grad - delta)).astype(jnp.bfloat16)
                key_sum[span, :] += tn(score_grad, query)
                query_grad = dot(score_grad, keys) * scale
                query_grad = rotate_back(query_grad, cos_ref[at, :], sin_ref[at, :])
                dq_ref[at, lanes] = query_grad.astype(jnp.bfloat16)
            part_ref[at, :rank] = nt(dq_ref[at, :], qb_ref[...]).astype(jnp.bfloat16)
            return carry

        lax.fori_loop(0, tokens // QUERIES, block, 0)
        part_ref[:, rank : rank + E] = (key_sum[...] * scale).astype(jnp.bfloat16)
        part_ref[:, rank + E :] = value_sum[...].astype(jnp.bfloat16)
        yield

    return Task(
        [
            (a, VMEM)
            for a in (
                gathered,
                queries,
                out_grad,
                o_rows,
                qb_cols,
                cosine,
                sine_tab,
                seg_col,
                seg_rows,
            )
        ],
        [
            (jax.ShapeDtypeStruct((tokens, width), jnp.bfloat16), VMEM),
            (jax.ShapeDtypeStruct((tokens, inner), jnp.bfloat16), VMEM),
        ],
        [pltpu.VMEM((tokens, E), jnp.float32), pltpu.VMEM((tokens, E), jnp.float32)],
        [],
        run,
    )


def feed_forward(two_all, grad_all, both_cols, down_rows, mixed_rows, out_grad, gain_two):
    line, rows, cols = two_all.shape
    units = down_rows.shape[0]
    far = line // 2
    chips, groups = lax.axis_size("seq") // 2, lax.axis_size("dp")
    masks = axis_masks("dp")
    at_mask = [(0, 0)] + masks
    order = list(range(far - 1, 0, -1)) + [0]
    slab = cols // (2 * chips)
    piece = slab // groups

    def run(ins, outs, scratch):
        two_ref, grad_ref, both_ref, down_ref, mixed_ref, dy_ref, gain_ref = ins
        mixed_out, low_out, vec_out, y_out, down_out, both_out = outs
        mine, give, beside, arrived, hidden, pair_grad, stage, sems, stage_sem = scratch
        core = here()[0] % 2

        def produce(j):
            block = device(at_mask[j])[1] * 2
            both = pl.ds(block, 2)
            x = two_ref[both].reshape(2 * rows, cols)
            dy = grad_ref[both].reshape(2 * rows, cols)
            act = dot(x, both_ref[...])
            gate, up = act[:, :units], act[:, units:]
            sigmoid = jax.nn.sigmoid(gate)
            silu = gate * sigmoid
            hid = (silu * up).astype(jnp.bfloat16)
            hidden[both] = hid.reshape(2, rows, units)
            y_out[both] = dot(hid, down_ref[...]).astype(jnp.bfloat16).reshape(2, rows, cols)
            hid_grad = nt(dy, down_ref[...])
            gate_grad = hid_grad * up * (sigmoid * (1.0 + gate * (1.0 - sigmoid)))
            up_grad = hid_grad * silu
            pair = jnp.concatenate([gate_grad, up_grad], axis=1).astype(jnp.bfloat16)
            pair_grad[both] = pair.reshape(2, rows, 2 * units)
            part = nt(pair, both_ref[...]).astype(jnp.bfloat16)

            @pl.when(core == 0)
            def _():
                mine[j], give[j] = part[:rows], part[rows:]

            @pl.when(core == 1)
            def _():
                mine[j], give[j] = part[rows:], part[:rows]

        across, sent = {}, {}

        def settle(j):
            across[j].wait_recv()

            def add(at):
                total = mine[j, at, :].astype(jnp.float32) + beside[j, at, :].astype(jnp.float32)
                mine[j, at, :] = total.astype(jnp.bfloat16)

            rows_loop(0, rows, add)
            sent[j] = remote(mine.at[j], arrived.at[j], sems.at[far + j], at_mask[j])

        last = None
        for j in order:
            produce(j)
            across[j] = remote(give.at[j], beside.at[j], sems.at[j], SIBLING)
            if last is not None:
                settle(last)
            last = j
        yield

        down_out[...] = tn(
            hidden[...].reshape(line * rows, units), grad_ref[...].reshape(line * rows, cols)
        ).astype(jnp.bfloat16)
        moves = []
        for index in range(2 * chips):
            slot = index % 2
            if index >= 2:
                for move in moves[(index - 2) * groups : (index - 1) * groups]:
                    move.wait()
            x = two_ref[:, :, index * slab : (index + 1) * slab].reshape(line * rows, slab)
            value = tn(x, pair_grad[...].reshape(line * rows, 2 * units))
            stage[slot] = value.astype(jnp.bfloat16).reshape(groups, piece, 2 * units)
            for group in range(groups):
                place = index * groups + group
                moves.append(
                    keep(stage.at[slot, group], both_out.at[place], stage_sem.at[slot, group])
                )
        for move in moves[-2 * groups :]:
            move.wait()

        across[0].wait_recv()
        for j in order[:-1]:
            sent[j].wait_recv()
        vec_out[...] = jnp.zeros_like(vec_out)
        gain = gain_ref[...]

        def finish(at):
            total = mine[0, at, :].astype(jnp.float32) + beside[0, at, :].astype(jnp.float32)
            for j in order[:-1]:
                total = total + arrived[j, at, :].astype(jnp.float32)
            value_grad, gain_grad = back_rows(mixed_ref[at, :], gain, total)
            mixed_grad = dy_ref[at, :] + value_grad
            mixed_out[at, :] = mixed_grad
            low_out[at, :] = mixed_grad.astype(jnp.bfloat16)
            vec_out[...] += gain_grad

        rows_loop(0, rows, finish)
        for copy in list(across.values()) + list(sent.values()):
            copy.wait_send()

    def low(*shape):
        return jax.ShapeDtypeStruct(shape, jnp.bfloat16)

    blocks = pltpu.VMEM((far, rows, cols), jnp.bfloat16)
    return Task(
        [
            (a, VMEM)
            for a in (two_all, grad_all, both_cols, down_rows, mixed_rows, out_grad, gain_two)
        ],
        [
            (jax.ShapeDtypeStruct((rows, cols), jnp.float32), VMEM),
            (low(rows, cols), VMEM),
            (jax.ShapeDtypeStruct((STEP, cols), jnp.float32), VMEM),
            (low(line, rows, cols), VMEM),
            (low(units, cols), VMEM),
            (low(2 * chips * groups, piece, 2 * units), ANY),
        ],
        [
            blocks,
            blocks,
            blocks,
            blocks,
            pltpu.VMEM((line, rows, units), jnp.bfloat16),
            pltpu.VMEM((line, rows, 2 * units), jnp.bfloat16),
            pltpu.VMEM((2, groups, piece, 2 * units), jnp.bfloat16),
            pltpu.SemaphoreType.DMA((2 * far, 2)),
            pltpu.SemaphoreType.DMA((2, groups)),
        ],
        [SIBLING] + masks,
        run,
    )


def chip_sum(partial):
    chips, rows, cols = partial.shape
    masks = axis_masks("chip")
    square = chips == 4
    middle = rows // 2 // STEP * STEP

    def run(ins, outs, scratch):
        (in_ref,), (out_ref,) = ins, outs
        arrived, held, local_sem, sems = scratch

        def block(j):
            return device(([(0, 0)] + masks)[j])[0] // 2

        def add(target, start, stop, *terms):
            def one(at):
                total = terms[0][at, :].astype(jnp.float32)
                for term in terms[1:]:
                    total = total + term[at, :].astype(jnp.float32)
                target[at, :] = total.astype(jnp.bfloat16)

            rows_loop(start, stop, one)

        own = keep(in_ref.at[block(0)], held.at[0], local_sem.at[0])
        if not square:
            copies = [
                remote(in_ref.at[block(j)], arrived.at[j - 1], sems.at[j - 1], masks[j - 1])
                for j in range(1, chips)
            ]
            yield
            own.wait()
            for copy in copies:
                copy.wait_recv()
            add(out_ref, 0, rows, held.at[0], *[arrived.at[j] for j in range(chips - 1)])
            for copy in copies:
                copy.wait_send()
            return
        first, second = pl.ds(0, middle), pl.ds(middle, rows - middle)
        over_x, over_y = (2, 0), (4, 0)
        copies = [
            remote(in_ref.at[block(3), first], arrived.at[2, first], sems.at[0], over_x),
            remote(in_ref.at[block(3), second], arrived.at[2, second], sems.at[1], over_y),
            remote(in_ref.at[block(1), first], arrived.at[0, first], sems.at[2], over_x),
            remote(in_ref.at[block(2), second], arrived.at[1, second], sems.at[3], over_y),
        ]
        loads = [
            keep(in_ref.at[block(2), first], held.at[1, first], local_sem.at[1]),
            keep(in_ref.at[block(1), second], held.at[1, second], local_sem.at[2]),
        ]
        yield
        loads[0].wait()
        copies[0].wait_recv()
        add(held.at[1], 0, middle, held.at[1], arrived.at[2])
        copies.append(remote(held.at[1, first], arrived.at[1, first], sems.at[4], over_y))
        loads[1].wait()
        copies[1].wait_recv()
        add(held.at[1], middle, rows, held.at[1], arrived.at[2])
        copies.append(remote(held.at[1, second], arrived.at[0, second], sems.at[5], over_x))
        yield
        own.wait()
        for copy in copies[2:]:
            copy.wait_recv()
        add(out_ref, 0, rows, held.at[0], arrived.at[0], arrived.at[1])
        for copy in copies:
            copy.wait_send()

    return Task(
        [(partial, ANY)],
        [(jax.ShapeDtypeStruct((rows, cols), jnp.bfloat16), VMEM)],
        [
            pltpu.VMEM((chips - 1, rows, cols), jnp.bfloat16),
            pltpu.VMEM((2, rows, cols), jnp.bfloat16),
            pltpu.SemaphoreType.DMA((3,)),
            pltpu.SemaphoreType.DMA((max(6, chips), 2)),
        ],
        masks,
        run,
    )


def dot(left, right):
    return jnp.dot(left, right, preferred_element_type=jnp.float32)


def back_rows(values, gain, upstream):
    inverse = lax.rsqrt(jnp.mean(values * values, axis=-1, keepdims=True) + eps_norm)
    scaled = upstream * gain
    value_grad = inverse * scaled - values * (inverse * inverse * inverse) * jnp.mean(
        scaled * values, axis=-1, keepdims=True
    )
    return value_grad, upstream * values * inverse


def columns(weight, parts):
    rows, cols = weight.shape
    low = weight.astype(jnp.bfloat16).reshape(rows, parts, cols // parts)
    return jnp.transpose(low, (1, 0, 2))


def join(pieces):
    parts, rows, cols = pieces.shape
    full = lax.all_gather(pieces.reshape(parts * rows, cols), "dp", axis=0, tiled=True)
    full = full.reshape(-1, parts, rows, cols)
    return jnp.transpose(full, (1, 0, 2, 3)).reshape(-1, cols)


def scatter_columns(grad, parts, groups):
    rows, cols = grad.shape
    piece = rows // (parts * groups)
    low = grad.astype(jnp.bfloat16).reshape(parts, groups, piece, cols)
    low = jnp.transpose(low, (1, 0, 2, 3)).reshape(rows, cols)
    own = lax.psum_scatter(low, "dp", scatter_dimension=0, tiled=True)
    return own.reshape(parts, piece, cols), low


def unfold(pieces):
    parts, rows, cols = pieces.shape
    return jnp.transpose(pieces, (1, 0, 2)).reshape(rows, parts * cols).astype(jnp.float32)


def chip_groups(parts):
    return [[chip * 2 + core for chip in range(parts // 2)] for core in range(2)]


def chip_gather(rows, parts):
    return lax.all_gather(rows, "seq", axis=0, tiled=True, axis_index_groups=chip_groups(parts))


def chip_scatter(rows, parts):
    return lax.psum_scatter(
        rows, "seq", scatter_dimension=0, tiled=True, axis_index_groups=chip_groups(parts)
    )


def local(
    block_input,
    lengths,
    cotangent,
    attn_gain,
    w_qa,
    q_gain,
    w_qb,
    w_k,
    k_gain,
    w_v,
    w_o,
    mlp_gain,
    w_gate,
    w_up,
    w_down,
):
    tok_rows = block_input.shape[1]
    parts = lax.axis_size("seq")
    groups = lax.axis_size("dp")
    me = lax.axis_index("seq")
    heads = H // parts
    group_tokens = tok_rows * parts
    first_row = me * tok_rows
    segment, places, offsets = layout(lengths[0], group_tokens)
    cos_all, sin_all = rope_tables(offsets, E)
    cosine = lax.dynamic_slice_in_dim(cos_all, first_row, tok_rows, 0)
    sine_tab = lax.dynamic_slice_in_dim(sin_all, first_row, tok_rows, 0)
    score_scale = 1.0 / math.sqrt(E)
    flat_rows = block_input.reshape(tok_rows, D)
    out_grad = cotangent.reshape(tok_rows, D)
    rank = w_qa.shape[1]
    inner = rank + 2 * E
    width = D // parts

    own_gains = [attn_gain, q_gain, k_gain, mlp_gain]
    spans = [g.shape[0] for g in own_gains]
    gain_block = jnp.concatenate(
        [jnp.pad(g, (0, 128 - g.shape[0]))[None] for g in own_gains]
        + [jnp.zeros((4, 128), jnp.float32)],
        axis=0,
    )
    gain_block = lax.reduce_precision(gain_block, 8, 7)
    inverse_one = lax.rsqrt(jnp.mean(flat_rows * flat_rows, axis=-1, keepdims=True) + eps_norm)
    scaled_cols = jnp.transpose(
        (flat_rows * inverse_one).reshape(tok_rows, parts, width), (1, 0, 2)
    )
    w_in = jnp.concatenate([w_qa, w_k, w_v], axis=1).astype(jnp.bfloat16)
    (gains, gains_line), (scaled_cols,), (in_rows,), (qb_cols,), o_low = launch(
        "start",
        0,
        [
            gather_both(gain_block),
            swap(scaled_cols, "seq"),
            swap(w_in, "dp", repeat=True),
            swap(columns(w_qb, parts), "seq"),
        ],
        passes=[w_o.astype(jnp.bfloat16)],
    )
    gain_one = gains[:, :, 0, : spans[0]].reshape(1, -1)
    gain_latent = gains[:, :, 1, : spans[1]].reshape(1, -1)
    gain_key = gains[:, :, 2, : spans[2]].reshape(1, -1)
    gain_two = gains[:, :, 3, : spans[3]].reshape(1, -1)
    gain_mine = gains_line[:, 0, : spans[0]].reshape(1, -1)

    o_rows = lax.all_gather(o_low, "dp", axis=0, tiled=True)
    qb_cols = join(qb_cols)

    in_rows = in_rows.reshape(width, inner)
    normed = (scaled_cols.reshape(group_tokens, width) * gain_mine).astype(jnp.bfloat16)
    partial = dot(normed, in_rows).astype(jnp.bfloat16).reshape(parts, tok_rows, inner)

    def latent_rows(total, row, vec):
        latent, key, value = total[:, :rank], total[:, rank : rank + E], total[:, rank + E :]
        low = jnp.concatenate(
            [rms_scale(latent, vec[0]), rotate(rms_scale(key, vec[1]), row[0], row[1]), value],
            axis=1,
        )
        return low, [total], None

    chips = parts // 2
    both_cols = fold(list(lax.optimization_barrier((w_gate, w_up))), chips, groups)
    (gathered, inner_own), (down_rows,) = launch(
        "latent",
        1,
        [
            exchange(
                partial,
                [cosine, sine_tab],
                [gain_latent, gain_key],
                latent_rows,
                [inner],
                inner,
                0,
            ),
            gather_chips(w_down.astype(jnp.bfloat16)),
        ],
        turns=[0, 0, 1, 0, 0, 0, 0, 1, 0, 0, 0],
    )
    gathered = gathered.reshape(group_tokens, inner)
    seg_col = segment[:, None]
    seg_rows = jnp.stack(
        [
            lax.slice_in_dim(segment, start, start + group_tokens // 2 + QUERIES)
            for start in [
                min(max(0, first - group_tokens // 2), group_tokens // 2 - QUERIES)
                for first in range(0, group_tokens, QUERIES)
            ]
        ]
    )[:, None, :]
    def mixed_function(total, row, vec):
        mixed = row[0] + total
        return rms_scale(mixed, vec[0]), [mixed], None

    down_rows = down_rows.reshape(-1, D)
    piece, wide = both_cols.shape[1:]
    attend_task = attend(
        gathered, qb_cols, o_rows, cos_all, sin_all, seg_col, seg_rows, parts
    )
    mixed_task = exchange(
        jax.ShapeDtypeStruct((parts, tok_rows, D), jnp.bfloat16),
        [flat_rows],
        [gain_two],
        mixed_function,
        [D],
        D,
        0,
        spread_axis="dp",
    )
    (_, q_rot, attended_low, two_all, mixed_rows), (grad_all,), (_, both_cols) = launch(
        "mixed",
        3,
        [
            chain(attend_task, mixed_task, {0: 0}),
            gather(out_grad.astype(jnp.bfloat16), "dp"),
            chain(swap(both_cols, "line"), gather_chips(both_cols), {0: 0}),
        ],
        turns=[2, 0, 0, 0, 0, 2, 1, 0, 1, 0, 2, 1, 0],
    )
    both_cols = both_cols.reshape(D, wide)
    ((mixed_grad, mixed_low, gain_two_grad, out_part, down_low, both_low),) = launch(
        "feed_forward",
        9,
        [
            feed_forward(
                two_all, grad_all, both_cols, down_rows, mixed_rows, out_grad, gain_two
            )
        ],
    )
    both_shard = chip_scatter(both_low.reshape(D, wide), parts).reshape(2 * groups, piece, wide)

    def out_function(total, row, vec):
        return None, [row[0] + total], None

    mixed_task = gather(mixed_low, "chip", VMEM)
    back_task = attend_back(
        gathered,
        q_rot,
        jax.ShapeDtypeStruct((parts, tok_rows, D), jnp.bfloat16),
        o_rows,
        qb_cols,
        cos_all,
        sin_all,
        seg_col,
        seg_rows,
    )
    (output_rows,), (mixed_all, query_grad, partial) = launch(
        "attend_back",
        4,
        [
            exchange(out_part, [mixed_rows], [], out_function, [D], 0, 0, sum_axis="dp"),
            chain(mixed_task, back_task, {2: 0}),
        ],
        turns=[1, 0, 0, 1, 1, 1, 1, 1],
    )
    o_low = jnp.einsum(
        "tf,td->fd",
        attended_low,
        mixed_all.reshape(group_tokens, D),
        preferred_element_type=jnp.float32,
    ).astype(jnp.bfloat16)
    o_low = tie(o_low, [both_shard])
    o_shard = lax.psum_scatter(o_low, "dp", scatter_dimension=0, tiled=True)
    qb_shard, qb_low = scatter_columns(
        jnp.einsum("tr,tf->rf", gathered[:, :rank], query_grad, preferred_element_type=jnp.float32),
        parts,
        groups,
    )

    def inner_function(total, row, vec):
        latent_grad, latent_gain = back_rows(row[0][:, :rank], vec[0], total[:, :rank])
        key_back = rotate_back(total[:, rank : rank + E], row[1], row[2])
        key_grad, key_gain = back_rows(row[0][:, rank : rank + E], vec[1], key_back)
        low = jnp.concatenate([latent_grad, key_grad, total[:, rank + E :]], axis=1)
        return low, [], jnp.concatenate([latent_gain, key_gain], axis=1)

    (in_grad, inner_gain_grad), (both_shard,) = launch(
        "inner_grad",
        5,
        [
            exchange(
                partial.reshape(parts, tok_rows, inner),
                [inner_own, cosine, sine_tab],
                [gain_latent, gain_key],
                inner_function,
                [],
                inner,
                rank + E,
            ),
            swap(both_shard, "line"),
        ],
        turns=[1, 0, 0, 0, 0, 0, 0, 0, 0, 0],
        needs=[o_low, qb_low],
    )
    in_grad = in_grad.reshape(group_tokens, inner)
    in_low = jnp.einsum("td,tr->dr", normed, in_grad, preferred_element_type=jnp.float32)
    in_low = in_low.astype(jnp.bfloat16).reshape(groups, -1, inner)
    normed_part = jnp.einsum("tr,dr->td", in_grad, in_rows, preferred_element_type=jnp.float32)
    normed_part = normed_part.astype(jnp.bfloat16).reshape(parts, tok_rows, width)

    (normed_grad,), (in_shard,), (down_shard,) = launch(
        "normed_grad",
        6,
        [
            swap(normed_part, "seq"),
            swap(in_low, "dp"),
            chip_sum(down_low.reshape(chips, -1, D)),
        ],
        turns=[0, 1, 2, 2],
    )
    in_shard = jnp.sum(in_shard.astype(jnp.float32), axis=0)
    normed_grad = jnp.transpose(normed_grad.astype(jnp.float32), (1, 0, 2)).reshape(tok_rows, D)
    input_part, gain_one_grad = back_rows(flat_rows, gain_one, normed_grad)
    input_grad = mixed_grad + input_part

    gain_grads = [
        jnp.sum(gain_one_grad, axis=0),
        jnp.sum(inner_gain_grad[:, :rank], axis=0),
        jnp.sum(inner_gain_grad[:, rank:], axis=0),
        jnp.sum(gain_two_grad, axis=0),
    ]
    gain_grads = jnp.stack(
        [
            jnp.pad(g.reshape(parts, groups, n), ((0, 0), (0, 0), (0, 128 - n)))
            for g, n in zip(gain_grads, spans, strict=True)
        ]
        + [jnp.zeros((parts, groups, 128), jnp.float32)] * 4,
        axis=2,
    )
    (gain_own,), (qb_shard,) = launch("end", 7, [sum_both(gain_grads), swap(qb_shard, "seq")])
    gate_grad, up_grad = unfold_pair(both_shard, chips, groups)
    return (
        output_rows.reshape(1, tok_rows, D),
        input_grad.reshape(1, tok_rows, D),
        gain_own[0, : spans[0]],
        in_shard[:, :rank],
        gain_own[1, : spans[1]],
        unfold(qb_shard),
        in_shard[:, rank : rank + E],
        gain_own[2, : spans[2]],
        in_shard[:, rank + E :],
        o_shard.astype(jnp.float32),
        gain_own[3, : spans[3]],
        gate_grad,
        up_grad,
        down_shard.astype(jnp.float32),
    )


def solution(mesh):
    return jax.shard_map(
        local,
        mesh=mesh,
        in_specs=(
            P("dp", "seq", None),
            P("dp", None),
            P("dp", "seq", None),
            P(("seq", "dp")),
            P(("seq", "dp"), None),
            P(("seq", "dp")),
            P(("seq", "dp"), None),
            P(("seq", "dp"), None),
            P(("seq", "dp")),
            P(("seq", "dp"), None),
            P(("seq", "dp"), None),
            P(("seq", "dp")),
            P(("seq", "dp"), None),
            P(("seq", "dp"), None),
            P(("seq", "dp"), None),
        ),
        out_specs=(
            P("dp", "seq", None),
            P("dp", "seq", None),
            P(("seq", "dp")),
            P(("seq", "dp"), None),
            P(("seq", "dp")),
            P(("seq", "dp"), None),
            P(("seq", "dp"), None),
            P(("seq", "dp")),
            P(("seq", "dp"), None),
            P(("seq", "dp"), None),
            P(("seq", "dp")),
            P(("seq", "dp"), None),
            P(("seq", "dp"), None),
            P(("seq", "dp"), None),
        ),
        check_vma=False,
    )
```
